32 devices in a mesh: dp: 2 (over core), ctx: 16 (over z, y, x).
Axes of the slice: x: 2, y: 2, z: 4, core: 2. Of those that a mesh axis runs over, the one named last changes fastest.
Arguments:
- inputs: bfloat16 [2, 2, 1024, 1024], P(None, 'dp', 'ctx'), may hold values from -6 to 6
- segment_ids: int32 [2, 2, 1024], P(None, 'dp'), may hold values from 0 to 3, never falling along the last dimension, each value on 1 to 512 neighbouring positions
- adapter_ids: int32 [2, 2], P(None, 'dp'), may hold values from 0 to 7
- w_query: bfloat16 [1024, 1024], P(('dp', 'ctx')), may hold values from -0.1875 to 0.1875
- w_key: bfloat16 [1024, 1024], P(('dp', 'ctx')), may hold values from -0.1875 to 0.1875
- w_value: bfloat16 [1024, 1024], P(('dp', 'ctx')), may hold values from -0.1875 to 0.1875
- w_out: bfloat16 [1024, 1024], P(('dp', 'ctx')), may hold values from -6 to 6
- w_gate: bfloat16 [1024, 4096], P(('dp', 'ctx')), may hold values from -0.1875 to 0.1875
- w_up: bfloat16 [1024, 4096], P(('dp', 'ctx')), may hold values from -0.1875 to 0.1875
- w_down: bfloat16 [4096, 1024], P(('dp', 'ctx')), may hold values from -0.09375 to 0.09375
- gain_attn: bfloat16 [1024], P(('dp', 'ctx')), may hold values from 0.5 to 1.5
- gain_ffn: bfloat16 [1024], P(('dp', 'ctx')), may hold values from 0.5 to 1.5
- attn_enter: bfloat16 [3, 8, 16, 1024], replicated, may hold values from -0.1875 to 0.1875
- attn_leave: bfloat16 [3, 8, 16, 1024], replicated, may hold values from -1.5 to 1.5
- out_enter: bfloat16 [8, 16, 1024], replicated, may hold values from -0.1875 to 0.1875
- out_leave: bfloat16 [8, 16, 1024], replicated, may hold values from -1.5 to 1.5
- mlp_enter: bfloat16 [2, 8, 16, 1024], replicated, may hold values from -0.1875 to 0.1875
- mlp_leave: bfloat16 [2, 8, 16, 4096], replicated, may hold values from -1.5 to 1.5
- last_enter: bfloat16 [8, 16, 4096], replicated, may hold values from -0.09375 to 0.09375
- last_leave: bfloat16 [8, 16, 1024], replicated, may hold values from -1.5 to 1.5
- out_grad: bfloat16 [2, 2, 1024, 1024], P(None, 'dp', 'ctx'), may hold values from -6 to 6
Outputs:
- output: bfloat16 [2, 2, 1024, 1024], P(None, 'dp', 'ctx')
- input_grad: float32 [2, 2, 1024, 1024], P(None, 'dp', 'ctx')
- grad_attn_enter: float32 [3, 8, 16, 1024], replicated
- grad_attn_leave: float32 [3, 8, 16, 1024], replicated
- grad_out_enter: float32 [8, 16, 1024], replicated
- grad_out_leave: float32 [8, 16, 1024], replicated
- grad_mlp_enter: float32 [2, 8, 16, 1024], replicated
- grad_mlp_leave: float32 [2, 8, 16, 4096], replicated
- grad_last_enter: float32 [8, 16, 4096], replicated
- grad_last_leave: float32 [8, 16, 1024], replicated
The draws below stay inside these ranges and needn't reach their ends.
Inputs may be any that keep to these rules, and one draw needn't show every extreme that they name: `segment_ids`: within each sequence segment numbers never fall; each of the 4 documents holds 1 to 512 tokens and one holds exactly 512.
All inputs are finite; a program needn't handle non-finite values.
Results may differ from the reference program's by a relative error of at most 0.025.
Values may be sent and summed in bfloat16 or wider, within the bound.
A program may use at most 256 MiB of HBM per device.

```python
import math
import jax
import jax.numpy as jnp
import numpy as np
from jax import lax

D = 1024
H = 16
HD = 64
FF = 4096
RANK = 16
ADAPTERS = 8
MICRO = 2
DOCS = 4
SEQ_LEN = 1024
SEQS = 2
DOC_MOST = 512


def touch_ends(array, own_key, least, largest):
    spot = [jax.random.randint(jax.random.fold_in(own_key, axis), (), 0, length) for axis, length in enumerate(array.shape)]
    main_axis = array.shape.index(max(array.shape))
    next_to = spot[:main_axis] + [(spot[main_axis] + 1) % array.shape[main_axis]] + spot[main_axis + 1:]
    return array.at[tuple(spot)].set(least).at[tuple(next_to)].set(largest)


def levels(own_key, extent, shards, smallest, top_value):
    def one(position, shards_of):
        heights = jax.random.uniform(jax.random.fold_in(jax.random.fold_in(own_key, 6), position), (shards_of,), jnp.float32, smallest / len(shards), top_value / len(shards))
        return jnp.repeat(jnp.exp(heights), extent[position] // shards_of).reshape((-1,) + (1,) * (len(extent) - position - 1))

    level = one(*shards[0])
    for cut in shards[1:]:
        level = level * one(*cut)
    return level


def profile(number_of, total, reach, slope):
    portions = [(1 << 20) // math.isqrt(grade ** slope) + 1 for grade in range(2, number_of + 1)]
    surplus, holding = total - reach - (number_of - 1), [1] * (number_of - 1)
    while surplus > 0:
        candidates = [i for i in range(number_of - 1) if holding[i] < reach]
        whole, left = sum([portions[i] for i in candidates]), surplus
        for i in candidates:
            more = min(reach - holding[i], max(1, left * portions[i] // whole), surplus)
            holding[i] = holding[i] + more
            surplus = surplus - more
    return np.array([reach] + holding)


def uneven_parts(own_key, amount, total, limit, lean):
    if amount == 2:
        one = jax.random.randint(own_key, (), max(1, total - limit), min(limit, total - 1) + 1)
        return jnp.stack([one, total - one])
    sizes = jnp.asarray(profile(amount, total, limit, lean), jnp.int32)
    pairs = (amount - 1) // 2
    source_of, sink = sizes[1:1 + 2 * pairs:2], sizes[2:2 + 2 * pairs:2]
    margin = jnp.minimum(source_of - 1, limit - sink)
    moved = jax.random.randint(jax.random.fold_in(own_key, 1), (pairs,), 0, 1 << 20) % (margin + 1)
    sizes = sizes.at[1:1 + 2 * pairs:2].set(source_of - moved).at[2:2 + 2 * pairs:2].set(sink + moved)
    return sizes[jax.random.permutation(jax.random.fold_in(own_key, 2), amount)]


def gaussian(rng, extent, deviation, bound, split=(), kind=jnp.bfloat16):
    loudness = levels(rng, extent, split, -0.22, 0.18) if split else 1.0
    values = jax.random.normal(rng, extent, jnp.float32) * deviation * loudness
    return jnp.minimum(jnp.maximum(values, -bound), bound).astype(kind)


def setup_inputs(seed: int = 0) -> dict:
    splits = jax.random.split(jax.random.key(seed), 22)
    return {
        "inputs": gaussian(splits[0], (MICRO, SEQS, SEQ_LEN, D), 1.0, 6.0, ((1, 2), (2, 16))),
        "segment_ids": jax.vmap(lambda own: jnp.searchsorted(jnp.cumsum(uneven_parts(own, DOCS, SEQ_LEN, DOC_MOST, 1)), jnp.arange(SEQ_LEN), side="right"))(jax.random.split(splits[1], MICRO * SEQS)).reshape((MICRO, SEQS, SEQ_LEN)).astype(jnp.int32),
        "adapter_ids": touch_ends(jax.random.randint(splits[2], (MICRO, SEQS), 0, ADAPTERS), jax.random.fold_in(splits[2], 1), 0, ADAPTERS - 1).astype(jnp.int32),
        "w_query": gaussian(splits[3], (D, D), D ** -0.5, 0.1875, ((0, 32),)),
        "w_key": gaussian(splits[4], (D, D), D ** -0.5, 0.1875, ((0, 32),)),
        "w_value": gaussian(splits[5], (D, D), D ** -0.5, 0.1875, ((0, 32),)),
        "w_out": gaussian(splits[6], (D, D), 1 ** -0.5, 6.0, ((0, 32),)),
        "w_gate": gaussian(splits[7], (D, FF), D ** -0.5, 0.1875, ((0, 32),)),
        "w_up": gaussian(splits[8], (D, FF), D ** -0.5, 0.1875, ((0, 32),)),
        "w_down": gaussian(splits[9], (FF, D), FF ** -0.5, 0.09375, ((0, 32),)),
        "gain_attn": jnp.clip(1.0 + 0.1 * jax.random.normal(splits[10], (D,), jnp.float32), 0.5, 1.5).astype(jnp.bfloat16),
        "gain_ffn": jnp.clip(1.0 + 0.1 * jax.random.normal(splits[11], (D,), jnp.float32), 0.5, 1.5).astype(jnp.bfloat16),
        "attn_enter": gaussian(splits[12], (3, ADAPTERS, RANK, D), D ** -0.5, 0.1875),
        "attn_leave": gaussian(splits[13], (3, ADAPTERS, RANK, D), RANK ** -0.5, 1.5),
        "out_enter": gaussian(splits[14], (ADAPTERS, RANK, D), D ** -0.5, 0.1875),
        "out_leave": gaussian(splits[15], (ADAPTERS, RANK, D), RANK ** -0.5, 1.5),
        "mlp_enter": gaussian(splits[16], (2, ADAPTERS, RANK, D), D ** -0.5, 0.1875),
        "mlp_leave": gaussian(splits[17], (2, ADAPTERS, RANK, FF), RANK ** -0.5, 1.5),
        "last_enter": gaussian(splits[18], (ADAPTERS, RANK, FF), FF ** -0.5, 0.09375),
        "last_leave": gaussian(splits[19], (ADAPTERS, RANK, D), RANK ** -0.5, 1.5),
        "out_grad": gaussian(splits[20], (MICRO, SEQS, SEQ_LEN, D), 1.0, 6.0, ((1, 2), (2, 16))),
    }


EPS = 1e-05
NEG = -1000000000.0
SCALE = 0.5
HIGH = lax.Precision.HIGHEST

@jax.custom_vjp
def low(v):
    return lax.optimization_barrier(v.astype(jnp.bfloat16)).astype(jnp.float32)

@jax.custom_vjp
def low_back(v):
    return v

def low_keep(v):
    return (low(v), None)

def low_pass(kept, grad):
    return (grad,)

def back_keep(v):
    return (v, None)

def back_low(kept, grad):
    return (low(grad),)
low.defvjp(low_keep, low_pass)
low_back.defvjp(back_keep, back_low)

def matmul(left, right):
    return jnp.dot(left, right, preferred_element_type=jnp.float32, precision=HIGH)

def rms_norm(rows, gain):
    return rows * lax.rsqrt(lax.optimization_barrier(jnp.mean(rows * rows, axis=-1, keepdims=True)) + EPS) * gain

def project(rows, weight, enter, leave):
    inner = low(low_back(matmul(rows, enter.T)))
    return matmul(rows, weight) + SCALE * matmul(inner, leave)

def attention(query, key, value, segments):
    length = query.shape[0]
    block = min(512, length)
    key_heads = key.reshape(length, H, HD)
    value_heads = value.reshape(length, H, HD)
    query_blocks = query.reshape(length // block, block, H, HD)
    segment_blocks = segments.reshape(length // block, block)

    def one_block(item):
        query_block, segment_block = item
        scores = jnp.einsum('qhd,khd->hqk', query_block, key_heads, precision=HIGH) * 0.125
        scores = jnp.where(segment_block[None, :, None] == segments[None, None, :], scores, NEG)
        scores = low_back(scores)
        shifted = scores - lax.optimization_barrier(jnp.max(scores, axis=-1, keepdims=True))
        weights = jnp.exp(shifted)
        probs = weights / lax.optimization_barrier(jnp.sum(weights, axis=-1, keepdims=True))
        return jnp.einsum('hqk,khd->qhd', low(probs), value_heads, precision=HIGH)
    mixed = lax.map(jax.checkpoint(one_block), (query_blocks, segment_blocks))
    return mixed.reshape(length, H * HD)

def layer(rows, segments, ident, frozen, adapters):
    query_w, key_w, value_w, out_w, gate_w, up_w, down_w, gain_one, gain_two = frozen
    attn_in, attn_out, out_in, out_out, mlp_in, mlp_out, last_in, last_out = adapters
    attn_in = attn_in[:, ident]
    attn_out = attn_out[:, ident]
    out_in = out_in[ident]
    out_out = out_out[ident]
    mlp_in = mlp_in[:, ident]
    mlp_out = mlp_out[:, ident]
    last_in = last_in[ident]
    last_out = last_out[ident]
    normed = low(rms_norm(rows, gain_one))
    query = low(low_back(project(normed, query_w, attn_in[0], attn_out[0])))
    key = low(low_back(project(normed, key_w, attn_in[1], attn_out[1])))
    value = low(low_back(project(normed, value_w, attn_in[2], attn_out[2])))
    mixed = low(low_back(attention(query, key, value, segments)))
    branch = low_back(project(mixed, out_w, out_in, out_out))
    middle = rows + branch
    normed_two = low(rms_norm(middle, gain_two))
    gate = low_back(project(normed_two, gate_w, mlp_in[0], mlp_out[0]))
    upper = low_back(project(normed_two, up_w, mlp_in[1], mlp_out[1]))
    hidden = low(gate * jax.nn.sigmoid(gate) * upper)
    return middle + low_back(project(hidden, down_w, last_in, last_out))

def reference(inputs, segment_ids, adapter_ids, w_query, w_key, w_value, w_out, w_gate, w_up, w_down, gain_attn, gain_ffn, attn_enter, attn_leave, out_enter, out_leave, mlp_enter, mlp_leave, last_enter, last_leave, out_grad):
    count = MICRO * SEQS
    frozen = tuple((item.astype(jnp.float32) for item in (w_query, w_key, w_value, w_out, w_gate, w_up, w_down, gain_attn, gain_ffn)))
    adapters = tuple((item.astype(jnp.float32) for item in (attn_enter, attn_leave, out_enter, out_leave, mlp_enter, mlp_leave, last_enter, last_leave)))
    rows = inputs.reshape(count, SEQ_LEN, D).astype(jnp.float32)
    segments = segment_ids.reshape(count, SEQ_LEN)
    idents = adapter_ids.reshape(count)

    def forward(rows, adapters):

        def one(carry, item):
            seq_rows, seq_segments, ident = item
            return (carry, layer(seq_rows, seq_segments, ident, frozen, adapters))
        return lax.scan(one, jnp.zeros((), jnp.float32), (rows, segments, idents))[1]
    result, pull = jax.vjp(forward, rows, adapters)
    row_grad, adapter_grads = pull(out_grad.reshape(count, SEQ_LEN, D).astype(jnp.float32))
    output = result.astype(jnp.bfloat16).reshape(MICRO, SEQS, SEQ_LEN, D)
    input_grad = row_grad.reshape(MICRO, SEQS, SEQ_LEN, D)
    return (output, input_grad, adapter_grads[0], adapter_grads[1], adapter_grads[2], adapter_grads[3], adapter_grads[4], adapter_grads[5], adapter_grads[6], adapter_grads[7])
```

```python
import functools

import jax
import jax.numpy as jnp
from jax import lax
from jax.experimental import pallas as pl
from jax.experimental.pallas import tpu as pltpu
from jax.sharding import PartitionSpec as P

H = 16
HD = 64


EPS = 1e-05
NEG = -1000000000.0
SCALE = 0.5


def rms_norm(rows, gain):
    inverse = lax.rsqrt(jnp.mean(rows * rows, axis=-1, keepdims=True) + EPS)
    return (rows * inverse * gain, inverse)


def norm_back(rows, inverse, gain, grad):
    weighted = grad * gain
    return inverse * weighted - rows * inverse**3 * jnp.mean(
        rows * weighted, axis=-1, keepdims=True
    )


def project(rows, weight, enter, leave):
    direct = jnp.einsum("sci,io->sco", rows, weight, preferred_element_type=jnp.float32)
    inner = jnp.einsum("sci,sri->scr", rows, enter, preferred_element_type=jnp.float32).astype(
        jnp.bfloat16
    )
    return (
        direct
        + SCALE * jnp.einsum("scr,sro->sco", inner, leave, preferred_element_type=jnp.float32),
        inner,
    )


def project_back(rows, inner, weight, enter, leave, grad):
    inner_grad = (
        SCALE * jnp.einsum("sco,sro->scr", grad, leave, preferred_element_type=jnp.float32)
    ).astype(jnp.bfloat16)
    rows_grad = jnp.einsum("sco,io->sci", grad, weight, preferred_element_type=jnp.float32)
    rows_grad = rows_grad + jnp.einsum(
        "scr,sri->sci", inner_grad, enter, preferred_element_type=jnp.float32
    )
    enter_grad = jnp.einsum("scr,sci->sri", inner_grad, rows, preferred_element_type=jnp.float32)
    leave_grad = SCALE * jnp.einsum("scr,sco->sro", inner, grad, preferred_element_type=jnp.float32)
    return (rows_grad, enter_grad, leave_grad)


def masked_scores(query_heads, key_block, seg_query, seg_key):
    seqs = query_heads.shape[0]
    key_heads = key_block.reshape(seqs, -1, H, HD)
    scores = (
        jnp.einsum("sqhd,skhd->shqk", query_heads, key_heads, preferred_element_type=jnp.float32)
        * 0.125
    )
    same = seg_query[:, None, :, None] == seg_key[:, None, None, :]
    return (jnp.where(same, scores, NEG), key_heads)


def forward_block(state, query_heads, seg_query, key_block, value_block, seg_key):
    best, total, accum = state
    seqs = query_heads.shape[0]
    scores, key_heads = masked_scores(query_heads, key_block, seg_query, seg_key)
    value_heads = value_block.reshape(seqs, -1, H, HD)
    new_best = jnp.maximum(best, jnp.max(scores, axis=-1))
    factor = jnp.exp(best - new_best)
    weights = jnp.exp(scores - new_best[..., None])
    total = total * factor + jnp.sum(weights, axis=-1)
    mixed = jnp.einsum(
        "shqk,skhd->sqhd",
        weights.astype(jnp.bfloat16),
        value_heads,
        preferred_element_type=jnp.float32,
    )
    accum = accum * jnp.transpose(factor, (0, 2, 1))[..., None] + mixed
    return (new_best, total, accum)


def attend(query, key, value, seg_rows, my_start):
    seqs, rows, width = query.shape
    query_heads = query.reshape(seqs, rows, H, HD)
    seg_query = lax.dynamic_slice_in_dim(seg_rows, my_start, rows, 1)
    state = (
        jnp.full((seqs, H, rows), -1e30, jnp.float32),
        jnp.zeros((seqs, H, rows), jnp.float32),
        jnp.zeros((seqs, rows, H, HD), jnp.float32),
    )

    def fold(carry, piece, start):
        key_piece, value_piece = piece
        count = key_piece.shape[1]
        block = 512

        def advance(index, inner_state):
            offset = index * block
            key_block = lax.dynamic_slice_in_dim(key_piece, offset, block, 1)
            value_block = lax.dynamic_slice_in_dim(value_piece, offset, block, 1)
            seg_key = lax.dynamic_slice_in_dim(seg_rows, offset, block, 1)
            return forward_block(
                inner_state, query_heads, seg_query, key_block, value_block, seg_key
            )

        return lax.fori_loop(0, count // block, advance, carry)

    best, total, accum = fold(
        state,
        (
            lax.all_gather(key, "ctx", axis=1, tiled=True),
            lax.all_gather(value, "ctx", axis=1, tiled=True),
        ),
        jnp.int32(0),
    )
    output = accum / jnp.transpose(total, (0, 2, 1))[..., None]
    return (output, best + jnp.log(total))


def block_grads(
    query_heads, grad_heads, log_total, delta, seg_query, key_block, value_block, seg_key
):
    seqs = query_heads.shape[0]
    scores, key_heads = masked_scores(query_heads, key_block, seg_query, seg_key)
    value_heads = value_block.reshape(seqs, -1, H, HD)
    probs = jnp.exp(scores - log_total[..., None])
    value_part = jnp.einsum(
        "shqk,sqhd->skhd",
        probs.astype(jnp.bfloat16),
        grad_heads,
        preferred_element_type=jnp.float32,
    )
    prob_grad = jnp.einsum(
        "sqhd,skhd->shqk", grad_heads, value_heads, preferred_element_type=jnp.float32
    )
    score_grad = (probs * (prob_grad - delta[..., None])).astype(jnp.bfloat16)
    query_part = 0.125 * jnp.einsum(
        "shqk,skhd->sqhd", score_grad, key_heads, preferred_element_type=jnp.float32
    )
    key_part = 0.125 * jnp.einsum(
        "shqk,sqhd->skhd", score_grad, query_heads, preferred_element_type=jnp.float32
    )
    return (query_part, key_part, value_part)


def attend_back(query, key, value, grad, output, log_total, seg_rows, my_start):
    seqs, rows, width = query.shape
    length = seg_rows.shape[1]
    query_heads = query.reshape(seqs, rows, H, HD)
    grad_heads = grad.reshape(seqs, rows, H, HD)
    seg_query = lax.dynamic_slice_in_dim(seg_rows, my_start, rows, 1)
    delta = jnp.transpose(jnp.sum(grad_heads.astype(jnp.float32) * output, axis=-1), (0, 2, 1))
    state = (
        jnp.zeros((seqs, rows, H, HD), jnp.float32),
        jnp.zeros((seqs, length, width), jnp.float32),
        jnp.zeros((seqs, length, width), jnp.float32),
    )

    def fold(carry, piece, start):
        key_piece, value_piece = piece
        count = key_piece.shape[1]
        block = 512

        def advance(index, inner_state):
            offset = index * block
            key_block = lax.dynamic_slice_in_dim(key_piece, offset, block, 1)
            value_block = lax.dynamic_slice_in_dim(value_piece, offset, block, 1)
            seg_key = lax.dynamic_slice_in_dim(seg_rows, offset, block, 1)
            query_part, key_part, value_part = block_grads(
                query_heads,
                grad_heads,
                log_total,
                delta,
                seg_query,
                key_block,
                value_block,
                seg_key,
            )
            query_grad, key_all, value_all = inner_state
            key_old = lax.dynamic_slice_in_dim(key_all, offset, block, 1)
            key_all = lax.dynamic_update_slice_in_dim(
                key_all, key_old + key_part.reshape(seqs, block, width), offset, 1
            )
            value_old = lax.dynamic_slice_in_dim(value_all, offset, block, 1)
            value_all = lax.dynamic_update_slice_in_dim(
                value_all, value_old + value_part.reshape(seqs, block, width), offset, 1
            )
            return (query_grad + query_part, key_all, value_all)

        return lax.fori_loop(0, count // block, advance, carry)

    folded = fold(
        state,
        (
            lax.all_gather(key, "ctx", axis=1, tiled=True),
            lax.all_gather(value, "ctx", axis=1, tiled=True),
        ),
        jnp.int32(0),
    )
    query_grad = folded[0]
    key_grad, value_grad = (
        lax.psum_scatter(
            folded[1].astype(jnp.bfloat16), "ctx", scatter_dimension=1, tiled=True
        ).astype(jnp.float32),
        lax.psum_scatter(
            folded[2].astype(jnp.bfloat16), "ctx", scatter_dimension=1, tiled=True
        ).astype(jnp.float32),
    )
    return (
        query_grad.reshape(seqs, rows, width).astype(jnp.bfloat16),
        key_grad.astype(jnp.bfloat16),
        value_grad.astype(jnp.bfloat16),
    )


def per_device(
    inputs,
    segment_ids,
    adapter_ids,
    w_query,
    w_key,
    w_value,
    w_out,
    w_gate,
    w_up,
    w_down,
    gain_attn,
    gain_ffn,
    attn_enter,
    attn_leave,
    out_enter,
    out_leave,
    mlp_enter,
    mlp_leave,
    last_enter,
    last_leave,
    out_grad,
):
    micro_count, seqs, rows, width = inputs.shape
    my_start = lax.axis_index("ctx") * rows
    adapter_count = attn_enter.shape[1]
    sum_attn_enter = jnp.zeros(attn_enter.shape, jnp.float32)
    sum_attn_leave = jnp.zeros(attn_leave.shape, jnp.float32)
    sum_out_enter = jnp.zeros(out_enter.shape, jnp.float32)
    sum_out_leave = jnp.zeros(out_leave.shape, jnp.float32)
    sum_mlp_enter = jnp.zeros(mlp_enter.shape, jnp.float32)
    sum_mlp_leave = jnp.zeros(mlp_leave.shape, jnp.float32)
    sum_last_enter = jnp.zeros(last_enter.shape, jnp.float32)
    sum_last_leave = jnp.zeros(last_leave.shape, jnp.float32)
    outputs = []
    gradients = []
    for micro in range(micro_count):
        frozen = (
            lax.all_gather(w_query, ("dp", "ctx"), axis=0, tiled=True),
            lax.all_gather(w_key, ("dp", "ctx"), axis=0, tiled=True),
            lax.all_gather(w_value, ("dp", "ctx"), axis=0, tiled=True),
            lax.all_gather(w_out, ("dp", "ctx"), axis=0, tiled=True),
            lax.all_gather(w_gate, ("dp", "ctx"), axis=0, tiled=True),
            lax.all_gather(w_up, ("dp", "ctx"), axis=0, tiled=True),
            lax.all_gather(w_down, ("dp", "ctx"), axis=0, tiled=True),
            lax.all_gather(gain_attn, ("dp", "ctx"), axis=0, tiled=True),
            lax.all_gather(gain_ffn, ("dp", "ctx"), axis=0, tiled=True),
        )
        query_w, key_w, value_w, out_w, gate_w, up_w, down_w, gain_one, gain_two = frozen
        chosen = adapter_ids[micro]
        attn_in = jnp.take(attn_enter, chosen, axis=1)
        attn_out = jnp.take(attn_leave, chosen, axis=1)
        out_in = jnp.take(out_enter, chosen, axis=0)
        out_out = jnp.take(out_leave, chosen, axis=0)
        mlp_in = jnp.take(mlp_enter, chosen, axis=1)
        mlp_out = jnp.take(mlp_leave, chosen, axis=1)
        last_in = jnp.take(last_enter, chosen, axis=0)
        last_out = jnp.take(last_leave, chosen, axis=0)
        seg_rows = segment_ids[micro]
        start_rows = inputs[micro].astype(jnp.float32)
        normed_f, inverse_one = rms_norm(start_rows, gain_one.astype(jnp.float32))
        normed = normed_f.astype(jnp.bfloat16)
        query_f, query_inner = project(normed, query_w, attn_in[0], attn_out[0])
        key_f, key_inner = project(normed, key_w, attn_in[1], attn_out[1])
        value_f, value_inner = project(normed, value_w, attn_in[2], attn_out[2])
        query = query_f.astype(jnp.bfloat16)
        key = key_f.astype(jnp.bfloat16)
        value = value_f.astype(jnp.bfloat16)
        mixed_f, log_total = attend(query, key, value, seg_rows, my_start)
        mixed = mixed_f.reshape(seqs, rows, width).astype(jnp.bfloat16)
        branch, out_inner = project(mixed, out_w, out_in, out_out)
        middle = start_rows + branch
        normed_two_f, inverse_two = rms_norm(middle, gain_two.astype(jnp.float32))
        normed_two = normed_two_f.astype(jnp.bfloat16)
        gate, gate_inner = project(normed_two, gate_w, mlp_in[0], mlp_out[0])
        upper, up_inner = project(normed_two, up_w, mlp_in[1], mlp_out[1])
        sigma = jax.nn.sigmoid(gate)
        hidden = (gate * sigma * upper).astype(jnp.bfloat16)
        closing, last_inner = project(hidden, down_w, last_in, last_out)
        outputs.append((middle + closing).astype(jnp.bfloat16))
        frozen = (
            lax.all_gather(w_query, ("dp", "ctx"), axis=0, tiled=True),
            lax.all_gather(w_key, ("dp", "ctx"), axis=0, tiled=True),
            lax.all_gather(w_value, ("dp", "ctx"), axis=0, tiled=True),
            lax.all_gather(w_out, ("dp", "ctx"), axis=0, tiled=True),
            lax.all_gather(w_gate, ("dp", "ctx"), axis=0, tiled=True),
            lax.all_gather(w_up, ("dp", "ctx"), axis=0, tiled=True),
            lax.all_gather(w_down, ("dp", "ctx"), axis=0, tiled=True),
            lax.all_gather(gain_attn, ("dp", "ctx"), axis=0, tiled=True),
            lax.all_gather(gain_ffn, ("dp", "ctx"), axis=0, tiled=True),
        )
        query_w, key_w, value_w, out_w, gate_w, up_w, down_w, gain_one, gain_two = frozen
        grad_rows = out_grad[micro].astype(jnp.float32)
        hidden_grad, last_in_grad, last_out_grad = project_back(
            hidden, last_inner, down_w, last_in, last_out, out_grad[micro]
        )
        gate_grad = (hidden_grad * upper * sigma * (1.0 + gate * (1.0 - sigma))).astype(
            jnp.bfloat16
        )
        up_grad = (hidden_grad * gate * sigma).astype(jnp.bfloat16)
        from_gate, gate_in_grad, gate_out_grad = project_back(
            normed_two, gate_inner, gate_w, mlp_in[0], mlp_out[0], gate_grad
        )
        from_up, up_in_grad, up_out_grad = project_back(
            normed_two, up_inner, up_w, mlp_in[1], mlp_out[1], up_grad
        )
        middle_grad = grad_rows + norm_back(
            middle, inverse_two, gain_two.astype(jnp.float32), from_gate + from_up
        )
        mixed_grad_f, out_in_grad, out_out_grad = project_back(
            mixed, out_inner, out_w, out_in, out_out, middle_grad.astype(jnp.bfloat16)
        )
        mixed_grad = mixed_grad_f.astype(jnp.bfloat16)
        query_grad, key_grad, value_grad = attend_back(
            query, key, value, mixed_grad, mixed_f, log_total, seg_rows, my_start
        )
        from_query, query_in_grad, query_out_grad = project_back(
            normed, query_inner, query_w, attn_in[0], attn_out[0], query_grad
        )
        from_key, key_in_grad, key_out_grad = project_back(
            normed, key_inner, key_w, attn_in[1], attn_out[1], key_grad
        )
        from_value, value_in_grad, value_out_grad = project_back(
            normed, value_inner, value_w, attn_in[2], attn_out[2], value_grad
        )
        gradients.append(
            middle_grad
            + norm_back(
                start_rows,
                inverse_one,
                gain_one.astype(jnp.float32),
                from_query + from_key + from_value,
            )
        )
        per_seq = (
            jnp.stack([query_in_grad, key_in_grad, value_in_grad]),
            jnp.stack([query_out_grad, key_out_grad, value_out_grad]),
            out_in_grad,
            out_out_grad,
            jnp.stack([gate_in_grad, up_in_grad]),
            jnp.stack([gate_out_grad, up_out_grad]),
            last_in_grad,
            last_out_grad,
        )
        onehot = (chosen[:, None] == jnp.arange(adapter_count, dtype=jnp.int32)[None, :]).astype(
            jnp.float32
        )
        sum_attn_enter = sum_attn_enter + jnp.einsum("sa,isrd->iard", onehot, per_seq[0])
        sum_attn_leave = sum_attn_leave + jnp.einsum("sa,isrd->iard", onehot, per_seq[1])
        sum_out_enter = sum_out_enter + jnp.einsum("sa,srd->ard", onehot, per_seq[2])
        sum_out_leave = sum_out_leave + jnp.einsum("sa,srd->ard", onehot, per_seq[3])
        sum_mlp_enter = sum_mlp_enter + jnp.einsum("sa,isrd->iard", onehot, per_seq[4])
        sum_mlp_leave = sum_mlp_leave + jnp.einsum("sa,isrf->iarf", onehot, per_seq[5])
        sum_last_enter = sum_last_enter + jnp.einsum("sa,srf->arf", onehot, per_seq[6])
        sum_last_leave = sum_last_leave + jnp.einsum("sa,srd->ard", onehot, per_seq[7])
    totals = (
        sum_attn_enter,
        sum_attn_leave,
        sum_out_enter,
        sum_out_leave,
        sum_mlp_enter,
        sum_mlp_leave,
        sum_last_enter,
        sum_last_leave,
    )
    summed = lax.psum(
        (totals[0], totals[1], totals[2], totals[3], totals[4], totals[5], totals[6], totals[7]),
        ("dp", "ctx"),
    )
    return (
        jnp.stack(outputs),
        jnp.stack(gradients),
        summed[0],
        summed[1],
        summed[2],
        summed[3],
        summed[4],
        summed[5],
        summed[6],
        summed[7],
    )


MESH = pl.DeviceIdType.MESH
BF = jnp.bfloat16
F32 = jnp.float32
SAME = (1, 4, 5)
PEERS = ((0, 1), (0, 4), (0, 5), (1, 0), (1, 1), (1, 4), (1, 5))
ACROSS = ((0, 2), (0, 8), (0, 10))
GREET = PEERS + ACROSS + ((1, 2), (1, 10))
GW = 2944


def dot(left, right):
    return lax.dot_general(left, right, (((1,), (0,)), ((), ())), preferred_element_type=F32)


def dot_t(left, right):
    return lax.dot_general(left, right, (((1,), (1,)), ((), ())), preferred_element_type=F32)


class Spot:
    def __init__(self, p, x, y, zl, zh):
        self.p, self.x, self.y, self.zl, self.zh = p, x, y, zl, zh

    def flip(self, a, b):
        return Spot(
            1 - self.p if a else self.p,
            1 - self.x if b & 1 else self.x,
            1 - self.y if b & 2 else self.y,
            1 - self.zl if b & 4 else self.zl,
            1 - self.zh if b & 8 else self.zh,
        )

    def device(self):
        return (self.p, self.x + 2 * self.y + 4 * self.zl + 8 * self.zh)

    def member(self):
        return self.p * 4 + self.zl * 2 + self.x

    def group(self):
        return self.zh * 2 + self.y


def here():
    p, c = lax.axis_index("dp"), lax.axis_index("ctx")
    return Spot(p, lax.rem(c, 2), lax.rem(lax.div(c, 2), 2), lax.rem(lax.div(c, 4), 2), lax.div(c, 8))


def part(index, size):
    return pl.ds(pl.multiple_of(index * size, size), size)


def remote(src, dst, ssem, rsem, spot):
    return pltpu.make_async_remote_copy(
        src_ref=src, dst_ref=dst, send_sem=ssem, recv_sem=rsem, device_id=spot.device(), device_id_type=MESH
    )


def pick(raw, mask):
    total = raw[0].astype(F32) * mask(0)
    for a in range(1, raw.shape[0]):
        total = total + raw[a].astype(F32) * mask(a)
    return total


def layer_kernel(names, *refs):
    R = dict(zip(names, refs, strict=True))
    g = lambda name: R[name]
    me = here()
    p, x, y, zl, zh = me.p, me.x, me.y, me.zl, me.zh
    j = me.member()
    own = part(j, 128)
    partner = me.flip(1, 0)
    late = []

    def send(src, dst, ssem, rsem, spot):
        copy = remote(src, dst, ssem, rsem, spot)
        copy.start()
        late.append(copy)

    def arrived(ref, ssem, rsem, spot):
        remote(ref, ref, ssem, rsem, spot).wait_recv()

    barrier = pltpu.get_barrier_semaphore()
    for a, b in GREET:
        pl.semaphore_signal(barrier, inc=1, device_id=me.flip(a, b).device(), device_id_type=MESH)
    pl.semaphore_wait(barrier, len(GREET))

    def reshard(src, dst, ssem, rsem):
        rows = pl.ds(pl.multiple_of((y * 4 + zl * 2 + x) * 128 + zh * 64, 64), 64)

        @pl.when(p == y)
        def _():
            pltpu.make_async_copy(src.at[zh], dst.at[rows], rsem.at[0]).start()
            remote(src.at[1 - zh], dst.at[rows], ssem.at[1], rsem.at[1], me.flip(0, 8)).start()

        @pl.when(p != y)
        def _():
            remote(src.at[zh], dst.at[rows], ssem.at[0], rsem.at[0], me.flip(1, 2)).start()
            remote(src.at[1 - zh], dst.at[rows], ssem.at[1], rsem.at[1], me.flip(1, 10)).start()

    def reshard_wait(dst, rsem):
        for k, t in enumerate((zh, 1 - zh)):
            rows = pl.ds(pl.multiple_of(j * 128 + t * 64, 64), 64)
            pltpu.make_async_copy(dst.at[rows], dst.at[rows], rsem.at[k]).wait()

    def reshard_sent(src, ssem):
        @pl.when(p != y)
        def _():
            remote(src.at[zh], src.at[zh], ssem.at[0], ssem.at[0], me.flip(1, 2)).wait_send()

        remote(src.at[zh], src.at[zh], ssem.at[1], ssem.at[1], me.flip(0, 8)).wait_send()

    def spread(view, ssem, rsem):
        mine = view(me)
        for k, b in enumerate(SAME):
            send(mine, mine, ssem.at[k], rsem.at[k], me.flip(0, b))
        send(mine, mine, ssem.at[3], rsem.at[3], partner)

    def spread_on(view, ssem, rsem):
        for k, b in enumerate(SAME):
            got = view(me.flip(0, b))
            arrived(got, ssem.at[k], rsem.at[k], me.flip(0, b))
            send(got, got, ssem.at[4 + k], rsem.at[4 + k], partner)

    def spread_end(view, ssem, rsem):
        arrived(view(partner), ssem.at[3], rsem.at[3], partner)
        for k, b in enumerate(SAME):
            arrived(view(me.flip(1, b)), ssem.at[4 + k], rsem.at[4 + k], partner)

    def across(views, ssem, rsem):
        for k, view in enumerate(views(me)):
            send(view, view, ssem.at[0, k], rsem.at[0, k], me.flip(0, 8))
            send(view, view, ssem.at[1, k], rsem.at[1, k], me.flip(0, 2))

    def across_on(views, ssem, rsem):
        for k, view in enumerate(views(me.flip(0, 8))):
            arrived(view, ssem.at[0, k], rsem.at[0, k], me.flip(0, 8))
            send(view, view, ssem.at[2, k], rsem.at[2, k], me.flip(0, 2))

    def across_end(views, ssem, rsem):
        for k, view in enumerate(views(me.flip(0, 2))):
            arrived(view, ssem.at[1, k], rsem.at[1, k], me.flip(0, 2))
        for k, view in enumerate(views(me.flip(0, 10))):
            arrived(view, ssem.at[2, k], rsem.at[2, k], me.flip(0, 2))

    def row_views(ref, columns):
        def views(spot):
            return [
                ref.at[pl.ds(pl.multiple_of(pp * 512 + spot.zh * 256 + zz * 128 + spot.y * 64, 64), 64), pl.ds(0, columns)]
                for pp in range(2)
                for zz in range(2)
            ]

        return views

    qkv_views, gu_views = row_views(g("qkvb"), 384), row_views(g("gub"), 1024)

    def down_views(spot):
        return [g("db").at[part(spot.group(), 128), pl.ds(0, 1024)]]

    def out_views(spot):
        k_row = (spot.p * 16 + spot.zh * 8 + spot.zl * 4 + spot.y * 2 + spot.x) * 32
        return [g("ob").at[pl.ds(pl.multiple_of(k_row, 32), 32), pl.ds(0, 1024)]]

    def gain_views(spot):
        return [g("gs").at[spot.group()]]

    my_row = pl.ds(pl.multiple_of((p * 16 + zh * 8 + zl * 4 + y * 2 + x) * 32, 32), 32)

    raws = (
        ("ae", g("ae_h")), ("al", g("al_h").at[:, :, :, own]), ("oe", g("oe_h")), ("ol", g("ol_h")),
        ("me", g("me_h")), ("ll", g("ll_h")),
    )
    locals_ = []
    for k, (name, src) in enumerate(raws):
        locals_.append(pltpu.make_async_copy(src, g(name), g("la").at[k]))
    for q in range(4):
        fb = part(p * 16 + (q // 2) * 8 + zl * 4 + (q % 2) * 2 + x, 128)
        locals_.append(pltpu.make_async_copy(g("ml_h").at[:, :, :, fb], g("ml").at[:, :, :, pl.ds(q * 128, 128)], g("la").at[8 + q]))
        locals_.append(pltpu.make_async_copy(g("le_h").at[:, :, fb], g("le").at[:, :, pl.ds(q * 128, 128)], g("la").at[12 + q]))

    reshard(g("x_h"), g("xf"), g("xs"), g("xr"))

    gain_mine = g("gs").at[me.group(), j]
    gain_local = pltpu.make_async_copy(g("gain_h"), gain_mine, g("g1r").at[7])
    gain_local.start()
    for k, (a, b) in enumerate(PEERS):
        send(g("gain_h"), gain_mine, g("g1s").at[k], g("g1r").at[k], me.flip(a, b))

    def columns_to(spot, k, start):
        t = spot.member()
        for i, name in enumerate(("wq_h", "wk_h", "wv_h")):
            start(g(name).at[:, part(t, 128)], g("qkvb").at[my_row, pl.ds(i * 128, 128)], ("q", k, i))

    def mlp_columns_to(spot, k, start):
        for i, name in enumerate(("wg_h", "wu_h")):
            for q in range(4):
                fb = part(spot.p * 16 + (q // 2) * 8 + spot.zl * 4 + (q % 2) * 2 + spot.x, 128)
                start(g(name).at[:, fb], g("gub").at[my_row, pl.ds(i * 512 + q * 128, 128)], ("m", k, i * 4 + q))

    def start_remote(spot):
        def start(src, dst, key):
            kind, k, i = key
            send(src, dst, g("w1" + kind + "s").at[k, i], g("w1" + kind + "r").at[k, i], spot)

        return start

    def start_local(src, dst, key):
        kind, k, i = key
        pltpu.make_async_copy(src, dst, g("w1" + kind + "r").at[k, i]).start()

    for k, (a, b) in enumerate(PEERS):
        columns_to(me.flip(a, b), k, start_remote(me.flip(a, b)))
    columns_to(me, 7, start_local)

    meta_local = pltpu.make_async_copy(g("meta_h"), g("meta").at[p], g("mr").at[1])
    meta_local.start()
    send(g("meta_h"), g("meta").at[p], g("ms").at[0], g("mr").at[0], partner)
    for copy in locals_:
        copy.start()

    out_mine = out_views(me)[0]
    out_local = pltpu.make_async_copy(g("wo_h"), out_mine, g("wor").at[3, 0])
    out_local.start()
    send(g("wo_h"), out_mine, g("wos").at[0, 0], g("wor").at[0, 0], me.flip(0, 8))
    send(g("wo_h"), out_mine, g("wos").at[1, 0], g("wor").at[1, 0], me.flip(0, 2))

    def x_view(spot):
        return g("xf").at[part(spot.member(), 128)]

    def og_view(spot):
        return g("ogf").at[part(spot.member(), 128)]

    def n2_view(spot):
        return g("n2f").at[part(spot.member(), 128)]

    reshard_wait(g("xf"), g("xr"))
    spread(x_view, g("axs"), g("axr"))

    for k, (a, b) in enumerate(PEERS):
        mlp_columns_to(me.flip(a, b), k, start_remote(me.flip(a, b)))
    mlp_columns_to(me, 7, start_local)

    for k, (a, b) in enumerate(PEERS):
        spot = me.flip(a, b)
        arrived(g("gs").at[me.group(), spot.member()], g("g1s").at[k], g("g1r").at[k], spot)
    gain_local.wait()
    across(gain_views, g("g2s"), g("g2r"))

    def rows_of(spot):
        return pl.ds(pl.multiple_of((spot.p * 16 + spot.zh * 8 + spot.zl * 4 + spot.y * 2 + spot.x) * 32, 32), 32)

    def first_end(kind, name, pieces):
        for k, (a, b) in enumerate(PEERS + ((0, 0),)):
            rows = rows_of(me.flip(a, b))
            for i in range(pieces):
                ref = g(name).at[rows, pl.ds(i * 128, 128)]
                pltpu.make_async_copy(ref, ref, g("w1" + kind + "r").at[k, i]).wait()

    first_end("q", "qkvb", 3)
    across(qkv_views, g("w2qs"), g("w2qr"))
    spread_on(x_view, g("axs"), g("axr"))
    reshard(g("og_h"), g("ogf"), g("os"), g("or"))
    first_end("m", "gub", 8)
    across(gu_views, g("w2ms"), g("w2mr"))
    down_mine = down_views(me)[0]
    down_local = pltpu.make_async_copy(g("wd_h"), down_mine, g("wdr").at[3, 0])
    down_local.start()
    send(g("wd_h"), down_mine, g("wds").at[0, 0], g("wdr").at[0, 0], me.flip(0, 8))
    send(g("wd_h"), down_mine, g("wds").at[1, 0], g("wdr").at[1, 0], me.flip(0, 2))

    across_on(gain_views, g("g2s"), g("g2r"))
    across_on(qkv_views, g("w2qs"), g("w2qr"))

    pltpu.make_async_copy(g("meta_h"), g("meta").at[p], g("mr").at[1]).wait()
    arrived(g("meta").at[1 - p], g("ms").at[0], g("mr").at[0], partner)
    for copy in locals_:
        copy.wait()
    ids = g("meta")[y, pl.ds(2 + zh, 1), :]

    def mask(width):
        return lambda a: (ids[:, 0:width] == a).astype(F32)

    def enter_columns(items):
        rows = [pick(item, mask(item.shape[-1])) for item in items]
        width = rows[0].shape[-1]
        rows.append(jnp.zeros((128 - 16 * len(rows), width), F32))
        return jnp.transpose(jnp.concatenate(rows, axis=0)).astype(BF)

    def leave_rows(ref, first, items):
        ref[pl.ds(first, 128), :] = jnp.zeros((128, ref.shape[1]), BF)
        column = 0
        for i, item in enumerate(items):
            width = item.shape[-1]
            ref[pl.ds(first + 16 * i, 16), pl.ds(column, width)] = (SCALE * pick(item, mask(width))).astype(BF)
            column += width

    g("qkvb")[pl.ds(0, 1024), pl.ds(384, 128)] = enter_columns([g("ae").at[i] for i in range(3)])
    leave_rows(g("qkvb"), 1024, [g("al").at[i] for i in range(3)])
    g("ob")[pl.ds(0, 1024), pl.ds(1024, 128)] = enter_columns([g("oe")])
    leave_rows(g("ob"), 1024, [g("ol")])
    g("gub")[pl.ds(0, 1024), pl.ds(1024, 128)] = enter_columns([g("me").at[i] for i in range(2)])
    leave_rows(g("gub"), 1024, [g("ml").at[i] for i in range(2)])
    g("db")[pl.ds(0, 512), pl.ds(1024, 128)] = enter_columns([g("le")])
    leave_rows(g("db"), 512, [g("ll")])

    seg_row = g("meta")[y, pl.ds(zh, 1), :]
    g("segc")[...] = jnp.transpose(jnp.broadcast_to(seg_row.astype(F32), (128, 1024)))

    across_end(gain_views, g("g2s"), g("g2r"))
    gains = jnp.sum(jnp.sum(g("gs")[...], axis=0), axis=0)
    gain_one = jnp.concatenate([gains[i : i + 1] for i in range(8)], axis=1)
    gain_two = jnp.concatenate([gains[i : i + 1] for i in range(8, 16)], axis=1)

    spread_end(x_view, g("axs"), g("axr"))
    reshard_wait(g("ogf"), g("or"))
    spread(og_view, g("aos"), g("aor"))
    across_end(qkv_views, g("w2qs"), g("w2qr"))

    def qkv_tile(t, carry):
        rows = part(t, 256)
        held = g("xf")[rows, :].astype(F32)
        inverse = lax.rsqrt(jnp.mean(held * held, axis=-1, keepdims=True) + EPS)
        normed = (held * inverse * gain_one).astype(BF)
        both = dot(normed, g("qkvb")[0:1024, :])
        inner = both[:, 384:512]
        qkv = both[:, 0:384] + dot(inner.astype(BF), g("qkvb")[1024:1152, 0:384])
        g("r1t")[:, rows] = jnp.transpose(inner).astype(BF)
        g("qb")[rows, :] = (qkv[:, 0:128].astype(BF).astype(F32) * 0.125).astype(BF)
        g("kb")[rows, :] = qkv[:, 128:256].astype(BF)
        g("vb")[rows, :] = qkv[:, 256:384].astype(BF)
        g("kt")[:, rows] = jnp.transpose(qkv[:, 128:256]).astype(BF)
        g("vt")[:, rows] = jnp.transpose(qkv[:, 256:384]).astype(BF)
        return carry

    lax.fori_loop(0, 4, qkv_tile, 0)

    out_local.wait()
    across_on(out_views, g("wos"), g("wor"))
    across_end(out_views, g("wos"), g("wor"))
    for q in range(4):
        fl = (0, 2 * (q % 2) + 8 * (q // 2))
        spread(lambda spot, fl=fl: out_views(spot.flip(*fl))[0], g("aws").at[q], g("awr").at[q])

    head_of = lax.broadcasted_iota(jnp.int32, (256, 128), 1) // HD

    def attend_tile(t, carry):
        rows = part(t, 256)
        queries = g("qb")[rows, :]
        same = g("segc")[:, 0:1] == g("meta")[y, pl.ds(zh, 1), rows].astype(F32)
        mixed = []
        for h in range(2):
            mine = jnp.where(head_of == h, queries.astype(F32), 0.0).astype(BF)
            scores = jnp.where(same, dot_t(g("kb")[...], mine), NEG)
            weights = jnp.exp(scores - jnp.max(scores, axis=0, keepdims=True))
            probs = (weights * (1.0 / jnp.sum(weights, axis=0, keepdims=True))).astype(BF)
            g("pr")[2 * t + h] = probs
            mixed.append(dot(g("vt")[h * HD : (h + 1) * HD, :], probs))
        mixed = jnp.concatenate(mixed, axis=0)
        g("att")[t] = mixed
        g("ath")[rows, :] = jnp.transpose(mixed).astype(BF)
        return carry

    lax.fori_loop(0, 4, attend_tile, 0)

    for k, (a, b) in enumerate(PEERS):
        spot = me.flip(a, b)
        send(g("ath").at[part(spot.member(), 128)], g("ato").at[:, own], g("a1s").at[k], g("a1r").at[k], spot)
    mine_local = pltpu.make_async_copy(g("ath").at[own], g("ato").at[:, own], g("a1r").at[7])
    mine_local.start()

    spread_on(og_view, g("aos"), g("aor"))
    for q in range(4):
        fl = (0, 2 * (q % 2) + 8 * (q // 2))
        spread_on(lambda spot, fl=fl: out_views(spot.flip(*fl))[0], g("aws").at[q], g("awr").at[q])
    across_on(gu_views, g("w2ms"), g("w2mr"))
    for q in range(4):
        fl = (0, 2 * (q % 2) + 8 * (q // 2))
        spread_end(lambda spot, fl=fl: out_views(spot.flip(*fl))[0], g("aws").at[q], g("awr").at[q])
    mine_local.wait()
    for k, (a, b) in enumerate(PEERS):
        spot = me.flip(a, b)
        arrived(g("ato").at[:, part(spot.member(), 128)], g("a1s").at[k], g("a1r").at[k], spot)

    start_rows = g("xf")[own, :].astype(F32)
    both = dot(g("ato")[...], g("ob")[0:1024, :])
    out_inner = both[:, 1024:1152]
    middle = start_rows + both[:, 0:1024] + dot(out_inner.astype(BF), g("ob")[1024:1152, 0:1024])
    g("mid")[...] = middle
    inverse = lax.rsqrt(jnp.mean(middle * middle, axis=-1, keepdims=True) + EPS)
    g("n2f")[own, :] = (middle * inverse * gain_two).astype(BF)
    g("rot")[...] = jnp.transpose(out_inner).astype(BF)
    spread(n2_view, g("ans"), g("anr"))

    down_local.wait()
    across_on(down_views, g("wds"), g("wdr"))
    across_end(gu_views, g("w2ms"), g("w2mr"))
    across_end(down_views, g("wds"), g("wdr"))
    spread_end(og_view, g("aos"), g("aor"))
    spread_on(n2_view, g("ans"), g("anr"))
    spread_end(n2_view, g("ans"), g("anr"))

    g("cml")[...] = jnp.zeros((128, 1024), F32)
    g("cle")[...] = jnp.zeros((128, 512), F32)

    def mlp_tile(i, carry):
        rows = part(lax.rem((1 - p) * 2 + i, 4), 256)
        both = dot(g("n2f")[rows, :], g("gub")[0:1024, :])
        inner = both[:, 1024:1152]
        pair = both[:, 0:1024] + dot(inner.astype(BF), g("gub")[1024:1152, 0:1024])
        gate, upper = pair[:, 0:512], pair[:, 512:1024]
        sigma = jax.nn.sigmoid(gate)
        hidden = (gate * sigma * upper).astype(BF)
        g("zd")[rows, :] = dot(hidden, g("db")[0:512, :]).astype(BF)
        back = dot_t(g("ogf")[rows, :], g("db")[:, 0:1024])
        inner_back = back[:, 512:640]
        hidden_grad = back[:, 0:512] + dot_t(inner_back.astype(BF), g("db")[0:512, 1024:1152])
        gate_grad = (hidden_grad * upper * sigma * (1.0 + gate * (1.0 - sigma))).astype(BF)
        up_grad = (hidden_grad * gate * sigma).astype(BF)
        pair_grad = jnp.concatenate([gate_grad, up_grad], axis=1)
        g("zn")[rows, :] = dot_t(pair_grad, g("gub")[:, 0:1024]).astype(BF)
        g("cml")[...] += dot(jnp.transpose(inner).astype(BF), pair_grad)
        g("cle")[...] += dot(jnp.transpose(inner_back).astype(BF), hidden)
        return carry

    def pair_send(name, k):
        send(g(name).at[part(1 - p, 512)], g("rp").at[k], g("rps").at[k], g("rpr").at[k], partner)

    def chip_send(name, k):
        arrived(g("rp").at[k], g("rps").at[k], g("rpr").at[k], partner)

        def add(i, carry):
            rows = part(i, 128)
            g("rc")[k, rows, :] = (
                g(name)[part(p * 4 + i, 128), :].astype(F32) + g("rp")[k, rows, :].astype(F32)
            ).astype(BF)
            return carry

        lax.fori_loop(0, 4, add, 0)
        for i, b in enumerate(SAME):
            spot = me.flip(0, b)
            send(g("rc").at[k, part(spot.zl * 2 + spot.x, 128)], g("rr").at[k, i], g("rrs").at[k, i], g("rrr").at[k, i], spot)

    def summed(name, k):
        for i, b in enumerate(SAME):
            arrived(g("rr").at[k, i], g("rrs").at[k, i], g("rrr").at[k, i], me.flip(0, b))
        total = g(name)[own, :].astype(F32) + g("rp")[k, part(zl * 2 + x, 128), :].astype(F32)
        for i in range(3):
            total = total + g("rr")[k, i].astype(F32)
        return total

    lax.fori_loop(0, 2, mlp_tile, 0)
    pair_send("zn", 0)
    pair_send("zd", 1)
    lax.fori_loop(2, 4, mlp_tile, 0)
    chip_send("zn", 0)
    for i in range(2):
        g("gd")[:, pl.ds(1408 + i * 512, 512)] = (SCALE * g("cml")[i * 16 : (i + 1) * 16, i * 512 : (i + 1) * 512]).astype(BF)
    g("gd")[:, pl.ds(2432, 512)] = g("cle")[0:16, :].astype(BF)

    own_grad = g("ogf")[own, :].astype(F32)
    total = summed("zn", 0)
    inner_back = total[:, 1024:1152]
    normed_grad = total[:, 0:1024] + dot_t(inner_back.astype(BF), g("gub")[0:1024, 1024:1152])
    middle = g("mid")[...]
    inverse = lax.rsqrt(jnp.mean(middle * middle, axis=-1, keepdims=True) + EPS)
    middle_grad = own_grad + norm_back(middle, inverse, gain_two, normed_grad)
    g("mg")[...] = middle_grad
    rounded = middle_grad.astype(BF)
    both = dot_t(rounded, g("ob")[:, 0:1024])
    out_back = both[:, 1024:1152]
    g("gao")[...] = (both[:, 0:1024] + dot_t(out_back.astype(BF), g("ob")[0:1024, 1024:1152])).astype(BF)
    for k, (a, b) in enumerate(PEERS):
        spot = me.flip(a, b)
        send(g("gao").at[:, part(spot.member(), 128)], g("gah").at[own], g("a2s").at[k], g("a2r").at[k], spot)
    mine_local = pltpu.make_async_copy(g("gao").at[:, own], g("gah").at[own], g("a2r").at[7])
    mine_local.start()
    chip_send("zd", 1)
    mlp_enter = dot(jnp.transpose(inner_back).astype(BF), g("n2f")[own, :])
    out_enter = dot(jnp.transpose(out_back).astype(BF), g("ato")[...])
    out_leave = SCALE * dot(g("rot")[...], rounded)
    g("gp")[4] = mlp_enter[0:16].astype(BF)
    g("gp")[5] = mlp_enter[16:32].astype(BF)
    g("gp")[3] = out_enter[0:16].astype(BF)
    g("gp")[6] = out_leave[0:16].astype(BF)
    mine_local.wait()
    for k, (a, b) in enumerate(PEERS):
        spot = me.flip(a, b)
        arrived(g("gah").at[part(spot.member(), 128)], g("a2s").at[k], g("a2r").at[k], spot)

    g("gk")[...] = jnp.zeros((1024, 128), F32)
    g("gv")[...] = jnp.zeros((1024, 128), F32)

    def attend_back_tile(t, carry):
        rows = part(t, 256)
        queries, grads = g("qb")[rows, :].astype(F32), g("gah")[rows, :].astype(F32)
        delta_parts = jnp.transpose(grads) * g("att")[t]
        query_grad = []
        for h in range(2):
            mine = jnp.where(head_of == h, queries, 0.0).astype(BF)
            grad = jnp.where(head_of == h, grads, 0.0).astype(BF)
            probs = g("pr")[2 * t + h]
            delta = jnp.sum(delta_parts[h * HD : (h + 1) * HD], axis=0, keepdims=True)
            score_grad = (probs.astype(F32) * (dot_t(g("vb")[...], grad) - delta)).astype(BF)
            g("gk")[...] += dot(score_grad, mine)
            g("gv")[...] += dot(probs, grad)
            query_grad.append(dot(g("kt")[h * HD : (h + 1) * HD, :], score_grad))
        g("gq")[rows, pl.ds(0, 128)] = (jnp.transpose(jnp.concatenate(query_grad, axis=0)) * 0.125).astype(BF)
        return carry

    lax.fori_loop(0, 4, attend_back_tile, 0)
    g("gq")[:, pl.ds(128, 128)] = g("gk")[...].astype(BF)
    g("gq")[:, pl.ds(256, 128)] = g("gv")[...].astype(BF)

    def qkv_back_tile(i, carry):
        rows = part(lax.rem((1 - p) * 2 + i, 4), 256)
        g("zq")[rows, :] = dot_t(g("gq")[rows, :], g("qkvb")[:, 0:384]).astype(BF)
        return carry

    lax.fori_loop(0, 2, qkv_back_tile, 0)
    pair_send("zq", 2)
    lax.fori_loop(2, 4, qkv_back_tile, 0)
    chip_send("zq", 2)

    leave = SCALE * dot(g("r1t")[...], g("gq")[...])
    for i in range(3):
        g("gd")[:, pl.ds(1024 + i * 128, 128)] = leave[i * 16 : (i + 1) * 16, i * 128 : (i + 1) * 128].astype(BF)
    total = summed("zd", 1)
    last_inner = total[:, 1024:1152]
    g("outv")[...] = (g("mid")[...] + total[:, 0:1024] + dot(last_inner.astype(BF), g("db")[512:640, 0:1024])).astype(BF)
    g("gp")[7] = (SCALE * dot(jnp.transpose(last_inner).astype(BF), g("ogf")[own, :]))[0:16].astype(BF)

    def give_back(src, dst, ssem, rsem):
        spot_same, spot_other = part(zh, 64), part(1 - zh, 64)

        @pl.when(p == y)
        def _():
            pltpu.make_async_copy(src.at[spot_same], dst.at[zh], rsem.at[0]).start()
            remote(src.at[spot_other], dst.at[zh], ssem.at[1], rsem.at[1], me.flip(0, 8)).start()

        @pl.when(p != y)
        def _():
            remote(src.at[spot_same], dst.at[zh], ssem.at[0], rsem.at[0], me.flip(1, 2)).start()
            remote(src.at[spot_other], dst.at[zh], ssem.at[1], rsem.at[1], me.flip(1, 10)).start()

    def give_back_wait(src, dst, ssem, rsem):
        pltpu.make_async_copy(dst.at[zh], dst.at[zh], rsem.at[0]).wait()
        pltpu.make_async_copy(dst.at[1 - zh], dst.at[1 - zh], rsem.at[1]).wait()

        @pl.when(p != y)
        def _():
            remote(src.at[part(zh, 64)], src.at[part(zh, 64)], ssem.at[0], rsem.at[0], me.flip(1, 2)).wait_send()

        remote(src.at[part(zh, 64)], src.at[part(zh, 64)], ssem.at[1], rsem.at[1], me.flip(0, 8)).wait_send()

    give_back(g("outv"), g("out_o"), g("bos"), g("bor"))

    total = summed("zq", 2)
    inner_back = total[:, 1024:1152]
    normed_grad = total[:, 0:1024] + dot_t(inner_back.astype(BF), g("qkvb")[0:1024, 384:512])
    start_rows = g("xf")[own, :].astype(F32)
    inverse = lax.rsqrt(jnp.mean(start_rows * start_rows, axis=-1, keepdims=True) + EPS)
    normed = (start_rows * inverse * gain_one).astype(BF)
    g("igv")[...] = (g("mg")[...] + norm_back(start_rows, inverse, gain_one, normed_grad)).astype(BF)
    give_back(g("igv"), g("ig_o"), g("bis"), g("bir"))
    attn_enter = dot(jnp.transpose(inner_back).astype(BF), normed)
    for i in range(3):
        g("gp")[i] = attn_enter[i * 16 : (i + 1) * 16].astype(BF)

    for k, (a, b) in enumerate(PEERS):
        spot = me.flip(a, b)
        send(g("gp").at[spot.member()], g("gr").at[k], g("gps").at[k], g("gpr").at[k], spot)
    block = g("gp")[j].astype(F32)
    for k, (a, b) in enumerate(PEERS):
        arrived(g("gr").at[k], g("gps").at[k], g("gpr").at[k], me.flip(a, b))
        block = block + g("gr")[k].astype(F32)
    g("gd")[:, pl.ds(0, 1024)] = block.astype(BF)

    def share_view(spot):
        return g("gall_o").at[spot.group(), spot.member()]

    share_local = pltpu.make_async_copy(g("gd"), share_view(me), g("gar").at[3, 0])
    share_local.start()
    for k, (a, b) in enumerate(ACROSS):
        send(g("gd"), share_view(me), g("gas").at[k, 0], g("gar").at[k, 0], me.flip(a, b))
    share_local.wait()
    spread(share_view, g("gbs").at[3], g("gbr").at[3])
    for k, (a, b) in enumerate(ACROSS):
        arrived(share_view(me.flip(a, b)), g("gas").at[k, 0], g("gar").at[k, 0], me.flip(a, b))
        spread(lambda spot, b=b: share_view(spot.flip(0, b)), g("gbs").at[k], g("gbr").at[k])
    flips = {0: 2, 1: 8, 2: 10, 3: 0}
    for k in (3, 0, 1, 2):
        spread_on(lambda spot, k=k: share_view(spot.flip(0, flips[k])), g("gbs").at[k], g("gbr").at[k])
    for k in (3, 0, 1, 2):
        spread_end(lambda spot, k=k: share_view(spot.flip(0, flips[k])), g("gbs").at[k], g("gbr").at[k])

    meta_out = pltpu.make_async_copy(g("meta"), g("meta_o"), g("mr").at[2])
    meta_out.start()
    give_back_wait(g("outv"), g("out_o"), g("bos"), g("bor"))
    give_back_wait(g("igv"), g("ig_o"), g("bis"), g("bir"))
    reshard_sent(g("x_h"), g("xs"))
    reshard_sent(g("og_h"), g("os"))
    for copy in late:
        copy.wait_send()
    meta_out.wait()


def layer_call(*args):
    V, S = pltpu.VMEM, pltpu.SemaphoreType.DMA
    inputs = [
        "x_h", "og_h", "meta_h", "gain_h", "wq_h", "wk_h", "wv_h", "wo_h", "wg_h", "wu_h", "wd_h", "ae_h", "al_h", "oe_h", "ol_h", "me_h", "ml_h", "le_h", "ll_h",
    ]
    outputs = {
        "out_o": ((2, 64, 1024), BF),
        "ig_o": ((2, 64, 1024), BF),
        "gall_o": ((4, 8, 16, GW), BF),
        "meta_o": ((2, 8, 1024), jnp.int32),
    }
    scratch = {
        "xf": V((1024, 1024), BF), "ogf": V((1024, 1024), BF), "n2f": V((1024, 1024), BF),
        "qkvb": V((1152, 512), BF), "ob": V((1152, 1152), BF), "gub": V((1152, 1152), BF), "db": V((640, 1152), BF),
        "ae": V((3, 8, 16, 1024), BF), "al": V((3, 8, 16, 128), BF), "oe": V((8, 16, 1024), BF), "ol": V((8, 16, 1024), BF),
        "me": V((2, 8, 16, 1024), BF), "ml": V((2, 8, 16, 512), BF), "le": V((8, 16, 512), BF), "ll": V((8, 16, 1024), BF),
        "meta": V((2, 8, 1024), jnp.int32), "gs": V((4, 8, 16, 128), F32), "segc": V((1024, 128), F32),
        "qb": V((1024, 128), BF), "kb": V((1024, 128), BF), "vb": V((1024, 128), BF), "kt": V((128, 1024), BF),
        "vt": V((128, 1024), BF), "r1t": V((128, 1024), BF), "pr": V((8, 1024, 256), BF), "att": V((4, 128, 256), F32),
        "ath": V((1024, 128), BF), "ato": V((128, 1024), BF), "mid": V((128, 1024), F32), "mg": V((128, 1024), F32),
        "rot": V((128, 128), BF), "zn": V((1024, 1152), BF), "zd": V((1024, 1152), BF), "zq": V((1024, 1152), BF),
        "rp": V((3, 512, 1152), BF), "rc": V((3, 512, 1152), BF), "rr": V((3, 3, 128, 1152), BF),
        "cml": V((128, 1024), F32), "cle": V((128, 512), F32), "gao": V((128, 1024), BF), "gah": V((1024, 128), BF),
        "gk": V((1024, 128), F32), "gv": V((1024, 128), F32), "gq": V((1024, 384), BF), "outv": V((128, 1024), BF),
        "igv": V((128, 1024), BF), "gp": V((8, 16, 1024), BF), "gr": V((7, 16, 1024), BF), "gd": V((16, GW), BF),
        "la": S((16,)), "xs": S((2,)), "xr": S((2,)), "os": S((2,)), "or": S((2,)), "g1s": S((7,)), "g1r": S((8,)),
        "g2s": S((3, 1)), "g2r": S((3, 1)), "w1qs": S((8, 3)), "w1qr": S((8, 3)), "w1ms": S((8, 8)), "w1mr": S((8, 8)),
        "w2qs": S((3, 4)), "w2qr": S((3, 4)), "w2ms": S((3, 4)), "w2mr": S((3, 4)), "wos": S((3, 1)), "wor": S((4, 1)),
        "wds": S((3, 1)), "wdr": S((4, 1)), "ms": S((1,)), "mr": S((3,)), "axs": S((7,)), "axr": S((7,)),
        "aos": S((7,)), "aor": S((7,)), "ans": S((7,)), "anr": S((7,)), "aws": S((4, 7)), "awr": S((4, 7)),
        "a1s": S((7,)), "a1r": S((8,)), "a2s": S((7,)), "a2r": S((8,)), "rps": S((3,)), "rpr": S((3,)),
        "rrs": S((3, 3)), "rrr": S((3, 3)), "bos": S((2,)), "bor": S((2,)), "bis": S((2,)), "bir": S((2,)),
        "gps": S((7,)), "gpr": S((7,)), "gas": S((3, 1)), "gar": S((4, 1)), "gbs": S((4, 7)), "gbr": S((4, 7)),
    }
    names = inputs + list(outputs) + list(scratch)
    return pl.pallas_call(
        functools.partial(layer_kernel, names),
        out_shape=[jax.ShapeDtypeStruct(shape, dtype) for shape, dtype in outputs.values()],
        in_specs=[pl.BlockSpec(memory_space=pl.ANY)] * len(inputs),
        out_specs=[pl.BlockSpec(memory_space=pl.ANY)] * len(outputs),
        scratch_shapes=list(scratch.values()),
        compiler_params=pltpu.CompilerParams(collective_id=0, has_side_effects=True, vmem_limit_bytes=63 * 2**20),
        name="layer",
    )(*args)


def place_kernel(ids, gall, out_i, ig_i, out_o, ig_o, ae_o, al_o, oe_o, ol_o, me_o, ml_o, le_o, ll_o):
    a = pl.program_id(0)
    outs = (ae_o, al_o, oe_o, ol_o, me_o, ml_o, le_o, ll_o)

    @pl.when(a == 0)
    def _():
        out_o[...] = out_i[...]
        ig_o[...] = ig_i[...].astype(F32)

    for ref in outs:
        ref[...] = jnp.zeros(ref.shape, F32)
    for group in range(4):
        ident = ids[group % 2, 2 + group // 2, 0]

        @pl.when(ident == a)
        def _(group=group):
            def block(member, first, width):
                return gall[group, member, :, first : first + width].astype(F32)

            for i in range(3):
                ae_o[i, 0] += block(i, 0, 1024)
                for m in range(8):
                    al_o[i, 0, :, m * 128 : (m + 1) * 128] += block(m, 1024 + i * 128, 128)
            oe_o[0] += block(3, 0, 1024)
            ol_o[0] += block(6, 0, 1024)
            ll_o[0] += block(7, 0, 1024)
            for i in range(2):
                me_o[i, 0] += block(4 + i, 0, 1024)
            for m in range(8):
                for q in range(4):
                    fb = ((m // 4) * 16 + (q // 2) * 8 + (m // 2 % 2) * 4 + (q % 2) * 2 + m % 2) * 128
                    le_o[0, :, fb : fb + 128] += block(m, 2432 + q * 128, 128)
                    for i in range(2):
                        ml_o[i, 0, :, fb : fb + 128] += block(m, 1408 + i * 512 + q * 128, 128)


def place_call(meta, gall, out, ig):
    def whole(shape):
        return pl.BlockSpec(shape, lambda a, ids: (0,) * len(shape))

    def four(n, width):
        return pl.BlockSpec((n, 1, 16, width), lambda a, ids: (0, a, 0, 0))

    def three(width):
        return pl.BlockSpec((1, 16, width), lambda a, ids: (a, 0, 0))

    shapes = ((3, 8, 16, 1024), (3, 8, 16, 1024), (8, 16, 1024), (8, 16, 1024), (2, 8, 16, 1024), (2, 8, 16, 4096), (8, 16, 4096), (8, 16, 1024))
    return pl.pallas_call(
        place_kernel,
        out_shape=[jax.ShapeDtypeStruct((2, 64, 1024), BF), jax.ShapeDtypeStruct((2, 64, 1024), F32)]
        + [jax.ShapeDtypeStruct(shape, F32) for shape in shapes],
        grid_spec=pltpu.PrefetchScalarGridSpec(
            num_scalar_prefetch=1,
            grid=(8,),
            in_specs=[whole((4, 8, 16, GW)), whole((2, 64, 1024)), whole((2, 64, 1024))],
            out_specs=[whole((2, 64, 1024)), whole((2, 64, 1024)), four(3, 1024), four(3, 1024), three(1024), three(1024),
                       four(2, 1024), four(2, 4096), three(4096), three(1024)],
        ),
        compiler_params=pltpu.CompilerParams(vmem_limit_bytes=32 * 2**20),
        name="place",
    )(meta, gall, out, ig)


def grouped(
    inputs, segment_ids, adapter_ids, w_query, w_key, w_value, w_out, w_gate, w_up, w_down, gain_attn, gain_ffn,
    attn_enter, attn_leave, out_enter, out_leave, mlp_enter, mlp_leave, last_enter, last_leave, out_grad,
):
    flat = lax.axis_index("dp") * 16 + lax.axis_index("ctx")
    seg = segment_ids[:, 0].reshape(2, 2, 2, 2, 2, 64)
    seg = jnp.transpose(seg, (0, 3, 2, 4, 1, 5)).reshape(2, 1024)
    ids = jnp.broadcast_to(adapter_ids, (2, 1024))
    meta = jnp.concatenate([seg, ids, jnp.zeros((4, 1024), jnp.int32)], axis=0)
    at = lax.broadcasted_iota(jnp.int32, (32, 32), 0) == flat
    gains = jnp.concatenate(
        [jnp.where(at, gain.astype(F32)[None, :], 0.0).reshape(8, 128) for gain in (gain_attn, gain_ffn)], axis=0
    )
    out, ig, gall, meta_all = layer_call(
        inputs[:, 0], out_grad[:, 0], meta, gains, w_query, w_key, w_value, w_out, w_gate, w_up, w_down,
        attn_enter, attn_leave, out_enter, out_leave, mlp_enter, mlp_leave, last_enter, last_leave,
    )
    out, ig, *grads = place_call(meta_all, gall, out, ig)
    return (out[:, None], ig[:, None], *grads)


def solution(mesh):
    def chosen(*args):
        sizes = (mesh.shape["dp"], mesh.shape["ctx"], *args[0].shape)
        return (grouped if sizes == (2, 16, 2, 1, 64, 1024) else per_device)(*args)

    return jax.shard_map(
        chosen,
        mesh=mesh,
        in_specs=(
            P(None, "dp", "ctx", None),
            P(None, "dp", None),
            P(None, "dp"),
            P(("dp", "ctx"), None),
            P(("dp", "ctx"), None),
            P(("dp", "ctx"), None),
            P(("dp", "ctx"), None),
            P(("dp", "ctx"), None),
            P(("dp", "ctx"), None),
            P(("dp", "ctx"), None),
            P(("dp", "ctx")),
            P(("dp", "ctx")),
            P(),
            P(),
            P(),
            P(),
            P(),
            P(),
            P(),
            P(),
            P(None, "dp", "ctx", None),
        ),
        out_specs=(
            P(None, "dp", "ctx", None),
            P(None, "dp", "ctx", None),
            P(),
            P(),
            P(),
            P(),
            P(),
            P(),
            P(),
            P(),
        ),
        check_vma=False,
    )
```

```python
import functools
import types

import jax
import jax.numpy as jnp
from jax import lax
from jax.experimental import pallas as pl
from jax.experimental.pallas import tpu as pltpu
from jax.sharding import PartitionSpec as P

H = 16
HD = 64


EPS = 1e-05
NEG = -1000000000.0
SCALE = 0.5


def rms_norm(rows, gain):
    inverse = lax.rsqrt(jnp.mean(rows * rows, axis=-1, keepdims=True) + EPS)
    return (rows * inverse * gain, inverse)


def norm_back(rows, inverse, gain, grad):
    weighted = grad * gain
    return inverse * weighted - rows * inverse**3 * jnp.mean(
        rows * weighted, axis=-1, keepdims=True
    )


def project(rows, weight, enter, leave):
    direct = jnp.einsum("sci,io->sco", rows, weight, preferred_element_type=jnp.float32)
    inner = jnp.einsum("sci,sri->scr", rows, enter, preferred_element_type=jnp.float32).astype(
        jnp.bfloat16
    )
    return (
        direct
        + SCALE * jnp.einsum("scr,sro->sco", inner, leave, preferred_element_type=jnp.float32),
        inner,
    )


def project_back(rows, inner, weight, enter, leave, grad):
    inner_grad = (
        SCALE * jnp.einsum("sco,sro->scr", grad, leave, preferred_element_type=jnp.float32)
    ).astype(jnp.bfloat16)
    rows_grad = jnp.einsum("sco,io->sci", grad, weight, preferred_element_type=jnp.float32)
    rows_grad = rows_grad + jnp.einsum(
        "scr,sri->sci", inner_grad, enter, preferred_element_type=jnp.float32
    )
    enter_grad = jnp.einsum("scr,sci->sri", inner_grad, rows, preferred_element_type=jnp.float32)
    leave_grad = SCALE * jnp.einsum("scr,sco->sro", inner, grad, preferred_element_type=jnp.float32)
    return (rows_grad, enter_grad, leave_grad)


def masked_scores(query_heads, key_block, seg_query, seg_key):
    seqs = query_heads.shape[0]
    key_heads = key_block.reshape(seqs, -1, H, HD)
    scores = (
        jnp.einsum("sqhd,skhd->shqk", query_heads, key_heads, preferred_element_type=jnp.float32)
        * 0.125
    )
    same = seg_query[:, None, :, None] == seg_key[:, None, None, :]
    return (jnp.where(same, scores, NEG), key_heads)


def forward_block(state, query_heads, seg_query, key_block, value_block, seg_key):
    best, total, accum = state
    seqs = query_heads.shape[0]
    scores, key_heads = masked_scores(query_heads, key_block, seg_query, seg_key)
    value_heads = value_block.reshape(seqs, -1, H, HD)
    new_best = jnp.maximum(best, jnp.max(scores, axis=-1))
    factor = jnp.exp(best - new_best)
    weights = jnp.exp(scores - new_best[..., None])
    total = total * factor + jnp.sum(weights, axis=-1)
    mixed = jnp.einsum(
        "shqk,skhd->sqhd",
        weights.astype(jnp.bfloat16),
        value_heads,
        preferred_element_type=jnp.float32,
    )
    accum = accum * jnp.transpose(factor, (0, 2, 1))[..., None] + mixed
    return (new_best, total, accum)


def attend(query, key, value, seg_rows, my_start):
    seqs, rows, width = query.shape
    query_heads = query.reshape(seqs, rows, H, HD)
    seg_query = lax.dynamic_slice_in_dim(seg_rows, my_start, rows, 1)
    state = (
        jnp.full((seqs, H, rows), -1e30, jnp.float32),
        jnp.zeros((seqs, H, rows), jnp.float32),
        jnp.zeros((seqs, rows, H, HD), jnp.float32),
    )

    def fold(carry, piece, start):
        key_piece, value_piece = piece
        count = key_piece.shape[1]
        block = 512

        def advance(index, inner_state):
            offset = index * block
            key_block = lax.dynamic_slice_in_dim(key_piece, offset, block, 1)
            value_block = lax.dynamic_slice_in_dim(value_piece, offset, block, 1)
            seg_key = lax.dynamic_slice_in_dim(seg_rows, offset, block, 1)
            return forward_block(
                inner_state, query_heads, seg_query, key_block, value_block, seg_key
            )

        return lax.fori_loop(0, count // block, advance, carry)

    best, total, accum = fold(
        state,
        (
            lax.all_gather(key, "ctx", axis=1, tiled=True),
            lax.all_gather(value, "ctx", axis=1, tiled=True),
        ),
        jnp.int32(0),
    )
    output = accum / jnp.transpose(total, (0, 2, 1))[..., None]
    return (output, best + jnp.log(total))


def block_grads(
    query_heads, grad_heads, log_total, delta, seg_query, key_block, value_block, seg_key
):
    seqs = query_heads.shape[0]
    scores, key_heads = masked_scores(query_heads, key_block, seg_query, seg_key)
    value_heads = value_block.reshape(seqs, -1, H, HD)
    probs = jnp.exp(scores - log_total[..., None])
    value_part = jnp.einsum(
        "shqk,sqhd->skhd",
        probs.astype(jnp.bfloat16),
        grad_heads,
        preferred_element_type=jnp.float32,
    )
    prob_grad = jnp.einsum(
        "sqhd,skhd->shqk", grad_heads, value_heads, preferred_element_type=jnp.float32
    )
    score_grad = (probs * (prob_grad - delta[..., None])).astype(jnp.bfloat16)
    query_part = 0.125 * jnp.einsum(
        "shqk,skhd->sqhd", score_grad, key_heads, preferred_element_type=jnp.float32
    )
    key_part = 0.125 * jnp.einsum(
        "shqk,sqhd->skhd", score_grad, query_heads, preferred_element_type=jnp.float32
    )
    return (query_part, key_part, value_part)


def attend_back(query, key, value, grad, output, log_total, seg_rows, my_start):
    seqs, rows, width = query.shape
    length = seg_rows.shape[1]
    query_heads = query.reshape(seqs, rows, H, HD)
    grad_heads = grad.reshape(seqs, rows, H, HD)
    seg_query = lax.dynamic_slice_in_dim(seg_rows, my_start, rows, 1)
    delta = jnp.transpose(jnp.sum(grad_heads.astype(jnp.float32) * output, axis=-1), (0, 2, 1))
    state = (
        jnp.zeros((seqs, rows, H, HD), jnp.float32),
        jnp.zeros((seqs, length, width), jnp.float32),
        jnp.zeros((seqs, length, width), jnp.float32),
    )

    def fold(carry, piece, start):
        key_piece, value_piece = piece
        count = key_piece.shape[1]
        block = 512

        def advance(index, inner_state):
            offset = index * block
            key_block = lax.dynamic_slice_in_dim(key_piece, offset, block, 1)
            value_block = lax.dynamic_slice_in_dim(value_piece, offset, block, 1)
            seg_key = lax.dynamic_slice_in_dim(seg_rows, offset, block, 1)
            query_part, key_part, value_part = block_grads(
                query_heads,
                grad_heads,
                log_total,
                delta,
                seg_query,
                key_block,
                value_block,
                seg_key,
            )
            query_grad, key_all, value_all = inner_state
            key_old = lax.dynamic_slice_in_dim(key_all, offset, block, 1)
            key_all = lax.dynamic_update_slice_in_dim(
                key_all, key_old + key_part.reshape(seqs, block, width), offset, 1
            )
            value_old = lax.dynamic_slice_in_dim(value_all, offset, block, 1)
            value_all = lax.dynamic_update_slice_in_dim(
                value_all, value_old + value_part.reshape(seqs, block, width), offset, 1
            )
            return (query_grad + query_part, key_all, value_all)

        return lax.fori_loop(0, count // block, advance, carry)

    folded = fold(
        state,
        (
            lax.all_gather(key, "ctx", axis=1, tiled=True),
            lax.all_gather(value, "ctx", axis=1, tiled=True),
        ),
        jnp.int32(0),
    )
    query_grad = folded[0]
    key_grad, value_grad = (
        lax.psum_scatter(
            folded[1].astype(jnp.bfloat16), "ctx", scatter_dimension=1, tiled=True
        ).astype(jnp.float32),
        lax.psum_scatter(
            folded[2].astype(jnp.bfloat16), "ctx", scatter_dimension=1, tiled=True
        ).astype(jnp.float32),
    )
    return (
        query_grad.reshape(seqs, rows, width).astype(jnp.bfloat16),
        key_grad.astype(jnp.bfloat16),
        value_grad.astype(jnp.bfloat16),
    )


def per_device(
    inputs,
    segment_ids,
    adapter_ids,
    w_query,
    w_key,
    w_value,
    w_out,
    w_gate,
    w_up,
    w_down,
    gain_attn,
    gain_ffn,
    attn_enter,
    attn_leave,
    out_enter,
    out_leave,
    mlp_enter,
    mlp_leave,
    last_enter,
    last_leave,
    out_grad,
):
    micro_count, seqs, rows, width = inputs.shape
    my_start = lax.axis_index("ctx") * rows
    adapter_count = attn_enter.shape[1]
    sum_attn_enter = jnp.zeros(attn_enter.shape, jnp.float32)
    sum_attn_leave = jnp.zeros(attn_leave.shape, jnp.float32)
    sum_out_enter = jnp.zeros(out_enter.shape, jnp.float32)
    sum_out_leave = jnp.zeros(out_leave.shape, jnp.float32)
    sum_mlp_enter = jnp.zeros(mlp_enter.shape, jnp.float32)
    sum_mlp_leave = jnp.zeros(mlp_leave.shape, jnp.float32)
    sum_last_enter = jnp.zeros(last_enter.shape, jnp.float32)
    sum_last_leave = jnp.zeros(last_leave.shape, jnp.float32)
    outputs = []
    gradients = []
    for micro in range(micro_count):
        frozen = (
            lax.all_gather(w_query, ("dp", "ctx"), axis=0, tiled=True),
            lax.all_gather(w_key, ("dp", "ctx"), axis=0, tiled=True),
            lax.all_gather(w_value, ("dp", "ctx"), axis=0, tiled=True),
            lax.all_gather(w_out, ("dp", "ctx"), axis=0, tiled=True),
            lax.all_gather(w_gate, ("dp", "ctx"), axis=0, tiled=True),
            lax.all_gather(w_up, ("dp", "ctx"), axis=0, tiled=True),
            lax.all_gather(w_down, ("dp", "ctx"), axis=0, tiled=True),
            lax.all_gather(gain_attn, ("dp", "ctx"), axis=0, tiled=True),
            lax.all_gather(gain_ffn, ("dp", "ctx"), axis=0, tiled=True),
        )
        query_w, key_w, value_w, out_w, gate_w, up_w, down_w, gain_one, gain_two = frozen
        chosen = adapter_ids[micro]
        attn_in = jnp.take(attn_enter, chosen, axis=1)
        attn_out = jnp.take(attn_leave, chosen, axis=1)
        out_in = jnp.take(out_enter, chosen, axis=0)
        out_out = jnp.take(out_leave, chosen, axis=0)
        mlp_in = jnp.take(mlp_enter, chosen, axis=1)
        mlp_out = jnp.take(mlp_leave, chosen, axis=1)
        last_in = jnp.take(last_enter, chosen, axis=0)
        last_out = jnp.take(last_leave, chosen, axis=0)
        seg_rows = segment_ids[micro]
        start_rows = inputs[micro].astype(jnp.float32)
        normed_f, inverse_one = rms_norm(start_rows, gain_one.astype(jnp.float32))
        normed = normed_f.astype(jnp.bfloat16)
        query_f, query_inner = project(normed, query_w, attn_in[0], attn_out[0])
        key_f, key_inner = project(normed, key_w, attn_in[1], attn_out[1])
        value_f, value_inner = project(normed, value_w, attn_in[2], attn_out[2])
        query = query_f.astype(jnp.bfloat16)
        key = key_f.astype(jnp.bfloat16)
        value = value_f.astype(jnp.bfloat16)
        mixed_f, log_total = attend(query, key, value, seg_rows, my_start)
        mixed = mixed_f.reshape(seqs, rows, width).astype(jnp.bfloat16)
        branch, out_inner = project(mixed, out_w, out_in, out_out)
        middle = start_rows + branch
        normed_two_f, inverse_two = rms_norm(middle, gain_two.astype(jnp.float32))
        normed_two = normed_two_f.astype(jnp.bfloat16)
        gate, gate_inner = project(normed_two, gate_w, mlp_in[0], mlp_out[0])
        upper, up_inner = project(normed_two, up_w, mlp_in[1], mlp_out[1])
        sigma = jax.nn.sigmoid(gate)
        hidden = (gate * sigma * upper).astype(jnp.bfloat16)
        closing, last_inner = project(hidden, down_w, last_in, last_out)
        outputs.append((middle + closing).astype(jnp.bfloat16))
        frozen = (
            lax.all_gather(w_query, ("dp", "ctx"), axis=0, tiled=True),
            lax.all_gather(w_key, ("dp", "ctx"), axis=0, tiled=True),
            lax.all_gather(w_value, ("dp", "ctx"), axis=0, tiled=True),
            lax.all_gather(w_out, ("dp", "ctx"), axis=0, tiled=True),
            lax.all_gather(w_gate, ("dp", "ctx"), axis=0, tiled=True),
            lax.all_gather(w_up, ("dp", "ctx"), axis=0, tiled=True),
            lax.all_gather(w_down, ("dp", "ctx"), axis=0, tiled=True),
            lax.all_gather(gain_attn, ("dp", "ctx"), axis=0, tiled=True),
            lax.all_gather(gain_ffn, ("dp", "ctx"), axis=0, tiled=True),
        )
        query_w, key_w, value_w, out_w, gate_w, up_w, down_w, gain_one, gain_two = frozen
        grad_rows = out_grad[micro].astype(jnp.float32)
        hidden_grad, last_in_grad, last_out_grad = project_back(
            hidden, last_inner, down_w, last_in, last_out, out_grad[micro]
        )
        gate_grad = (hidden_grad * upper * sigma * (1.0 + gate * (1.0 - sigma))).astype(
            jnp.bfloat16
        )
        up_grad = (hidden_grad * gate * sigma).astype(jnp.bfloat16)
        from_gate, gate_in_grad, gate_out_grad = project_back(
            normed_two, gate_inner, gate_w, mlp_in[0], mlp_out[0], gate_grad
        )
        from_up, up_in_grad, up_out_grad = project_back(
            normed_two, up_inner, up_w, mlp_in[1], mlp_out[1], up_grad
        )
        middle_grad = grad_rows + norm_back(
            middle, inverse_two, gain_two.astype(jnp.float32), from_gate + from_up
        )
        mixed_grad_f, out_in_grad, out_out_grad = project_back(
            mixed, out_inner, out_w, out_in, out_out, middle_grad.astype(jnp.bfloat16)
        )
        mixed_grad = mixed_grad_f.astype(jnp.bfloat16)
        query_grad, key_grad, value_grad = attend_back(
            query, key, value, mixed_grad, mixed_f, log_total, seg_rows, my_start
        )
        from_query, query_in_grad, query_out_grad = project_back(
            normed, query_inner, query_w, attn_in[0], attn_out[0], query_grad
        )
        from_key, key_in_grad, key_out_grad = project_back(
            normed, key_inner, key_w, attn_in[1], attn_out[1], key_grad
        )
        from_value, value_in_grad, value_out_grad = project_back(
            normed, value_inner, value_w, attn_in[2], attn_out[2], value_grad
        )
        gradients.append(
            middle_grad
            + norm_back(
                start_rows,
                inverse_one,
                gain_one.astype(jnp.float32),
                from_query + from_key + from_value,
            )
        )
        per_seq = (
            jnp.stack([query_in_grad, key_in_grad, value_in_grad]),
            jnp.stack([query_out_grad, key_out_grad, value_out_grad]),
            out_in_grad,
            out_out_grad,
            jnp.stack([gate_in_grad, up_in_grad]),
            jnp.stack([gate_out_grad, up_out_grad]),
            last_in_grad,
            last_out_grad,
        )
        onehot = (chosen[:, None] == jnp.arange(adapter_count, dtype=jnp.int32)[None, :]).astype(
            jnp.float32
        )
        sum_attn_enter = sum_attn_enter + jnp.einsum("sa,isrd->iard", onehot, per_seq[0])
        sum_attn_leave = sum_attn_leave + jnp.einsum("sa,isrd->iard", onehot, per_seq[1])
        sum_out_enter = sum_out_enter + jnp.einsum("sa,srd->ard", onehot, per_seq[2])
        sum_out_leave = sum_out_leave + jnp.einsum("sa,srd->ard", onehot, per_seq[3])
        sum_mlp_enter = sum_mlp_enter + jnp.einsum("sa,isrd->iard", onehot, per_seq[4])
        sum_mlp_leave = sum_mlp_leave + jnp.einsum("sa,isrf->iarf", onehot, per_seq[5])
        sum_last_enter = sum_last_enter + jnp.einsum("sa,srf->arf", onehot, per_seq[6])
        sum_last_leave = sum_last_leave + jnp.einsum("sa,srd->ard", onehot, per_seq[7])
    totals = (
        sum_attn_enter,
        sum_attn_leave,
        sum_out_enter,
        sum_out_leave,
        sum_mlp_enter,
        sum_mlp_leave,
        sum_last_enter,
        sum_last_leave,
    )
    summed = lax.psum(
        (totals[0], totals[1], totals[2], totals[3], totals[4], totals[5], totals[6], totals[7]),
        ("dp", "ctx"),
    )
    return (
        jnp.stack(outputs),
        jnp.stack(gradients),
        summed[0],
        summed[1],
        summed[2],
        summed[3],
        summed[4],
        summed[5],
        summed[6],
        summed[7],
    )


MESH = pl.DeviceIdType.MESH
BF = jnp.bfloat16
F32 = jnp.float32
SAME = (1, 4, 5)
PEERS = ((0, 1), (0, 4), (0, 5), (1, 0), (1, 1), (1, 4), (1, 5))
ACROSS = ((0, 2), (0, 8), (0, 10))
GREET = PEERS + ACROSS + ((1, 2), (1, 10))
GW = 2944


def dot(left, right):
    return lax.dot_general(left, right, (((1,), (0,)), ((), ())), preferred_element_type=F32)


def dot_t(left, right):
    return lax.dot_general(left, right, (((1,), (1,)), ((), ())), preferred_element_type=F32)


class Spot:
    def __init__(self, p, x, y, zl, zh):
        self.p, self.x, self.y, self.zl, self.zh = p, x, y, zl, zh

    def flip(self, a, b):
        return Spot(
            1 - self.p if a else self.p,
            1 - self.x if b & 1 else self.x,
            1 - self.y if b & 2 else self.y,
            1 - self.zl if b & 4 else self.zl,
            1 - self.zh if b & 8 else self.zh,
        )

    def device(self):
        return (self.p, self.x + 2 * self.y + 4 * self.zl + 8 * self.zh)

    def member(self):
        return self.p * 4 + self.zl * 2 + self.x

    def group(self):
        return self.zh * 2 + self.y


def here():
    p, c = lax.axis_index("dp"), lax.axis_index("ctx")
    return Spot(p, lax.rem(c, 2), lax.rem(lax.div(c, 2), 2), lax.rem(lax.div(c, 4), 2), lax.div(c, 8))


def part(index, size):
    return pl.ds(pl.multiple_of(index * size, size), size)


def remote(src, dst, ssem, rsem, spot):
    return pltpu.make_async_remote_copy(
        src_ref=src, dst_ref=dst, send_sem=ssem, recv_sem=rsem, device_id=spot.device(), device_id_type=MESH
    )


def pick(raw, mask):
    total = raw[0].astype(F32) * mask(0)
    for a in range(1, raw.shape[0]):
        total = total + raw[a].astype(F32) * mask(a)
    return total


def layer_kernel(names, *refs):
    R = types.SimpleNamespace(**dict(zip(names, refs, strict=True)))
    me = here()
    p, x, y, zl, zh = me.p, me.x, me.y, me.zl, me.zh
    j = me.member()
    own = part(j, 128)
    partner = me.flip(1, 0)
    late = []

    def send(src, dst, ssem, rsem, spot):
        copy = remote(src, dst, ssem, rsem, spot)
        copy.start()
        late.append(copy)

    def arrived(ref, ssem, rsem, spot):
        remote(ref, ref, ssem, rsem, spot).wait_recv()

    barrier = pltpu.get_barrier_semaphore()
    for a, b in GREET:
        pl.semaphore_signal(barrier, inc=1, device_id=me.flip(a, b).device(), device_id_type=MESH)
    pl.semaphore_wait(barrier, len(GREET))

    def reshard(src, dst, ssem, rsem):
        rows = pl.ds(pl.multiple_of((y * 4 + zl * 2 + x) * 128 + zh * 64, 64), 64)

        @pl.when(p == y)
        def _():
            pltpu.make_async_copy(src.at[zh], dst.at[rows], rsem.at[0]).start()
            remote(src.at[1 - zh], dst.at[rows], ssem.at[1], rsem.at[1], me.flip(0, 8)).start()

        @pl.when(p != y)
        def _():
            remote(src.at[zh], dst.at[rows], ssem.at[0], rsem.at[0], me.flip(1, 2)).start()
            remote(src.at[1 - zh], dst.at[rows], ssem.at[1], rsem.at[1], me.flip(1, 10)).start()

    def reshard_wait(dst, rsem):
        for k, t in enumerate((zh, 1 - zh)):
            rows = pl.ds(pl.multiple_of(j * 128 + t * 64, 64), 64)
            pltpu.make_async_copy(dst.at[rows], dst.at[rows], rsem.at[k]).wait()

    def reshard_sent(src, ssem):
        @pl.when(p != y)
        def _():
            remote(src.at[zh], src.at[zh], ssem.at[0], ssem.at[0], me.flip(1, 2)).wait_send()

        remote(src.at[zh], src.at[zh], ssem.at[1], ssem.at[1], me.flip(0, 8)).wait_send()

    def spread(view, ssem, rsem):
        mine = view(me)
        for k, b in enumerate(SAME):
            send(mine, mine, ssem.at[k], rsem.at[k], me.flip(0, b))
        send(mine, mine, ssem.at[3], rsem.at[3], partner)

    def spread_on(view, ssem, rsem):
        for k, b in enumerate(SAME):
            got = view(me.flip(0, b))
            arrived(got, ssem.at[k], rsem.at[k], me.flip(0, b))
            send(got, got, ssem.at[4 + k], rsem.at[4 + k], partner)

    def spread_end(view, ssem, rsem):
        arrived(view(partner), ssem.at[3], rsem.at[3], partner)
        for k, b in enumerate(SAME):
            arrived(view(me.flip(1, b)), ssem.at[4 + k], rsem.at[4 + k], partner)

    def across(views, ssem, rsem):
        for k, view in enumerate(views(me)):
            send(view, view, ssem.at[0, k], rsem.at[0, k], me.flip(0, 8))
            send(view, view, ssem.at[1, k], rsem.at[1, k], me.flip(0, 2))

    def across_on(views, ssem, rsem):
        for k, view in enumerate(views(me.flip(0, 8))):
            arrived(view, ssem.at[0, k], rsem.at[0, k], me.flip(0, 8))
            send(view, view, ssem.at[2, k], rsem.at[2, k], me.flip(0, 2))

    def across_end(views, ssem, rsem):
        for k, view in enumerate(views(me.flip(0, 2))):
            arrived(view, ssem.at[1, k], rsem.at[1, k], me.flip(0, 2))
        for k, view in enumerate(views(me.flip(0, 10))):
            arrived(view, ssem.at[2, k], rsem.at[2, k], me.flip(0, 2))

    def row_views(ref, columns):
        def views(spot):
            return [
                ref.at[pl.ds(pl.multiple_of(pp * 512 + spot.zh * 256 + zz * 128 + spot.y * 64, 64), 64), pl.ds(0, columns)]
                for pp in range(2)
                for zz in range(2)
            ]

        return views

    qkv_views, gu_views = row_views(R.qkvb, 384), row_views(R.gub, 1024)

    def down_views(spot):
        return [R.db.at[part(spot.group(), 128), pl.ds(0, 1024)]]

    def out_views(spot):
        k_row = (spot.p * 16 + spot.zh * 8 + spot.zl * 4 + spot.y * 2 + spot.x) * 32
        return [R.ob.at[pl.ds(pl.multiple_of(k_row, 32), 32), pl.ds(0, 1024)]]

    def gain_views(spot):
        return [R.gs.at[spot.group()]]

    my_row = pl.ds(pl.multiple_of((p * 16 + zh * 8 + zl * 4 + y * 2 + x) * 32, 32), 32)

    raws = (
        (R.ae, R.ae_h), (R.al, R.al_h.at[:, :, :, own]), (R.oe, R.oe_h), (R.ol, R.ol_h), (R.me, R.me_h), (R.ll, R.ll_h),
    )
    locals_ = []
    for k, (dst, src) in enumerate(raws):
        locals_.append(pltpu.make_async_copy(src, dst, R.la.at[k]))
    for q in range(4):
        fb = part(p * 16 + (q // 2) * 8 + zl * 4 + (q % 2) * 2 + x, 128)
        locals_.append(pltpu.make_async_copy(R.ml_h.at[:, :, :, fb], R.ml.at[:, :, :, pl.ds(q * 128, 128)], R.la.at[8 + q]))
        locals_.append(pltpu.make_async_copy(R.le_h.at[:, :, fb], R.le.at[:, :, pl.ds(q * 128, 128)], R.la.at[12 + q]))

    reshard(R.x_h, R.xf, R.xs, R.xr)

    gain_mine = R.gs.at[me.group(), j]
    gain_local = pltpu.make_async_copy(R.gain_h, gain_mine, R.g1r.at[7])
    gain_local.start()
    for k, (a, b) in enumerate(PEERS):
        send(R.gain_h, gain_mine, R.g1s.at[k], R.g1r.at[k], me.flip(a, b))

    def columns_to(spot, k, start):
        t = spot.member()
        for i, src in enumerate((R.wq_h, R.wk_h, R.wv_h)):
            start(src.at[:, part(t, 128)], R.qkvb.at[my_row, pl.ds(i * 128, 128)], R.w1qs.at[k, i], R.w1qr.at[k, i])

    def mlp_columns_to(spot, k, start):
        for i, src in enumerate((R.wg_h, R.wu_h)):
            for q in range(4):
                fb = part(spot.p * 16 + (q // 2) * 8 + spot.zl * 4 + (q % 2) * 2 + spot.x, 128)
                at = (k, i * 4 + q)
                start(src.at[:, fb], R.gub.at[my_row, pl.ds(i * 512 + q * 128, 128)], R.w1ms.at[*at], R.w1mr.at[*at])

    def start_remote(spot):
        return lambda src, dst, ssem, rsem: send(src, dst, ssem, rsem, spot)

    def start_local(src, dst, ssem, rsem):
        pltpu.make_async_copy(src, dst, rsem).start()

    for k, (a, b) in enumerate(PEERS):
        columns_to(me.flip(a, b), k, start_remote(me.flip(a, b)))
    columns_to(me, 7, start_local)

    meta_local = pltpu.make_async_copy(R.meta_h, R.meta.at[p], R.mr.at[1])
    meta_local.start()
    send(R.meta_h, R.meta.at[p], R.ms.at[0], R.mr.at[0], partner)
    for copy in locals_:
        copy.start()

    out_mine = out_views(me)[0]
    out_local = pltpu.make_async_copy(R.wo_h, out_mine, R.wor.at[3, 0])
    out_local.start()
    send(R.wo_h, out_mine, R.wos.at[0, 0], R.wor.at[0, 0], me.flip(0, 8))
    send(R.wo_h, out_mine, R.wos.at[1, 0], R.wor.at[1, 0], me.flip(0, 2))

    def x_view(spot):
        return R.xf.at[part(spot.member(), 128)]

    def og_view(spot):
        return R.ogf.at[part(spot.member(), 128)]

    def n2_view(spot):
        return R.n2f.at[part(spot.member(), 128)]

    reshard_wait(R.xf, R.xr)
    spread(x_view, R.axs, R.axr)

    for k, (a, b) in enumerate(PEERS):
        mlp_columns_to(me.flip(a, b), k, start_remote(me.flip(a, b)))
    mlp_columns_to(me, 7, start_local)

    for k, (a, b) in enumerate(PEERS):
        spot = me.flip(a, b)
        arrived(R.gs.at[me.group(), spot.member()], R.g1s.at[k], R.g1r.at[k], spot)
    gain_local.wait()
    across(gain_views, R.g2s, R.g2r)

    def rows_of(spot):
        return pl.ds(pl.multiple_of((spot.p * 16 + spot.zh * 8 + spot.zl * 4 + spot.y * 2 + spot.x) * 32, 32), 32)

    def first_end(target, rsem, pieces):
        for k, (a, b) in enumerate(PEERS + ((0, 0),)):
            rows = rows_of(me.flip(a, b))
            for i in range(pieces):
                ref = target.at[rows, pl.ds(i * 128, 128)]
                pltpu.make_async_copy(ref, ref, rsem.at[k, i]).wait()

    first_end(R.qkvb, R.w1qr, 3)
    across(qkv_views, R.w2qs, R.w2qr)
    spread_on(x_view, R.axs, R.axr)
    reshard(R.og_h, R.ogf, R.os, R.ors)
    first_end(R.gub, R.w1mr, 8)
    across(gu_views, R.w2ms, R.w2mr)
    down_mine = down_views(me)[0]
    down_local = pltpu.make_async_copy(R.wd_h, down_mine, R.wdr.at[3, 0])
    down_local.start()
    send(R.wd_h, down_mine, R.wds.at[0, 0], R.wdr.at[0, 0], me.flip(0, 8))
    send(R.wd_h, down_mine, R.wds.at[1, 0], R.wdr.at[1, 0], me.flip(0, 2))

    across_on(gain_views, R.g2s, R.g2r)
    across_on(qkv_views, R.w2qs, R.w2qr)

    pltpu.make_async_copy(R.meta_h, R.meta.at[p], R.mr.at[1]).wait()
    arrived(R.meta.at[1 - p], R.ms.at[0], R.mr.at[0], partner)
    for copy in locals_:
        copy.wait()
    ids = R.meta[y, pl.ds(2 + zh, 1), :]

    def mask(width):
        return lambda a: (ids[:, 0:width] == a).astype(F32)

    def enter_columns(items):
        rows = [pick(item, mask(item.shape[-1])) for item in items]
        width = rows[0].shape[-1]
        rows.append(jnp.zeros((128 - 16 * len(rows), width), F32))
        return jnp.transpose(jnp.concatenate(rows, axis=0)).astype(BF)

    def leave_rows(ref, first, items):
        ref[pl.ds(first, 128), :] = jnp.zeros((128, ref.shape[1]), BF)
        column = 0
        for i, item in enumerate(items):
            width = item.shape[-1]
            ref[pl.ds(first + 16 * i, 16), pl.ds(column, width)] = (SCALE * pick(item, mask(width))).astype(BF)
            column += width

    R.qkvb[pl.ds(0, 1024), pl.ds(384, 128)] = enter_columns([R.ae.at[i] for i in range(3)])
    leave_rows(R.qkvb, 1024, [R.al.at[i] for i in range(3)])
    R.ob[pl.ds(0, 1024), pl.ds(1024, 128)] = enter_columns([R.oe])
    leave_rows(R.ob, 1024, [R.ol])
    R.gub[pl.ds(0, 1024), pl.ds(1024, 128)] = enter_columns([R.me.at[i] for i in range(2)])
    leave_rows(R.gub, 1024, [R.ml.at[i] for i in range(2)])
    R.db[pl.ds(0, 512), pl.ds(1024, 128)] = enter_columns([R.le])
    leave_rows(R.db, 512, [R.ll])

    seg_row = R.meta[y, pl.ds(zh, 1), :]
    R.segc[...] = jnp.transpose(jnp.broadcast_to(seg_row.astype(F32), (128, 1024)))

    across_end(gain_views, R.g2s, R.g2r)
    gains = jnp.sum(jnp.sum(R.gs[...], axis=0), axis=0)
    gain_one = jnp.concatenate([gains[i : i + 1] for i in range(8)], axis=1)
    gain_two = jnp.concatenate([gains[i : i + 1] for i in range(8, 16)], axis=1)

    spread_end(x_view, R.axs, R.axr)
    reshard_wait(R.ogf, R.ors)
    spread(og_view, R.aos, R.aor)
    across_end(qkv_views, R.w2qs, R.w2qr)

    def qkv_tile(t, carry):
        rows = part(t, 256)
        held = R.xf[rows, :].astype(F32)
        inverse = lax.rsqrt(jnp.mean(held * held, axis=-1, keepdims=True) + EPS)
        normed = (held * inverse * gain_one).astype(BF)
        both = dot(normed, R.qkvb[0:1024, :])
        inner = both[:, 384:512]
        qkv = both[:, 0:384] + dot(inner.astype(BF), R.qkvb[1024:1152, 0:384])
        R.r1t[:, rows] = jnp.transpose(inner).astype(BF)
        R.qb[rows, :] = (qkv[:, 0:128].astype(BF).astype(F32) * 0.125).astype(BF)
        R.kb[rows, :] = qkv[:, 128:256].astype(BF)
        R.vb[rows, :] = qkv[:, 256:384].astype(BF)
        R.kt[:, rows] = jnp.transpose(qkv[:, 128:256]).astype(BF)
        R.vt[:, rows] = jnp.transpose(qkv[:, 256:384]).astype(BF)
        return carry

    lax.fori_loop(0, 4, qkv_tile, 0)

    out_local.wait()
    across_on(out_views, R.wos, R.wor)
    across_end(out_views, R.wos, R.wor)
    for q in range(4):
        fl = (0, 2 * (q % 2) + 8 * (q // 2))
        spread(lambda spot, fl=fl: out_views(spot.flip(*fl))[0], R.aws.at[q], R.awr.at[q])

    head_of = lax.broadcasted_iota(jnp.int32, (256, 128), 1) // HD

    def attend_tile(t, carry):
        rows = part(t, 256)
        queries = R.qb[rows, :]
        same = R.segc[:, 0:1] == R.meta[y, pl.ds(zh, 1), rows].astype(F32)
        mixed = []
        for h in range(2):
            mine = jnp.where(head_of == h, queries.astype(F32), 0.0).astype(BF)
            scores = jnp.where(same, dot_t(R.kb[...], mine), NEG)
            weights = jnp.exp(scores - jnp.max(scores, axis=0, keepdims=True))
            probs = (weights * (1.0 / jnp.sum(weights, axis=0, keepdims=True))).astype(BF)
            R.pr[2 * t + h] = probs
            mixed.append(dot(R.vt[h * HD : (h + 1) * HD, :], probs))
        mixed = jnp.concatenate(mixed, axis=0)
        R.att[t] = mixed
        R.ath[rows, :] = jnp.transpose(mixed).astype(BF)
        return carry

    lax.fori_loop(0, 4, attend_tile, 0)

    for k, (a, b) in enumerate(PEERS):
        spot = me.flip(a, b)
        send(R.ath.at[part(spot.member(), 128)], R.ato.at[:, own], R.a1s.at[k], R.a1r.at[k], spot)
    mine_local = pltpu.make_async_copy(R.ath.at[own], R.ato.at[:, own], R.a1r.at[7])
    mine_local.start()

    spread_on(og_view, R.aos, R.aor)
    for q in range(4):
        fl = (0, 2 * (q % 2) + 8 * (q // 2))
        spread_on(lambda spot, fl=fl: out_views(spot.flip(*fl))[0], R.aws.at[q], R.awr.at[q])
    across_on(gu_views, R.w2ms, R.w2mr)
    for q in range(4):
        fl = (0, 2 * (q % 2) + 8 * (q // 2))
        spread_end(lambda spot, fl=fl: out_views(spot.flip(*fl))[0], R.aws.at[q], R.awr.at[q])
    mine_local.wait()
    for k, (a, b) in enumerate(PEERS):
        spot = me.flip(a, b)
        arrived(R.ato.at[:, part(spot.member(), 128)], R.a1s.at[k], R.a1r.at[k], spot)

    start_rows = R.xf[own, :].astype(F32)
    both = dot(R.ato[...], R.ob[0:1024, :])
    out_inner = both[:, 1024:1152]
    middle = start_rows + both[:, 0:1024] + dot(out_inner.astype(BF), R.ob[1024:1152, 0:1024])
    R.mid[...] = middle
    inverse = lax.rsqrt(jnp.mean(middle * middle, axis=-1, keepdims=True) + EPS)
    R.n2f[own, :] = (middle * inverse * gain_two).astype(BF)
    R.rot[...] = jnp.transpose(out_inner).astype(BF)
    spread(n2_view, R.ans, R.anr)

    down_local.wait()
    across_on(down_views, R.wds, R.wdr)
    across_end(gu_views, R.w2ms, R.w2mr)
    across_end(down_views, R.wds, R.wdr)
    spread_end(og_view, R.aos, R.aor)
    spread_on(n2_view, R.ans, R.anr)
    spread_end(n2_view, R.ans, R.anr)

    R.cml[...] = jnp.zeros((128, 1024), F32)
    R.cle[...] = jnp.zeros((128, 512), F32)

    def mlp_tile(i, carry):
        rows = part(lax.rem((1 - p) * 2 + i, 4), 256)
        both = dot(R.n2f[rows, :], R.gub[0:1024, :])
        inner = both[:, 1024:1152]
        pair = both[:, 0:1024] + dot(inner.astype(BF), R.gub[1024:1152, 0:1024])
        gate, upper = pair[:, 0:512], pair[:, 512:1024]
        sigma = jax.nn.sigmoid(gate)
        hidden = (gate * sigma * upper).astype(BF)
        R.zd[rows, :] = dot(hidden, R.db[0:512, :]).astype(BF)
        back = dot_t(R.ogf[rows, :], R.db[:, 0:1024])
        inner_back = back[:, 512:640]
        hidden_grad = back[:, 0:512] + dot_t(inner_back.astype(BF), R.db[0:512, 1024:1152])
        gate_grad = (hidden_grad * upper * sigma * (1.0 + gate * (1.0 - sigma))).astype(BF)
        up_grad = (hidden_grad * gate * sigma).astype(BF)
        pair_grad = jnp.concatenate([gate_grad, up_grad], axis=1)
        R.zn[rows, :] = dot_t(pair_grad, R.gub[:, 0:1024]).astype(BF)
        R.cml[...] += dot(jnp.transpose(inner).astype(BF), pair_grad)
        R.cle[...] += dot(jnp.transpose(inner_back).astype(BF), hidden)
        return carry

    def pair_send(parts, k):
        send(parts.at[part(1 - p, 512)], R.rp.at[k], R.rps.at[k], R.rpr.at[k], partner)

    def chip_send(parts, k):
        arrived(R.rp.at[k], R.rps.at[k], R.rpr.at[k], partner)

        def add(i, carry):
            rows = part(i, 128)
            R.rc[k, rows, :] = (
                parts[part(p * 4 + i, 128), :].astype(F32) + R.rp[k, rows, :].astype(F32)
            ).astype(BF)
            return carry

        lax.fori_loop(0, 4, add, 0)
        for i, b in enumerate(SAME):
            spot = me.flip(0, b)
            send(R.rc.at[k, part(spot.zl * 2 + spot.x, 128)], R.rr.at[k, i], R.rrs.at[k, i], R.rrr.at[k, i], spot)

    def summed(parts, k):
        for i, b in enumerate(SAME):
            arrived(R.rr.at[k, i], R.rrs.at[k, i], R.rrr.at[k, i], me.flip(0, b))
        total = parts[own, :].astype(F32) + R.rp[k, part(zl * 2 + x, 128), :].astype(F32)
        for i in range(3):
            total = total + R.rr[k, i].astype(F32)
        return total

    lax.fori_loop(0, 2, mlp_tile, 0)
    pair_send(R.zn, 0)
    pair_send(R.zd, 1)
    lax.fori_loop(2, 4, mlp_tile, 0)
    chip_send(R.zn, 0)
    for i in range(2):
        R.gd[:, pl.ds(1408 + i * 512, 512)] = (SCALE * R.cml[i * 16 : (i + 1) * 16, i * 512 : (i + 1) * 512]).astype(BF)
    R.gd[:, pl.ds(2432, 512)] = R.cle[0:16, :].astype(BF)

    own_grad = R.ogf[own, :].astype(F32)
    total = summed(R.zn, 0)
    inner_back = total[:, 1024:1152]
    normed_grad = total[:, 0:1024] + dot_t(inner_back.astype(BF), R.gub[0:1024, 1024:1152])
    middle = R.mid[...]
    inverse = lax.rsqrt(jnp.mean(middle * middle, axis=-1, keepdims=True) + EPS)
    middle_grad = own_grad + norm_back(middle, inverse, gain_two, normed_grad)
    R.mg[...] = middle_grad
    rounded = middle_grad.astype(BF)
    both = dot_t(rounded, R.ob[:, 0:1024])
    out_back = both[:, 1024:1152]
    R.gao[...] = (both[:, 0:1024] + dot_t(out_back.astype(BF), R.ob[0:1024, 1024:1152])).astype(BF)
    for k, (a, b) in enumerate(PEERS):
        spot = me.flip(a, b)
        send(R.gao.at[:, part(spot.member(), 128)], R.gah.at[own], R.a2s.at[k], R.a2r.at[k], spot)
    mine_local = pltpu.make_async_copy(R.gao.at[:, own], R.gah.at[own], R.a2r.at[7])
    mine_local.start()
    chip_send(R.zd, 1)
    mlp_enter = dot(jnp.transpose(inner_back).astype(BF), R.n2f[own, :])
    out_enter = dot(jnp.transpose(out_back).astype(BF), R.ato[...])
    out_leave = SCALE * dot(R.rot[...], rounded)
    R.gp[4] = mlp_enter[0:16].astype(BF)
    R.gp[5] = mlp_enter[16:32].astype(BF)
    R.gp[3] = out_enter[0:16].astype(BF)
    R.gp[6] = out_leave[0:16].astype(BF)
    mine_local.wait()
    for k, (a, b) in enumerate(PEERS):
        spot = me.flip(a, b)
        arrived(R.gah.at[part(spot.member(), 128)], R.a2s.at[k], R.a2r.at[k], spot)

    R.gk[...] = jnp.zeros((1024, 128), F32)
    R.gv[...] = jnp.zeros((1024, 128), F32)

    def attend_back_tile(t, carry):
        rows = part(t, 256)
        queries, grads = R.qb[rows, :].astype(F32), R.gah[rows, :].astype(F32)
        delta_parts = jnp.transpose(grads) * R.att[t]
        query_grad = []
        for h in range(2):
            mine = jnp.where(head_of == h, queries, 0.0).astype(BF)
            grad = jnp.where(head_of == h, grads, 0.0).astype(BF)
            probs = R.pr[2 * t + h]
            delta = jnp.sum(delta_parts[h * HD : (h + 1) * HD], axis=0, keepdims=True)
            score_grad = (probs.astype(F32) * (dot_t(R.vb[...], grad) - delta)).astype(BF)
            R.gk[...] += dot(score_grad, mine)
            R.gv[...] += dot(probs, grad)
            query_grad.append(dot(R.kt[h * HD : (h + 1) * HD, :], score_grad))
        R.gq[rows, pl.ds(0, 128)] = (jnp.transpose(jnp.concatenate(query_grad, axis=0)) * 0.125).astype(BF)
        return carry

    lax.fori_loop(0, 4, attend_back_tile, 0)
    R.gq[:, pl.ds(128, 128)] = R.gk[...].astype(BF)
    R.gq[:, pl.ds(256, 128)] = R.gv[...].astype(BF)

    def qkv_back_tile(i, carry):
        rows = part(lax.rem((1 - p) * 2 + i, 4), 256)
        R.zq[rows, :] = dot_t(R.gq[rows, :], R.qkvb[:, 0:384]).astype(BF)
        return carry

    lax.fori_loop(0, 2, qkv_back_tile, 0)
    pair_send(R.zq, 2)
    lax.fori_loop(2, 4, qkv_back_tile, 0)
    chip_send(R.zq, 2)

    leave = SCALE * dot(R.r1t[...], R.gq[...])
    for i in range(3):
        R.gd[:, pl.ds(1024 + i * 128, 128)] = leave[i * 16 : (i + 1) * 16, i * 128 : (i + 1) * 128].astype(BF)
    total = summed(R.zd, 1)
    last_inner = total[:, 1024:1152]
    R.outv[...] = (R.mid[...] + total[:, 0:1024] + dot(last_inner.astype(BF), R.db[512:640, 0:1024])).astype(BF)
    R.gp[7] = (SCALE * dot(jnp.transpose(last_inner).astype(BF), R.ogf[own, :]))[0:16].astype(BF)

    def give_back(src, dst, ssem, rsem):
        spot_same, spot_other = part(zh, 64), part(1 - zh, 64)

        @pl.when(p == y)
        def _():
            pltpu.make_async_copy(src.at[spot_same], dst.at[zh], rsem.at[0]).start()
            remote(src.at[spot_other], dst.at[zh], ssem.at[1], rsem.at[1], me.flip(0, 8)).start()

        @pl.when(p != y)
        def _():
            remote(src.at[spot_same], dst.at[zh], ssem.at[0], rsem.at[0], me.flip(1, 2)).start()
            remote(src.at[spot_other], dst.at[zh], ssem.at[1], rsem.at[1], me.flip(1, 10)).start()

    def give_back_wait(src, dst, ssem, rsem):
        pltpu.make_async_copy(dst.at[zh], dst.at[zh], rsem.at[0]).wait()
        pltpu.make_async_copy(dst.at[1 - zh], dst.at[1 - zh], rsem.at[1]).wait()

        @pl.when(p != y)
        def _():
            remote(src.at[part(zh, 64)], src.at[part(zh, 64)], ssem.at[0], rsem.at[0], me.flip(1, 2)).wait_send()

        remote(src.at[part(zh, 64)], src.at[part(zh, 64)], ssem.at[1], rsem.at[1], me.flip(0, 8)).wait_send()

    give_back(R.outv, R.out_o, R.bos, R.bor)

    total = summed(R.zq, 2)
    inner_back = total[:, 1024:1152]
    normed_grad = total[:, 0:1024] + dot_t(inner_back.astype(BF), R.qkvb[0:1024, 384:512])
    start_rows = R.xf[own, :].astype(F32)
    inverse = lax.rsqrt(jnp.mean(start_rows * start_rows, axis=-1, keepdims=True) + EPS)
    normed = (start_rows * inverse * gain_one).astype(BF)
    R.igv[...] = (R.mg[...] + norm_back(start_rows, inverse, gain_one, normed_grad)).astype(BF)
    give_back(R.igv, R.ig_o, R.bis, R.bir)
    attn_enter = dot(jnp.transpose(inner_back).astype(BF), normed)
    for i in range(3):
        R.gp[i] = attn_enter[i * 16 : (i + 1) * 16].astype(BF)

    for k, (a, b) in enumerate(PEERS):
        spot = me.flip(a, b)
        send(R.gp.at[spot.member()], R.gr.at[k], R.gps.at[k], R.gpr.at[k], spot)
    block = R.gp[j].astype(F32)
    for k, (a, b) in enumerate(PEERS):
        arrived(R.gr.at[k], R.gps.at[k], R.gpr.at[k], me.flip(a, b))
        block = block + R.gr[k].astype(F32)
    R.gd[:, pl.ds(0, 1024)] = block.astype(BF)

    def share_view(spot):
        return R.gall_o.at[spot.group(), spot.member()]

    share_local = pltpu.make_async_copy(R.gd, share_view(me), R.gar.at[3, 0])
    share_local.start()
    for k, (a, b) in enumerate(ACROSS):
        send(R.gd, share_view(me), R.gas.at[k, 0], R.gar.at[k, 0], me.flip(a, b))
    share_local.wait()
    spread(share_view, R.gbs.at[3], R.gbr.at[3])
    for k, (a, b) in enumerate(ACROSS):
        arrived(share_view(me.flip(a, b)), R.gas.at[k, 0], R.gar.at[k, 0], me.flip(a, b))
        spread(lambda spot, b=b: share_view(spot.flip(0, b)), R.gbs.at[k], R.gbr.at[k])
    flips = {0: 2, 1: 8, 2: 10, 3: 0}
    for k in (3, 0, 1, 2):
        spread_on(lambda spot, k=k: share_view(spot.flip(0, flips[k])), R.gbs.at[k], R.gbr.at[k])
    for k in (3, 0, 1, 2):
        spread_end(lambda spot, k=k: share_view(spot.flip(0, flips[k])), R.gbs.at[k], R.gbr.at[k])

    meta_out = pltpu.make_async_copy(R.meta, R.meta_o, R.mr.at[2])
    meta_out.start()
    give_back_wait(R.outv, R.out_o, R.bos, R.bor)
    give_back_wait(R.igv, R.ig_o, R.bis, R.bir)
    reshard_sent(R.x_h, R.xs)
    reshard_sent(R.og_h, R.os)
    for copy in late:
        copy.wait_send()
    meta_out.wait()


def layer_call(**inputs):
    V, S = pltpu.VMEM, pltpu.SemaphoreType.DMA
    outputs = dict(
        out_o=((2, 64, 1024), BF),
        ig_o=((2, 64, 1024), BF),
        gall_o=((4, 8, 16, GW), BF),
        meta_o=((2, 8, 1024), jnp.int32),
    )
    scratch = dict(
        xf=V((1024, 1024), BF), ogf=V((1024, 1024), BF), n2f=V((1024, 1024), BF),
        qkvb=V((1152, 512), BF), ob=V((1152, 1152), BF), gub=V((1152, 1152), BF), db=V((640, 1152), BF),
        ae=V((3, 8, 16, 1024), BF), al=V((3, 8, 16, 128), BF), oe=V((8, 16, 1024), BF), ol=V((8, 16, 1024), BF),
        me=V((2, 8, 16, 1024), BF), ml=V((2, 8, 16, 512), BF), le=V((8, 16, 512), BF), ll=V((8, 16, 1024), BF),
        meta=V((2, 8, 1024), jnp.int32), gs=V((4, 8, 16, 128), F32), segc=V((1024, 128), F32),
        qb=V((1024, 128), BF), kb=V((1024, 128), BF), vb=V((1024, 128), BF), kt=V((128, 1024), BF),
        vt=V((128, 1024), BF), r1t=V((128, 1024), BF), pr=V((8, 1024, 256), BF), att=V((4, 128, 256), F32),
        ath=V((1024, 128), BF), ato=V((128, 1024), BF), mid=V((128, 1024), F32), mg=V((128, 1024), F32),
        rot=V((128, 128), BF), zn=V((1024, 1152), BF), zd=V((1024, 1152), BF), zq=V((1024, 1152), BF),
        rp=V((3, 512, 1152), BF), rc=V((3, 512, 1152), BF), rr=V((3, 3, 128, 1152), BF),
        cml=V((128, 1024), F32), cle=V((128, 512), F32), gao=V((128, 1024), BF), gah=V((1024, 128), BF),
        gk=V((1024, 128), F32), gv=V((1024, 128), F32), gq=V((1024, 384), BF), outv=V((128, 1024), BF),
        igv=V((128, 1024), BF), gp=V((8, 16, 1024), BF), gr=V((7, 16, 1024), BF), gd=V((16, GW), BF),
        la=S((16,)), xs=S((2,)), xr=S((2,)), os=S((2,)), ors=S((2,)), g1s=S((7,)), g1r=S((8,)),
        g2s=S((3, 1)), g2r=S((3, 1)), w1qs=S((8, 3)), w1qr=S((8, 3)), w1ms=S((8, 8)), w1mr=S((8, 8)),
        w2qs=S((3, 4)), w2qr=S((3, 4)), w2ms=S((3, 4)), w2mr=S((3, 4)), wos=S((3, 1)), wor=S((4, 1)),
        wds=S((3, 1)), wdr=S((4, 1)), ms=S((1,)), mr=S((3,)), axs=S((7,)), axr=S((7,)),
        aos=S((7,)), aor=S((7,)), ans=S((7,)), anr=S((7,)), aws=S((4, 7)), awr=S((4, 7)),
        a1s=S((7,)), a1r=S((8,)), a2s=S((7,)), a2r=S((8,)), rps=S((3,)), rpr=S((3,)),
        rrs=S((3, 3)), rrr=S((3, 3)), bos=S((2,)), bor=S((2,)), bis=S((2,)), bir=S((2,)),
        gps=S((7,)), gpr=S((7,)), gas=S((3, 1)), gar=S((4, 1)), gbs=S((4, 7)), gbr=S((4, 7)),
    )
    names = list(inputs) + list(outputs) + list(scratch)
    return pl.pallas_call(
        functools.partial(layer_kernel, names),
        out_shape=[jax.ShapeDtypeStruct(shape, dtype) for shape, dtype in outputs.values()],
        in_specs=[pl.BlockSpec(memory_space=pl.ANY)] * len(inputs),
        out_specs=[pl.BlockSpec(memory_space=pl.ANY)] * len(outputs),
        scratch_shapes=list(scratch.values()),
        compiler_params=pltpu.CompilerParams(collective_id=0, has_side_effects=True, vmem_limit_bytes=63 * 2**20),
        name="layer",
    )(*inputs.values())


def place_kernel(ids, gall, out_i, ig_i, out_o, ig_o, ae_o, al_o, oe_o, ol_o, me_o, ml_o, le_o, ll_o):
    a = pl.program_id(0)
    outs = (ae_o, al_o, oe_o, ol_o, me_o, ml_o, le_o, ll_o)

    @pl.when(a == 0)
    def _():
        out_o[...] = out_i[...]
        ig_o[...] = ig_i[...].astype(F32)

    for ref in outs:
        ref[...] = jnp.zeros(ref.shape, F32)
    for group in range(4):
        ident = ids[group % 2, 2 + group // 2, 0]

        @pl.when(ident == a)
        def _(group=group):
            def block(member, first, width):
                return gall[group, member, :, first : first + width].astype(F32)

            for i in range(3):
                ae_o[i, 0] += block(i, 0, 1024)
                for m in range(8):
                    al_o[i, 0, :, m * 128 : (m + 1) * 128] += block(m, 1024 + i * 128, 128)
            oe_o[0] += block(3, 0, 1024)
            ol_o[0] += block(6, 0, 1024)
            ll_o[0] += block(7, 0, 1024)
            for i in range(2):
                me_o[i, 0] += block(4 + i, 0, 1024)
            for m in range(8):
                for q in range(4):
                    fb = ((m // 4) * 16 + (q // 2) * 8 + (m // 2 % 2) * 4 + (q % 2) * 2 + m % 2) * 128
                    le_o[0, :, fb : fb + 128] += block(m, 2432 + q * 128, 128)
                    for i in range(2):
                        ml_o[i, 0, :, fb : fb + 128] += block(m, 1408 + i * 512 + q * 128, 128)


def place_call(meta, gall, out, ig):
    def whole(shape):
        return pl.BlockSpec(shape, lambda a, ids: (0,) * len(shape))

    def four(n, width):
        return pl.BlockSpec((n, 1, 16, width), lambda a, ids: (0, a, 0, 0))

    def three(width):
        return pl.BlockSpec((1, 16, width), lambda a, ids: (a, 0, 0))

    shapes = ((3, 8, 16, 1024), (3, 8, 16, 1024), (8, 16, 1024), (8, 16, 1024), (2, 8, 16, 1024), (2, 8, 16, 4096), (8, 16, 4096), (8, 16, 1024))
    return pl.pallas_call(
        place_kernel,
        out_shape=[jax.ShapeDtypeStruct((2, 64, 1024), BF), jax.ShapeDtypeStruct((2, 64, 1024), F32)]
        + [jax.ShapeDtypeStruct(shape, F32) for shape in shapes],
        grid_spec=pltpu.PrefetchScalarGridSpec(
            num_scalar_prefetch=1,
            grid=(8,),
            in_specs=[whole((4, 8, 16, GW)), whole((2, 64, 1024)), whole((2, 64, 1024))],
            out_specs=[whole((2, 64, 1024)), whole((2, 64, 1024)), four(3, 1024), four(3, 1024), three(1024), three(1024),
                       four(2, 1024), four(2, 4096), three(4096), three(1024)],
        ),
        compiler_params=pltpu.CompilerParams(vmem_limit_bytes=32 * 2**20),
        name="place",
    )(meta, gall, out, ig)


def grouped(
    inputs, segment_ids, adapter_ids, w_query, w_key, w_value, w_out, w_gate, w_up, w_down, gain_attn, gain_ffn,
    attn_enter, attn_leave, out_enter, out_leave, mlp_enter, mlp_leave, last_enter, last_leave, out_grad,
):
    flat = lax.axis_index("dp") * 16 + lax.axis_index("ctx")
    seg = segment_ids[:, 0].reshape(2, 2, 2, 2, 2, 64)
    seg = jnp.transpose(seg, (0, 3, 2, 4, 1, 5)).reshape(2, 1024)
    ids = jnp.broadcast_to(adapter_ids, (2, 1024))
    meta = jnp.concatenate([seg, ids, jnp.zeros((4, 1024), jnp.int32)], axis=0)
    at = lax.broadcasted_iota(jnp.int32, (32, 32), 0) == flat
    gains = jnp.concatenate(
        [jnp.where(at, gain.astype(F32)[None, :], 0.0).reshape(8, 128) for gain in (gain_attn, gain_ffn)], axis=0
    )
    out, ig, gall, meta_all = layer_call(
        x_h=inputs[:, 0], og_h=out_grad[:, 0], meta_h=meta, gain_h=gains, wq_h=w_query, wk_h=w_key, wv_h=w_value, wo_h=w_out,
        wg_h=w_gate, wu_h=w_up, wd_h=w_down, ae_h=attn_enter, al_h=attn_leave, oe_h=out_enter, ol_h=out_leave,
        me_h=mlp_enter, ml_h=mlp_leave, le_h=last_enter, ll_h=last_leave,
    )
    out, ig, *grads = place_call(meta_all, gall, out, ig)
    return (out[:, None], ig[:, None], *grads)


def solution(mesh):
    def chosen(*args):
        sizes = (mesh.shape["dp"], mesh.shape["ctx"], *args[0].shape)
        return (grouped if sizes == (2, 16, 2, 1, 64, 1024) else per_device)(*args)

    return jax.shard_map(
        chosen,
        mesh=mesh,
        in_specs=(
            P(None, "dp", "ctx", None),
            P(None, "dp", None),
            P(None, "dp"),
            P(("dp", "ctx"), None),
            P(("dp", "ctx"), None),
            P(("dp", "ctx"), None),
            P(("dp", "ctx"), None),
            P(("dp", "ctx"), None),
            P(("dp", "ctx"), None),
            P(("dp", "ctx"), None),
            P(("dp", "ctx")),
            P(("dp", "ctx")),
            P(),
            P(),
            P(),
            P(),
            P(),
            P(),
            P(),
            P(),
            P(None, "dp", "ctx", None),
        ),
        out_specs=(
            P(None, "dp", "ctx", None),
            P(None, "dp", "ctx", None),
            P(),
            P(),
            P(),
            P(),
            P(),
            P(),
            P(),
            P(),
        ),
        check_vma=False,
    )
```

```python
import functools
import types

import jax
import jax.numpy as jnp
from jax import lax
from jax.experimental import pallas as pl
from jax.experimental.pallas import tpu as pltpu
from jax.sharding import PartitionSpec as P

H = 16
HD = 64


EPS = 1e-05
NEG = -1000000000.0
SCALE = 0.5


def rms_norm(rows, gain):
    inverse = lax.rsqrt(jnp.mean(rows * rows, axis=-1, keepdims=True) + EPS)
    return (rows * inverse * gain, inverse)


def norm_back(rows, inverse, gain, grad):
    weighted = grad * gain
    return inverse * weighted - rows * inverse**3 * jnp.mean(
        rows * weighted, axis=-1, keepdims=True
    )


def project(rows, weight, enter, leave):
    direct = jnp.einsum("sci,io->sco", rows, weight, preferred_element_type=jnp.float32)
    inner = jnp.einsum("sci,sri->scr", rows, enter, preferred_element_type=jnp.float32).astype(
        jnp.bfloat16
    )
    return (
        direct
        + SCALE * jnp.einsum("scr,sro->sco", inner, leave, preferred_element_type=jnp.float32),
        inner,
    )


def project_back(rows, inner, weight, enter, leave, grad):
    inner_grad = (
        SCALE * jnp.einsum("sco,sro->scr", grad, leave, preferred_element_type=jnp.float32)
    ).astype(jnp.bfloat16)
    rows_grad = jnp.einsum("sco,io->sci", grad, weight, preferred_element_type=jnp.float32)
    rows_grad = rows_grad + jnp.einsum(
        "scr,sri->sci", inner_grad, enter, preferred_element_type=jnp.float32
    )
    enter_grad = jnp.einsum("scr,sci->sri", inner_grad, rows, preferred_element_type=jnp.float32)
    leave_grad = SCALE * jnp.einsum("scr,sco->sro", inner, grad, preferred_element_type=jnp.float32)
    return (rows_grad, enter_grad, leave_grad)


def masked_scores(query_heads, key_block, seg_query, seg_key):
    seqs = query_heads.shape[0]
    key_heads = key_block.reshape(seqs, -1, H, HD)
    scores = (
        jnp.einsum("sqhd,skhd->shqk", query_heads, key_heads, preferred_element_type=jnp.float32)
        * 0.125
    )
    same = seg_query[:, None, :, None] == seg_key[:, None, None, :]
    return (jnp.where(same, scores, NEG), key_heads)


def forward_block(state, query_heads, seg_query, key_block, value_block, seg_key):
    best, total, accum = state
    seqs = query_heads.shape[0]
    scores, key_heads = masked_scores(query_heads, key_block, seg_query, seg_key)
    value_heads = value_block.reshape(seqs, -1, H, HD)
    new_best = jnp.maximum(best, jnp.max(scores, axis=-1))
    factor = jnp.exp(best - new_best)
    weights = jnp.exp(scores - new_best[..., None])
    total = total * factor + jnp.sum(weights, axis=-1)
    mixed = jnp.einsum(
        "shqk,skhd->sqhd",
        weights.astype(jnp.bfloat16),
        value_heads,
        preferred_element_type=jnp.float32,
    )
    accum = accum * jnp.transpose(factor, (0, 2, 1))[..., None] + mixed
    return (new_best, total, accum)


def attend(query, key, value, seg_rows, my_start):
    seqs, rows, width = query.shape
    query_heads = query.reshape(seqs, rows, H, HD)
    seg_query = lax.dynamic_slice_in_dim(seg_rows, my_start, rows, 1)
    state = (
        jnp.full((seqs, H, rows), -1e30, jnp.float32),
        jnp.zeros((seqs, H, rows), jnp.float32),
        jnp.zeros((seqs, rows, H, HD), jnp.float32),
    )

    def fold(carry, piece, start):
        key_piece, value_piece = piece
        count = key_piece.shape[1]
        block = 512

        def advance(index, inner_state):
            offset = index * block
            key_block = lax.dynamic_slice_in_dim(key_piece, offset, block, 1)
            value_block = lax.dynamic_slice_in_dim(value_piece, offset, block, 1)
            seg_key = lax.dynamic_slice_in_dim(seg_rows, offset, block, 1)
            return forward_block(
                inner_state, query_heads, seg_query, key_block, value_block, seg_key
            )

        return lax.fori_loop(0, count // block, advance, carry)

    best, total, accum = fold(
        state,
        (
            lax.all_gather(key, "ctx", axis=1, tiled=True),
            lax.all_gather(value, "ctx", axis=1, tiled=True),
        ),
        jnp.int32(0),
    )
    output = accum / jnp.transpose(total, (0, 2, 1))[..., None]
    return (output, best + jnp.log(total))


def block_grads(
    query_heads, grad_heads, log_total, delta, seg_query, key_block, value_block, seg_key
):
    seqs = query_heads.shape[0]
    scores, key_heads = masked_scores(query_heads, key_block, seg_query, seg_key)
    value_heads = value_block.reshape(seqs, -1, H, HD)
    probs = jnp.exp(scores - log_total[..., None])
    value_part = jnp.einsum(
        "shqk,sqhd->skhd",
        probs.astype(jnp.bfloat16),
        grad_heads,
        preferred_element_type=jnp.float32,
    )
    prob_grad = jnp.einsum(
        "sqhd,skhd->shqk", grad_heads, value_heads, preferred_element_type=jnp.float32
    )
    score_grad = (probs * (prob_grad - delta[..., None])).astype(jnp.bfloat16)
    query_part = 0.125 * jnp.einsum(
        "shqk,skhd->sqhd", score_grad, key_heads, preferred_element_type=jnp.float32
    )
    key_part = 0.125 * jnp.einsum(
        "shqk,sqhd->skhd", score_grad, query_heads, preferred_element_type=jnp.float32
    )
    return (query_part, key_part, value_part)


def attend_back(query, key, value, grad, output, log_total, seg_rows, my_start):
    seqs, rows, width = query.shape
    length = seg_rows.shape[1]
    query_heads = query.reshape(seqs, rows, H, HD)
    grad_heads = grad.reshape(seqs, rows, H, HD)
    seg_query = lax.dynamic_slice_in_dim(seg_rows, my_start, rows, 1)
    delta = jnp.transpose(jnp.sum(grad_heads.astype(jnp.float32) * output, axis=-1), (0, 2, 1))
    state = (
        jnp.zeros((seqs, rows, H, HD), jnp.float32),
        jnp.zeros((seqs, length, width), jnp.float32),
        jnp.zeros((seqs, length, width), jnp.float32),
    )

    def fold(carry, piece, start):
        key_piece, value_piece = piece
        count = key_piece.shape[1]
        block = 512

        def advance(index, inner_state):
            offset = index * block
            key_block = lax.dynamic_slice_in_dim(key_piece, offset, block, 1)
            value_block = lax.dynamic_slice_in_dim(value_piece, offset, block, 1)
            seg_key = lax.dynamic_slice_in_dim(seg_rows, offset, block, 1)
            query_part, key_part, value_part = block_grads(
                query_heads,
                grad_heads,
                log_total,
                delta,
                seg_query,
                key_block,
                value_block,
                seg_key,
            )
            query_grad, key_all, value_all = inner_state
            key_old = lax.dynamic_slice_in_dim(key_all, offset, block, 1)
            key_all = lax.dynamic_update_slice_in_dim(
                key_all, key_old + key_part.reshape(seqs, block, width), offset, 1
            )
            value_old = lax.dynamic_slice_in_dim(value_all, offset, block, 1)
            value_all = lax.dynamic_update_slice_in_dim(
                value_all, value_old + value_part.reshape(seqs, block, width), offset, 1
            )
            return (query_grad + query_part, key_all, value_all)

        return lax.fori_loop(0, count // block, advance, carry)

    folded = fold(
        state,
        (
            lax.all_gather(key, "ctx", axis=1, tiled=True),
            lax.all_gather(value, "ctx", axis=1, tiled=True),
        ),
        jnp.int32(0),
    )
    query_grad = folded[0]
    key_grad, value_grad = (
        lax.psum_scatter(
            folded[1].astype(jnp.bfloat16), "ctx", scatter_dimension=1, tiled=True
        ).astype(jnp.float32),
        lax.psum_scatter(
            folded[2].astype(jnp.bfloat16), "ctx", scatter_dimension=1, tiled=True
        ).astype(jnp.float32),
    )
    return (
        query_grad.reshape(seqs, rows, width).astype(jnp.bfloat16),
        key_grad.astype(jnp.bfloat16),
        value_grad.astype(jnp.bfloat16),
    )


def per_device(
    inputs,
    segment_ids,
    adapter_ids,
    w_query,
    w_key,
    w_value,
    w_out,
    w_gate,
    w_up,
    w_down,
    gain_attn,
    gain_ffn,
    attn_enter,
    attn_leave,
    out_enter,
    out_leave,
    mlp_enter,
    mlp_leave,
    last_enter,
    last_leave,
    out_grad,
):
    micro_count, seqs, rows, width = inputs.shape
    my_start = lax.axis_index("ctx") * rows
    adapter_count = attn_enter.shape[1]
    sum_attn_enter = jnp.zeros(attn_enter.shape, jnp.float32)
    sum_attn_leave = jnp.zeros(attn_leave.shape, jnp.float32)
    sum_out_enter = jnp.zeros(out_enter.shape, jnp.float32)
    sum_out_leave = jnp.zeros(out_leave.shape, jnp.float32)
    sum_mlp_enter = jnp.zeros(mlp_enter.shape, jnp.float32)
    sum_mlp_leave = jnp.zeros(mlp_leave.shape, jnp.float32)
    sum_last_enter = jnp.zeros(last_enter.shape, jnp.float32)
    sum_last_leave = jnp.zeros(last_leave.shape, jnp.float32)
    outputs = []
    gradients = []
    for micro in range(micro_count):
        frozen = (
            lax.all_gather(w_query, ("dp", "ctx"), axis=0, tiled=True),
            lax.all_gather(w_key, ("dp", "ctx"), axis=0, tiled=True),
            lax.all_gather(w_value, ("dp", "ctx"), axis=0, tiled=True),
            lax.all_gather(w_out, ("dp", "ctx"), axis=0, tiled=True),
            lax.all_gather(w_gate, ("dp", "ctx"), axis=0, tiled=True),
            lax.all_gather(w_up, ("dp", "ctx"), axis=0, tiled=True),
            lax.all_gather(w_down, ("dp", "ctx"), axis=0, tiled=True),
            lax.all_gather(gain_attn, ("dp", "ctx"), axis=0, tiled=True),
            lax.all_gather(gain_ffn, ("dp", "ctx"), axis=0, tiled=True),
        )
        query_w, key_w, value_w, out_w, gate_w, up_w, down_w, gain_one, gain_two = frozen
        chosen = adapter_ids[micro]
        attn_in = jnp.take(attn_enter, chosen, axis=1)
        attn_out = jnp.take(attn_leave, chosen, axis=1)
        out_in = jnp.take(out_enter, chosen, axis=0)
        out_out = jnp.take(out_leave, chosen, axis=0)
        mlp_in = jnp.take(mlp_enter, chosen, axis=1)
        mlp_out = jnp.take(mlp_leave, chosen, axis=1)
        last_in = jnp.take(last_enter, chosen, axis=0)
        last_out = jnp.take(last_leave, chosen, axis=0)
        seg_rows = segment_ids[micro]
        start_rows = inputs[micro].astype(jnp.float32)
        normed_f, inverse_one = rms_norm(start_rows, gain_one.astype(jnp.float32))
        normed = normed_f.astype(jnp.bfloat16)
        query_f, query_inner = project(normed, query_w, attn_in[0], attn_out[0])
        key_f, key_inner = project(normed, key_w, attn_in[1], attn_out[1])
        value_f, value_inner = project(normed, value_w, attn_in[2], attn_out[2])
        query = query_f.astype(jnp.bfloat16)
        key = key_f.astype(jnp.bfloat16)
        value = value_f.astype(jnp.bfloat16)
        mixed_f, log_total = attend(query, key, value, seg_rows, my_start)
        mixed = mixed_f.reshape(seqs, rows, width).astype(jnp.bfloat16)
        branch, out_inner = project(mixed, out_w, out_in, out_out)
        middle = start_rows + branch
        normed_two_f, inverse_two = rms_norm(middle, gain_two.astype(jnp.float32))
        normed_two = normed_two_f.astype(jnp.bfloat16)
        gate, gate_inner = project(normed_two, gate_w, mlp_in[0], mlp_out[0])
        upper, up_inner = project(normed_two, up_w, mlp_in[1], mlp_out[1])
        sigma = jax.nn.sigmoid(gate)
        hidden = (gate * sigma * upper).astype(jnp.bfloat16)
        closing, last_inner = project(hidden, down_w, last_in, last_out)
        outputs.append((middle + closing).astype(jnp.bfloat16))
        frozen = (
            lax.all_gather(w_query, ("dp", "ctx"), axis=0, tiled=True),
            lax.all_gather(w_key, ("dp", "ctx"), axis=0, tiled=True),
            lax.all_gather(w_value, ("dp", "ctx"), axis=0, tiled=True),
            lax.all_gather(w_out, ("dp", "ctx"), axis=0, tiled=True),
            lax.all_gather(w_gate, ("dp", "ctx"), axis=0, tiled=True),
            lax.all_gather(w_up, ("dp", "ctx"), axis=0, tiled=True),
            lax.all_gather(w_down, ("dp", "ctx"), axis=0, tiled=True),
            lax.all_gather(gain_attn, ("dp", "ctx"), axis=0, tiled=True),
            lax.all_gather(gain_ffn, ("dp", "ctx"), axis=0, tiled=True),
        )
        query_w, key_w, value_w, out_w, gate_w, up_w, down_w, gain_one, gain_two = frozen
        grad_rows = out_grad[micro].astype(jnp.float32)
        hidden_grad, last_in_grad, last_out_grad = project_back(
            hidden, last_inner, down_w, last_in, last_out, out_grad[micro]
        )
        gate_grad = (hidden_grad * upper * sigma * (1.0 + gate * (1.0 - sigma))).astype(
            jnp.bfloat16
        )
        up_grad = (hidden_grad * gate * sigma).astype(jnp.bfloat16)
        from_gate, gate_in_grad, gate_out_grad = project_back(
            normed_two, gate_inner, gate_w, mlp_in[0], mlp_out[0], gate_grad
        )
        from_up, up_in_grad, up_out_grad = project_back(
            normed_two, up_inner, up_w, mlp_in[1], mlp_out[1], up_grad
        )
        middle_grad = grad_rows + norm_back(
            middle, inverse_two, gain_two.astype(jnp.float32), from_gate + from_up
        )
        mixed_grad_f, out_in_grad, out_out_grad = project_back(
            mixed, out_inner, out_w, out_in, out_out, middle_grad.astype(jnp.bfloat16)
        )
        mixed_grad = mixed_grad_f.astype(jnp.bfloat16)
        query_grad, key_grad, value_grad = attend_back(
            query, key, value, mixed_grad, mixed_f, log_total, seg_rows, my_start
        )
        from_query, query_in_grad, query_out_grad = project_back(
            normed, query_inner, query_w, attn_in[0], attn_out[0], query_grad
        )
        from_key, key_in_grad, key_out_grad = project_back(
            normed, key_inner, key_w, attn_in[1], attn_out[1], key_grad
        )
        from_value, value_in_grad, value_out_grad = project_back(
            normed, value_inner, value_w, attn_in[2], attn_out[2], value_grad
        )
        gradients.append(
            middle_grad
            + norm_back(
                start_rows,
                inverse_one,
                gain_one.astype(jnp.float32),
                from_query + from_key + from_value,
            )
        )
        per_seq = (
            jnp.stack([query_in_grad, key_in_grad, value_in_grad]),
            jnp.stack([query_out_grad, key_out_grad, value_out_grad]),
            out_in_grad,
            out_out_grad,
            jnp.stack([gate_in_grad, up_in_grad]),
            jnp.stack([gate_out_grad, up_out_grad]),
            last_in_grad,
            last_out_grad,
        )
        onehot = (chosen[:, None] == jnp.arange(adapter_count, dtype=jnp.int32)[None, :]).astype(
            jnp.float32
        )
        sum_attn_enter = sum_attn_enter + jnp.einsum("sa,isrd->iard", onehot, per_seq[0])
        sum_attn_leave = sum_attn_leave + jnp.einsum("sa,isrd->iard", onehot, per_seq[1])
        sum_out_enter = sum_out_enter + jnp.einsum("sa,srd->ard", onehot, per_seq[2])
        sum_out_leave = sum_out_leave + jnp.einsum("sa,srd->ard", onehot, per_seq[3])
        sum_mlp_enter = sum_mlp_enter + jnp.einsum("sa,isrd->iard", onehot, per_seq[4])
        sum_mlp_leave = sum_mlp_leave + jnp.einsum("sa,isrf->iarf", onehot, per_seq[5])
        sum_last_enter = sum_last_enter + jnp.einsum("sa,srf->arf", onehot, per_seq[6])
        sum_last_leave = sum_last_leave + jnp.einsum("sa,srd->ard", onehot, per_seq[7])
    totals = (
        sum_attn_enter,
        sum_attn_leave,
        sum_out_enter,
        sum_out_leave,
        sum_mlp_enter,
        sum_mlp_leave,
        sum_last_enter,
        sum_last_leave,
    )
    summed = lax.psum(
        (totals[0], totals[1], totals[2], totals[3], totals[4], totals[5], totals[6], totals[7]),
        ("dp", "ctx"),
    )
    return (
        jnp.stack(outputs),
        jnp.stack(gradients),
        summed[0],
        summed[1],
        summed[2],
        summed[3],
        summed[4],
        summed[5],
        summed[6],
        summed[7],
    )


MESH = pl.DeviceIdType.MESH
BF = jnp.bfloat16
F32 = jnp.float32
SAME = (1, 4, 5)
PEERS = ((0, 1), (0, 4), (0, 5), (1, 0), (1, 1), (1, 4), (1, 5))
ACROSS = ((0, 2), (0, 8), (0, 10))
GREET = PEERS + ACROSS + ((1, 2), (1, 10))
DOUBLE = (8, 4, 1, 2)
FAR = 32
HELD = (0, 8, 4, 12, 1, 9, 5, 13, 2, 10, 6, 14, 3, 11, 7, 15)
WIDTHS = (1536, 896, 512)


def dot(left, right):
    return lax.dot_general(left, right, (((1,), (0,)), ((), ())), preferred_element_type=F32)


def dot_t(left, right):
    return lax.dot_general(left, right, (((1,), (1,)), ((), ())), preferred_element_type=F32)


class Spot:
    def __init__(self, p, x, y, zl, zh):
        self.p, self.x, self.y, self.zl, self.zh = p, x, y, zl, zh

    def flip(self, a, b):
        return Spot(
            1 - self.p if a else self.p,
            1 - self.x if b & 1 else self.x,
            1 - self.y if b & 2 else self.y,
            1 - self.zl if b & 4 else self.zl,
            1 - self.zh if b & 8 else self.zh,
        )

    def device(self):
        return (self.p, self.x + 2 * self.y + 4 * self.zl + 8 * self.zh)

    def member(self):
        return self.p * 4 + self.zl * 2 + self.x

    def group(self):
        return self.zh * 2 + self.y


def here():
    p, c = lax.axis_index("dp"), lax.axis_index("ctx")
    return Spot(p, lax.rem(c, 2), lax.rem(lax.div(c, 2), 2), lax.rem(lax.div(c, 4), 2), lax.div(c, 8))


def part(index, size):
    return pl.ds(pl.multiple_of(index * size, size), size)


def remote(src, dst, ssem, rsem, spot):
    return pltpu.make_async_remote_copy(
        src_ref=src, dst_ref=dst, send_sem=ssem, recv_sem=rsem, device_id=spot.device(), device_id_type=MESH
    )


def pick(raw, mask):
    total = raw[0].astype(F32) * mask(0)
    for a in range(1, raw.shape[0]):
        total = total + raw[a].astype(F32) * mask(a)
    return total


def layer_kernel(names, *refs):
    R = types.SimpleNamespace(**dict(zip(names, refs, strict=True)))
    me = here()
    p, x, y, zl, zh = me.p, me.x, me.y, me.zl, me.zh
    j = me.member()
    own = part(j, 128)
    partner = me.flip(1, 0)
    late = []

    def send(src, dst, ssem, rsem, spot):
        copy = remote(src, dst, ssem, rsem, spot)
        copy.start()
        late.append(copy)

    def arrived(ref, ssem, rsem, spot):
        remote(ref, ref, ssem, rsem, spot).wait_recv()

    barrier = pltpu.get_barrier_semaphore()
    for a, b in GREET:
        pl.semaphore_signal(barrier, inc=1, device_id=me.flip(a, b).device(), device_id_type=MESH)
    pl.semaphore_wait(barrier, len(GREET))

    def reshard(src, dst, ssem, rsem):
        rows = pl.ds(pl.multiple_of((y * 4 + zl * 2 + x) * 128 + zh * 64, 64), 64)

        @pl.when(p == y)
        def _():
            pltpu.make_async_copy(src.at[zh], dst.at[rows], rsem.at[0]).start()
            remote(src.at[1 - zh], dst.at[rows], ssem.at[1], rsem.at[1], me.flip(0, 8)).start()

        @pl.when(p != y)
        def _():
            remote(src.at[zh], dst.at[rows], ssem.at[0], rsem.at[0], me.flip(1, 2)).start()
            remote(src.at[1 - zh], dst.at[rows], ssem.at[1], rsem.at[1], me.flip(1, 10)).start()

    def reshard_wait(dst, rsem):
        for k, t in enumerate((zh, 1 - zh)):
            rows = pl.ds(pl.multiple_of(j * 128 + t * 64, 64), 64)
            pltpu.make_async_copy(dst.at[rows], dst.at[rows], rsem.at[k]).wait()

    def reshard_sent(src, ssem):
        @pl.when(p != y)
        def _():
            remote(src.at[zh], src.at[zh], ssem.at[0], ssem.at[0], me.flip(1, 2)).wait_send()

        remote(src.at[zh], src.at[zh], ssem.at[1], ssem.at[1], me.flip(0, 8)).wait_send()

    def spread(ref, ssem, rsem):
        mine = ref.at[own]
        for k, spot in enumerate((me.flip(0, 1), me.flip(0, 4), partner)):
            send(mine, mine, ssem.at[k], rsem.at[k], spot)

    def rows_at(ref, spot, k):
        first, rows = ((0, FAR), (FAR, 128 - FAR))[k]
        return ref.at[pl.ds(pl.multiple_of(spot.member() * 128 + first, 32), rows)]

    def spread_on(ref, ssem, rsem):
        for k, (came, on) in enumerate(((1, 4), (4, 1))):
            spot = me.flip(0, came)
            got, half = ref.at[part(spot.member(), 128)], rows_at(ref, spot, k)
            arrived(got, ssem.at[k], rsem.at[k], spot)
            send(half, half, ssem.at[3 + k], rsem.at[3 + k], me.flip(0, on))
            send(got, got, ssem.at[5 + k], rsem.at[5 + k], partner)

    def spread_far(ref, ssem, rsem):
        for k, on in enumerate((4, 1)):
            half = rows_at(ref, me.flip(0, 5), k)
            arrived(half, ssem.at[3 + k], rsem.at[3 + k], me.flip(0, on))
            send(half, half, ssem.at[7 + k], rsem.at[7 + k], partner)

    def spread_end(ref, ssem, rsem):
        arrived(ref.at[part(partner.member(), 128)], ssem.at[2], rsem.at[2], partner)
        for k, came in enumerate((1, 4)):
            arrived(ref.at[part(me.flip(1, came).member(), 128)], ssem.at[5 + k], rsem.at[5 + k], partner)
            arrived(rows_at(ref, me.flip(1, 5), k), ssem.at[7 + k], rsem.at[7 + k], partner)

    def share(view, ssem, rsem):
        mine = view(me)
        for k, b in enumerate(SAME):
            send(mine, mine, ssem.at[k], rsem.at[k], me.flip(0, b))
        send(mine, mine, ssem.at[3], rsem.at[3], partner)

    def share_on(view, ssem, rsem):
        for k, b in enumerate(SAME):
            got = view(me.flip(0, b))
            arrived(got, ssem.at[k], rsem.at[k], me.flip(0, b))
            send(got, got, ssem.at[4 + k], rsem.at[4 + k], partner)

    def share_end(view, ssem, rsem):
        arrived(view(partner), ssem.at[3], rsem.at[3], partner)
        for k, b in enumerate(SAME):
            arrived(view(me.flip(1, b)), ssem.at[4 + k], rsem.at[4 + k], partner)

    def double(view, ssem, rsem, step):
        for k in range(2**step):
            ref, n = view(me.flip(0, HELD[k])), 2**step - 1 + k
            send(ref, ref, ssem.at[n], rsem.at[n], me.flip(0, DOUBLE[step]))
        if step == 0:
            send(view(me), view(me), ssem.at[15], rsem.at[15], partner)

    def double_on(view, ssem, rsem, step):
        for k in range(2**step):
            ref, n = view(me.flip(0, HELD[2**step + k])), 2**step - 1 + k
            arrived(ref, ssem.at[n], rsem.at[n], me.flip(0, DOUBLE[step]))
            send(ref, ref, ssem.at[16 + n], rsem.at[16 + n], partner)
        if step < 3:
            double(view, ssem, rsem, step + 1)

    def double_end(view, ssem, rsem):
        for k in range(16):
            arrived(view(me.flip(1, HELD[k])), ssem.at[15 + k], rsem.at[15 + k], partner)

    def across(views, ssem, rsem, axis, pieces=(0,)):
        for k in pieces:
            view = views(me)[k]
            send(view, view, ssem.at[axis, k], rsem.at[axis, k], me.flip(0, (8, 2)[axis]))

    def across_on(views, ssem, rsem, pieces=(0,)):
        for k in pieces:
            view = views(me.flip(0, 8))[k]
            arrived(view, ssem.at[0, k], rsem.at[0, k], me.flip(0, 8))
            send(view, view, ssem.at[2, k], rsem.at[2, k], me.flip(0, 2))

    def across_end(views, ssem, rsem):
        for k, view in enumerate(views(me.flip(0, 2))):
            arrived(view, ssem.at[1, k], rsem.at[1, k], me.flip(0, 2))
        for k, view in enumerate(views(me.flip(0, 10))):
            arrived(view, ssem.at[2, k], rsem.at[2, k], me.flip(0, 2))

    def row_views(ref, columns):
        def views(spot):
            return [
                ref.at[pl.ds(pl.multiple_of(pp * 512 + spot.zh * 256 + zz * 128 + spot.y * 64, 64), 64), pl.ds(0, columns)]
                for pp in range(2)
                for zz in range(2)
            ]

        return views

    qkv_views, gu_views = row_views(R.qkvb, 384), row_views(R.gub, 1024)

    def down_views(spot):
        return [R.db.at[part(spot.group(), 128), pl.ds(0, 1024)]]

    def out_view(spot):
        k_row = (spot.p * 16 + spot.zh * 8 + spot.zl * 4 + spot.y * 2 + spot.x) * 32
        return R.ob.at[pl.ds(pl.multiple_of(k_row, 32), 32), pl.ds(0, 1024)]

    def gain_views(spot):
        return [R.gs.at[spot.group()]]

    my_row = pl.ds(pl.multiple_of((p * 16 + zh * 8 + zl * 4 + y * 2 + x) * 32, 32), 32)

    raws = (
        (R.ae, R.ae_h), (R.al, R.al_h.at[:, :, :, own]), (R.oe, R.oe_h), (R.ol, R.ol_h), (R.me, R.me_h), (R.ll, R.ll_h),
    )
    locals_ = []
    for k, (dst, src) in enumerate(raws):
        locals_.append(pltpu.make_async_copy(src, dst, R.la.at[k]))
    for q in range(4):
        fb = part(p * 16 + (q // 2) * 8 + zl * 4 + (q % 2) * 2 + x, 128)
        locals_.append(pltpu.make_async_copy(R.ml_h.at[:, :, :, fb], R.ml.at[:, :, :, pl.ds(q * 128, 128)], R.la.at[8 + q]))
        locals_.append(pltpu.make_async_copy(R.le_h.at[:, :, fb], R.le.at[:, :, pl.ds(q * 128, 128)], R.la.at[12 + q]))

    reshard(R.x_h, R.xf, R.xs, R.xr)

    gain_mine = R.gs.at[me.group(), j]
    gain_local = pltpu.make_async_copy(R.gain_h, gain_mine, R.g1r.at[7])
    gain_local.start()
    for k, (a, b) in enumerate(PEERS):
        send(R.gain_h, gain_mine, R.g1s.at[k], R.g1r.at[k], me.flip(a, b))

    def columns_to(spot, k, start):
        t = spot.member()
        for i, src in enumerate((R.wq_h, R.wk_h, R.wv_h)):
            start(src.at[:, part(t, 128)], R.qkvb.at[my_row, pl.ds(i * 128, 128)], R.w1qs.at[k, i], R.w1qr.at[k, i])

    def mlp_columns_to(spot, k, start):
        for i, src in enumerate((R.wg_h, R.wu_h)):
            for q in range(4):
                fb = part(spot.p * 16 + (q // 2) * 8 + spot.zl * 4 + (q % 2) * 2 + spot.x, 128)
                at = (k, i * 4 + q)
                start(src.at[:, fb], R.gub.at[my_row, pl.ds(i * 512 + q * 128, 128)], R.w1ms.at[*at], R.w1mr.at[*at])

    def start_remote(spot):
        return lambda src, dst, ssem, rsem: send(src, dst, ssem, rsem, spot)

    def start_local(src, dst, ssem, rsem):
        pltpu.make_async_copy(src, dst, rsem).start()

    for k, (a, b) in enumerate(PEERS):
        columns_to(me.flip(a, b), k, start_remote(me.flip(a, b)))
    columns_to(me, 7, start_local)

    meta_local = pltpu.make_async_copy(R.meta_h, R.meta.at[p], R.mr.at[1])
    meta_local.start()
    send(R.meta_h, R.meta.at[p], R.ms.at[0], R.mr.at[0], partner)
    for copy in locals_:
        copy.start()

    out_local = pltpu.make_async_copy(R.wo_h, out_view(me), R.wor.at[31])
    out_local.start()
    send(R.wo_h, out_view(me), R.wos.at[0], R.wor.at[0], me.flip(0, DOUBLE[0]))
    send(R.wo_h, out_view(me), R.wos.at[15], R.wor.at[15], partner)
    for k, (a, b) in enumerate(PEERS):
        mlp_columns_to(me.flip(a, b), k, start_remote(me.flip(a, b)))
    mlp_columns_to(me, 7, start_local)

    reshard_wait(R.xf, R.xr)
    spread(R.xf, R.axs, R.axr)

    def rows_of(spot):
        return pl.ds(pl.multiple_of((spot.p * 16 + spot.zh * 8 + spot.zl * 4 + spot.y * 2 + spot.x) * 32, 32), 32)

    def first_end(target, rsem, pieces):
        for k, (a, b) in enumerate(PEERS + ((0, 0),)):
            rows = rows_of(me.flip(a, b))
            for i in range(pieces):
                ref = target.at[rows, pl.ds(i * 128, 128)]
                pltpu.make_async_copy(ref, ref, rsem.at[k, i]).wait()

    first_end(R.qkvb, R.w1qr, 3)
    across(qkv_views, R.w2qs, R.w2qr, 0, range(4))
    across(qkv_views, R.w2qs, R.w2qr, 1, range(4))
    reshard(R.og_h, R.ogf, R.os, R.ors)
    for k, (a, b) in enumerate(PEERS):
        spot = me.flip(a, b)
        arrived(R.gs.at[me.group(), spot.member()], R.g1s.at[k], R.g1r.at[k], spot)
    gain_local.wait()
    across(gain_views, R.g2s, R.g2r, 0)
    across(gain_views, R.g2s, R.g2r, 1)
    spread_on(R.xf, R.axs, R.axr)
    out_local.wait()
    double_on(out_view, R.wos, R.wor, 0)
    across_on(qkv_views, R.w2qs, R.w2qr, range(4))
    first_end(R.gub, R.w1mr, 8)
    across(gu_views, R.w2ms, R.w2mr, 1, range(4))
    across(gu_views, R.w2ms, R.w2mr, 0, (0,))
    down_mine = down_views(me)[0]
    down_local = pltpu.make_async_copy(R.wd_h, down_mine, R.wdr.at[3, 0])
    down_local.start()
    across_on(gain_views, R.g2s, R.g2r)

    pltpu.make_async_copy(R.meta_h, R.meta.at[p], R.mr.at[1]).wait()
    arrived(R.meta.at[1 - p], R.ms.at[0], R.mr.at[0], partner)
    for copy in locals_:
        copy.wait()
    ids = R.meta[y, pl.ds(2 + zh, 1), :]

    def mask(width):
        return lambda a: (ids[:, 0:width] == a).astype(F32)

    def enter_columns(items):
        rows = [pick(item, mask(item.shape[-1])) for item in items]
        width = rows[0].shape[-1]
        rows.append(jnp.zeros((128 - 16 * len(rows), width), F32))
        return jnp.transpose(jnp.concatenate(rows, axis=0)).astype(BF)

    def leave_rows(ref, first, items):
        ref[pl.ds(first, 128), :] = jnp.zeros((128, ref.shape[1]), BF)
        column = 0
        for i, item in enumerate(items):
            width = item.shape[-1]
            ref[pl.ds(first + 16 * i, 16), pl.ds(column, width)] = (SCALE * pick(item, mask(width))).astype(BF)
            column += width

    R.qkvb[pl.ds(0, 1024), pl.ds(384, 128)] = enter_columns([R.ae.at[i] for i in range(3)])
    leave_rows(R.qkvb, 1024, [R.al.at[i] for i in range(3)])
    R.ob[pl.ds(0, 1024), pl.ds(1024, 128)] = enter_columns([R.oe])
    leave_rows(R.ob, 1024, [R.ol])
    R.gub[pl.ds(0, 1024), pl.ds(1024, 128)] = enter_columns([R.me.at[i] for i in range(2)])
    leave_rows(R.gub, 1024, [R.ml.at[i] for i in range(2)])
    R.db[pl.ds(0, 512), pl.ds(1024, 128)] = enter_columns([R.le])
    leave_rows(R.db, 512, [R.ll])

    seg_row = R.meta[y, pl.ds(zh, 1), :]
    R.segc[...] = jnp.transpose(jnp.broadcast_to(seg_row.astype(F32), (128, 1024)))

    across(gu_views, R.w2ms, R.w2mr, 0, (1,))
    double_on(out_view, R.wos, R.wor, 1)
    across_end(gain_views, R.g2s, R.g2r)
    gains = jnp.sum(jnp.sum(R.gs[...], axis=0), axis=0)
    gain_one = jnp.concatenate([gains[i : i + 1] for i in range(8)], axis=1)
    gain_two = jnp.concatenate([gains[i : i + 1] for i in range(8, 16)], axis=1)

    spread_far(R.xf, R.axs, R.axr)
    spread_end(R.xf, R.axs, R.axr)
    reshard_wait(R.ogf, R.ors)
    spread(R.ogf, R.aos, R.aor)
    across(gu_views, R.w2ms, R.w2mr, 0, (2,))
    double_on(out_view, R.wos, R.wor, 2)
    across_end(qkv_views, R.w2qs, R.w2qr)

    def qkv_tile(t, carry):
        rows = part(t, 256)
        held = R.xf[rows, :].astype(F32)
        inverse = lax.rsqrt(jnp.mean(held * held, axis=-1, keepdims=True) + EPS)
        normed = (held * inverse * gain_one).astype(BF)
        both = dot(normed, R.qkvb[0:1024, :])
        inner = both[:, 384:512]
        qkv = both[:, 0:384] + dot(inner.astype(BF), R.qkvb[1024:1152, 0:384])
        R.n1c[rows, :] = (R.xf[rows, own].astype(F32) * inverse * R.g1v[:, own]).astype(BF)
        R.r1t[:, rows] = jnp.transpose(inner).astype(BF)
        R.qb[rows, :] = (qkv[:, 0:128].astype(BF).astype(F32) * 0.125).astype(BF)
        R.kb[rows, :] = qkv[:, 128:256].astype(BF)
        R.vb[rows, :] = qkv[:, 256:384].astype(BF)
        R.kt[:, rows] = jnp.transpose(qkv[:, 128:256]).astype(BF)
        R.vt[:, rows] = jnp.transpose(qkv[:, 256:384]).astype(BF)
        return carry

    R.g1v[...] = gain_one
    lax.fori_loop(0, 4, qkv_tile, 0)

    across(gu_views, R.w2ms, R.w2mr, 0, (3,))

    head_of = lax.broadcasted_iota(jnp.int32, (256, 128), 1) // HD

    def attend_tile(t, carry):
        rows = part(t, 256)
        queries = R.qb[rows, :]
        same = R.segc[:, 0:1] == R.meta[y, pl.ds(zh, 1), rows].astype(F32)
        mixed = []
        for h in range(2):
            mine = jnp.where(head_of == h, queries.astype(F32), 0.0).astype(BF)
            scores = jnp.where(same, dot_t(R.kb[...], mine), NEG)
            weights = jnp.exp(scores - jnp.max(scores, axis=0, keepdims=True))
            probs = (weights * (1.0 / jnp.sum(weights, axis=0, keepdims=True))).astype(BF)
            R.pr[2 * t + h] = probs
            mixed.append(dot(R.vt[h * HD : (h + 1) * HD, :], probs))
        mixed = jnp.concatenate(mixed, axis=0)
        R.att[t] = mixed
        R.ath[rows, :] = jnp.transpose(mixed).astype(BF)
        return carry

    lax.fori_loop(0, 4, attend_tile, 0)

    for k, (a, b) in enumerate(PEERS):
        spot = me.flip(a, b)
        send(R.ath.at[part(spot.member(), 128)], R.ato.at[:, own], R.a1s.at[k], R.a1r.at[k], spot)
    mine_local = pltpu.make_async_copy(R.ath.at[own], R.ato.at[:, own], R.a1r.at[7])
    mine_local.start()

    send(R.wd_h, down_mine, R.wds.at[0, 0], R.wdr.at[0, 0], me.flip(0, 8))
    send(R.wd_h, down_mine, R.wds.at[1, 0], R.wdr.at[1, 0], me.flip(0, 2))
    spread_on(R.ogf, R.aos, R.aor)
    across_on(gu_views, R.w2ms, R.w2mr, (0, 1))
    mine_local.wait()
    for k, (a, b) in enumerate(PEERS):
        spot = me.flip(a, b)
        arrived(R.ato.at[:, part(spot.member(), 128)], R.a1s.at[k], R.a1r.at[k], spot)

    double_on(out_view, R.wos, R.wor, 3)
    double_end(out_view, R.wos, R.wor)
    start_rows = R.xf[own, :].astype(F32)
    both = dot(R.ato[...], R.ob[0:1024, :])
    out_inner = both[:, 1024:1152]
    middle = start_rows + both[:, 0:1024] + dot(out_inner.astype(BF), R.ob[1024:1152, 0:1024])
    R.mid[...] = middle
    inverse = lax.rsqrt(jnp.mean(middle * middle, axis=-1, keepdims=True) + EPS)
    R.n2f[own, :] = (middle * inverse * gain_two).astype(BF)
    R.rot[...] = jnp.transpose(out_inner).astype(BF)
    spread(R.n2f, R.ans, R.anr)

    down_local.wait()
    across_on(gu_views, R.w2ms, R.w2mr, (2, 3))
    across_on(down_views, R.wds, R.wdr)
    spread_far(R.ogf, R.aos, R.aor)
    spread_end(R.ogf, R.aos, R.aor)
    spread_on(R.n2f, R.ans, R.anr)
    spread_far(R.n2f, R.ans, R.anr)
    spread_end(R.n2f, R.ans, R.anr)
    across_end(gu_views, R.w2ms, R.w2mr)
    across_end(down_views, R.wds, R.wdr)

    R.cml[...] = jnp.zeros((128, 1024), F32)
    R.cle[...] = jnp.zeros((128, 512), F32)

    def mlp_tile(i, carry):
        rows = part(lax.rem((1 - p) * 2 + i, 4), 256)
        both = dot(R.n2f[rows, :], R.gub[0:1024, :])
        inner = both[:, 1024:1152]
        pair = both[:, 0:1024] + dot(inner.astype(BF), R.gub[1024:1152, 0:1024])
        gate, upper = pair[:, 0:512], pair[:, 512:1024]
        sigma = jax.nn.sigmoid(gate)
        hidden = (gate * sigma * upper).astype(BF)
        R.zd[rows, :] = dot(hidden, R.db[0:512, :]).astype(BF)
        back = dot_t(R.ogf[rows, :], R.db[:, 0:1024])
        inner_back = back[:, 512:640]
        hidden_grad = back[:, 0:512] + dot_t(inner_back.astype(BF), R.db[0:512, 1024:1152])
        gate_grad = (hidden_grad * upper * sigma * (1.0 + gate * (1.0 - sigma))).astype(BF)
        up_grad = (hidden_grad * gate * sigma).astype(BF)
        pair_grad = jnp.concatenate([gate_grad, up_grad], axis=1)
        R.zn[rows, :] = dot_t(pair_grad, R.gub[:, 0:1024]).astype(BF)
        R.cml[...] += dot(jnp.transpose(inner).astype(BF), pair_grad)
        R.cle[...] += dot(jnp.transpose(inner_back).astype(BF), hidden)
        return carry

    def pair_send(parts, k):
        send(parts.at[part(1 - p, 512)], R.rp.at[k], R.rps.at[k], R.rpr.at[k], partner)

    def chip_send(parts, k):
        arrived(R.rp.at[k], R.rps.at[k], R.rpr.at[k], partner)

        def add(i, carry):
            rows = part(i, 128)
            R.rc[k, rows, :] = (
                parts[part(p * 4 + i, 128), :].astype(F32) + R.rp[k, rows, :].astype(F32)
            ).astype(BF)
            return carry

        lax.fori_loop(0, 4, add, 0)
        for i, b in enumerate(SAME):
            spot = me.flip(0, b)
            send(R.rc.at[k, part(spot.zl * 2 + spot.x, 128)], R.rr.at[k, i], R.rrs.at[k, i], R.rrr.at[k, i], spot)

    def summed(parts, k):
        for i, b in enumerate(SAME):
            arrived(R.rr.at[k, i], R.rrs.at[k, i], R.rrr.at[k, i], me.flip(0, b))
        total = parts[own, :].astype(F32) + R.rp[k, part(zl * 2 + x, 128), :].astype(F32)
        for i in range(3):
            total = total + R.rr[k, i].astype(F32)
        return total

    lax.fori_loop(0, 2, mlp_tile, 0)
    pair_send(R.zn, 0)
    pair_send(R.zd, 1)
    lax.fori_loop(2, 4, mlp_tile, 0)
    chip_send(R.zn, 0)
    for i in range(2):
        R.da[:, pl.ds(i * 512, 512)] = (SCALE * R.cml[i * 16 : (i + 1) * 16, i * 512 : (i + 1) * 512]).astype(BF)
    R.da[:, pl.ds(1024, 512)] = R.cle[0:16, :].astype(BF)

    def first_view(spot):
        return R.ga_o.at[spot.group(), spot.member()]

    def second_view(spot):
        return R.gb_o.at[spot.group(), spot.member()]

    def third_view(spot):
        return R.gc_o.at[spot.group(), spot.member()]

    first_local = pltpu.make_async_copy(R.da, first_view(me), R.gar.at[31])
    first_local.start()
    first_local.wait()
    double(first_view, R.gas, R.gar, 0)

    own_grad = R.ogf[own, :].astype(F32)
    total = summed(R.zn, 0)
    inner_back = total[:, 1024:1152]
    normed_grad = total[:, 0:1024] + dot_t(inner_back.astype(BF), R.gub[0:1024, 1024:1152])
    middle = R.mid[...]
    inverse = lax.rsqrt(jnp.mean(middle * middle, axis=-1, keepdims=True) + EPS)
    middle_grad = own_grad + norm_back(middle, inverse, gain_two, normed_grad)
    R.mg[...] = middle_grad
    rounded = middle_grad.astype(BF)
    both = dot_t(rounded, R.ob[:, 0:1024])
    out_back = both[:, 1024:1152]
    R.gao[...] = (both[:, 0:1024] + dot_t(out_back.astype(BF), R.ob[0:1024, 1024:1152])).astype(BF)
    for k, (a, b) in enumerate(PEERS):
        spot = me.flip(a, b)
        send(R.gao.at[:, part(spot.member(), 128)], R.gah.at[own], R.a2s.at[k], R.a2r.at[k], spot)
    mine_local = pltpu.make_async_copy(R.gao.at[:, own], R.gah.at[own], R.a2r.at[7])
    mine_local.start()
    R.ib[0, own, :] = (inner_back + pltpu.roll(out_back, 32, 1)).astype(BF)

    def rank_view(i):
        return lambda spot: R.ib.at[i, part(spot.member(), 128)]

    share(rank_view(0), R.ibs.at[0], R.ibr.at[0])
    out_leave = (SCALE * dot(R.rot[...], rounded))[0:16].astype(BF)
    for i in range(8):
        R.gp[i] = out_leave[:, i * 128 : (i + 1) * 128]
    for k, (a, b) in enumerate(PEERS):
        spot = me.flip(a, b)
        send(R.gp.at[spot.member()], R.gr.at[k], R.gps.at[k], R.gpr.at[k], spot)
    chip_send(R.zd, 1)
    double_on(first_view, R.gas, R.gar, 0)
    mine_local.wait()
    for k, (a, b) in enumerate(PEERS):
        spot = me.flip(a, b)
        arrived(R.gah.at[part(spot.member(), 128)], R.a2s.at[k], R.a2r.at[k], spot)

    share_on(rank_view(0), R.ibs.at[0], R.ibr.at[0])
    R.gk[...] = jnp.zeros((1024, 128), F32)
    R.gv[...] = jnp.zeros((1024, 128), F32)

    def attend_back_tile(t, carry):
        rows = part(t, 256)
        queries, grads = R.qb[rows, :].astype(F32), R.gah[rows, :].astype(F32)
        delta_parts = jnp.transpose(grads) * R.att[t]
        query_grad = []
        for h in range(2):
            mine = jnp.where(head_of == h, queries, 0.0).astype(BF)
            grad = jnp.where(head_of == h, grads, 0.0).astype(BF)
            probs = R.pr[2 * t + h]
            delta = jnp.sum(delta_parts[h * HD : (h + 1) * HD], axis=0, keepdims=True)
            score_grad = (probs.astype(F32) * (dot_t(R.vb[...], grad) - delta)).astype(BF)
            R.gk[...] += dot(score_grad, mine)
            R.gv[...] += dot(probs, grad)
            query_grad.append(dot(R.kt[h * HD : (h + 1) * HD, :], score_grad))
        R.gq[rows, pl.ds(0, 128)] = (jnp.transpose(jnp.concatenate(query_grad, axis=0)) * 0.125).astype(BF)
        return carry

    lax.fori_loop(0, 4, attend_back_tile, 0)
    double_on(first_view, R.gas, R.gar, 1)
    R.gq[:, pl.ds(128, 128)] = R.gk[...].astype(BF)
    R.gq[:, pl.ds(256, 128)] = R.gv[...].astype(BF)

    def qkv_back_tile(i, carry):
        rows = part(lax.rem((1 - p) * 2 + i, 4), 256)
        R.zq[rows, :] = dot_t(R.gq[rows, :], R.qkvb[:, 0:384]).astype(BF)
        return carry

    lax.fori_loop(0, 2, qkv_back_tile, 0)
    pair_send(R.zq, 2)
    lax.fori_loop(2, 4, qkv_back_tile, 0)
    chip_send(R.zq, 2)

    double_on(first_view, R.gas, R.gar, 2)
    leave = SCALE * dot(R.r1t[...], R.gq[...])
    for i in range(3):
        R.db2[:, pl.ds(i * 128, 128)] = leave[i * 16 : (i + 1) * 16, i * 128 : (i + 1) * 128].astype(BF)
    share_end(rank_view(0), R.ibs.at[0], R.ibr.at[0])
    ranks = jnp.transpose(R.ib[0].astype(F32)).astype(BF)
    mlp_enter, out_enter = dot(ranks, R.n2f[:, own]), dot(ranks, R.ath[...])
    block = R.gp[j].astype(F32)
    for k, (a, b) in enumerate(PEERS):
        arrived(R.gr.at[k], R.gps.at[k], R.gpr.at[k], me.flip(a, b))
        block = block + R.gr[k].astype(F32)
    R.db2[:, pl.ds(384, 128)] = out_enter[32:48].astype(BF)
    R.db2[:, pl.ds(512, 128)] = block.astype(BF)
    R.db2[:, pl.ds(640, 128)] = mlp_enter[0:16].astype(BF)
    R.db2[:, pl.ds(768, 128)] = mlp_enter[16:32].astype(BF)
    second_local = pltpu.make_async_copy(R.db2, second_view(me), R.gbr.at[31])
    second_local.start()
    second_local.wait()
    double(second_view, R.gbs, R.gbr, 0)

    total = summed(R.zd, 1)
    last_inner = total[:, 1024:1152]
    R.ib[1, own, :] = last_inner.astype(BF)
    share(rank_view(1), R.ibs.at[1], R.ibr.at[1])
    R.outv[...] = (R.mid[...] + total[:, 0:1024] + dot(last_inner.astype(BF), R.db[512:640, 0:1024])).astype(BF)

    def give_back(src, dst, ssem, rsem):
        spot_same, spot_other = part(zh, 64), part(1 - zh, 64)

        @pl.when(p == y)
        def _():
            pltpu.make_async_copy(src.at[spot_same], dst.at[zh], rsem.at[0]).start()
            remote(src.at[spot_other], dst.at[zh], ssem.at[1], rsem.at[1], me.flip(0, 8)).start()

        @pl.when(p != y)
        def _():
            remote(src.at[spot_same], dst.at[zh], ssem.at[0], rsem.at[0], me.flip(1, 2)).start()
            remote(src.at[spot_other], dst.at[zh], ssem.at[1], rsem.at[1], me.flip(1, 10)).start()

    def give_back_wait(src, dst, ssem, rsem):
        pltpu.make_async_copy(dst.at[zh], dst.at[zh], rsem.at[0]).wait()
        pltpu.make_async_copy(dst.at[1 - zh], dst.at[1 - zh], rsem.at[1]).wait()

        @pl.when(p != y)
        def _():
            remote(src.at[part(zh, 64)], src.at[part(zh, 64)], ssem.at[0], rsem.at[0], me.flip(1, 2)).wait_send()

        remote(src.at[part(zh, 64)], src.at[part(zh, 64)], ssem.at[1], rsem.at[1], me.flip(0, 8)).wait_send()

    give_back(R.outv, R.out_o, R.bos, R.bor)
    double_on(second_view, R.gbs, R.gbr, 0)
    share_on(rank_view(1), R.ibs.at[1], R.ibr.at[1])
    double_on(second_view, R.gbs, R.gbr, 1)

    total = summed(R.zq, 2)
    inner_back = total[:, 1024:1152]
    normed_grad = total[:, 0:1024] + dot_t(inner_back.astype(BF), R.qkvb[0:1024, 384:512])
    start_rows = R.xf[own, :].astype(F32)
    inverse = lax.rsqrt(jnp.mean(start_rows * start_rows, axis=-1, keepdims=True) + EPS)
    R.ib[2, own, :] = inner_back.astype(BF)
    share(rank_view(2), R.ibs.at[2], R.ibr.at[2])
    R.igv[...] = (R.mg[...] + norm_back(start_rows, inverse, gain_one, normed_grad)).astype(BF)

    share_end(rank_view(1), R.ibs.at[1], R.ibr.at[1])
    last_leave = SCALE * dot(jnp.transpose(R.ib[1].astype(F32)).astype(BF), R.ogf[:, own])
    R.dc[:, pl.ds(384, 128)] = last_leave[0:16].astype(BF)
    share_on(rank_view(2), R.ibs.at[2], R.ibr.at[2])
    share_end(rank_view(2), R.ibs.at[2], R.ibr.at[2])
    attn_enter = dot(jnp.transpose(R.ib[2].astype(F32)).astype(BF), R.n1c[...])
    for i in range(3):
        R.dc[:, pl.ds(i * 128, 128)] = attn_enter[i * 16 : (i + 1) * 16].astype(BF)

    third_local = pltpu.make_async_copy(R.dc, third_view(me), R.gcr.at[3, 0])
    third_local.start()
    for k, (a, b) in enumerate(ACROSS):
        send(R.dc, third_view(me), R.gcs.at[k, 0], R.gcr.at[k, 0], me.flip(a, b))
    third_local.wait()
    share(third_view, R.gds.at[3], R.gdr.at[3])
    double_on(second_view, R.gbs, R.gbr, 2)
    give_back(R.igv, R.ig_o, R.bis, R.bir)
    for k, (a, b) in enumerate(ACROSS):
        arrived(third_view(me.flip(a, b)), R.gcs.at[k, 0], R.gcr.at[k, 0], me.flip(a, b))
        share(lambda spot, b=b: third_view(spot.flip(0, b)), R.gds.at[k], R.gdr.at[k])
    double_on(first_view, R.gas, R.gar, 3)
    flips = {0: 2, 1: 8, 2: 10, 3: 0}
    for k in (3, 0, 1, 2):
        share_on(lambda spot, k=k: third_view(spot.flip(0, flips[k])), R.gds.at[k], R.gdr.at[k])
    double_on(second_view, R.gbs, R.gbr, 3)
    double_end(first_view, R.gas, R.gar)
    double_end(second_view, R.gbs, R.gbr)
    for k in (3, 0, 1, 2):
        share_end(lambda spot, k=k: third_view(spot.flip(0, flips[k])), R.gds.at[k], R.gdr.at[k])

    meta_out = pltpu.make_async_copy(R.meta, R.meta_o, R.mr.at[2])
    meta_out.start()
    give_back_wait(R.outv, R.out_o, R.bos, R.bor)
    give_back_wait(R.igv, R.ig_o, R.bis, R.bir)
    reshard_sent(R.x_h, R.xs)
    reshard_sent(R.og_h, R.os)
    for copy in late:
        copy.wait_send()
    meta_out.wait()


def layer_call(**inputs):
    V, S = pltpu.VMEM, pltpu.SemaphoreType.DMA
    outputs = dict(
        out_o=((2, 64, 1024), BF),
        ig_o=((2, 64, 1024), BF),
        ga_o=((4, 8, 16, WIDTHS[0]), BF),
        gb_o=((4, 8, 16, WIDTHS[1]), BF),
        gc_o=((4, 8, 16, WIDTHS[2]), BF),
        meta_o=((2, 8, 1024), jnp.int32),
    )
    scratch = dict(
        xf=V((1024, 1024), BF), ogf=V((1024, 1024), BF), n2f=V((1024, 1024), BF),
        qkvb=V((1152, 512), BF), ob=V((1152, 1152), BF), gub=V((1152, 1152), BF), db=V((640, 1152), BF),
        ae=V((3, 8, 16, 1024), BF), al=V((3, 8, 16, 128), BF), oe=V((8, 16, 1024), BF), ol=V((8, 16, 1024), BF),
        me=V((2, 8, 16, 1024), BF), ml=V((2, 8, 16, 512), BF), le=V((8, 16, 512), BF), ll=V((8, 16, 1024), BF),
        meta=V((2, 8, 1024), jnp.int32), gs=V((4, 8, 16, 128), F32), segc=V((1024, 128), F32),
        qb=V((1024, 128), BF), kb=V((1024, 128), BF), vb=V((1024, 128), BF), kt=V((128, 1024), BF),
        vt=V((128, 1024), BF), r1t=V((128, 1024), BF), pr=V((8, 1024, 256), BF), att=V((4, 128, 256), F32),
        ath=V((1024, 128), BF), ato=V((128, 1024), BF), mid=V((128, 1024), F32), mg=V((128, 1024), F32),
        rot=V((128, 128), BF), zn=V((1024, 1152), BF), zd=V((1024, 1152), BF), zq=V((1024, 1152), BF),
        rp=V((3, 512, 1152), BF), rc=V((3, 512, 1152), BF), rr=V((3, 3, 128, 1152), BF),
        cml=V((128, 1024), F32), cle=V((128, 512), F32), gao=V((128, 1024), BF), gah=V((1024, 128), BF),
        gk=V((1024, 128), F32), gv=V((1024, 128), F32), gq=V((1024, 384), BF), outv=V((128, 1024), BF),
        igv=V((128, 1024), BF), gp=V((8, 16, 128), BF), gr=V((7, 16, 128), BF), da=V((16, WIDTHS[0]), BF),
        db2=V((16, WIDTHS[1]), BF), dc=V((16, WIDTHS[2]), BF), ib=V((3, 1024, 128), BF), n1c=V((1024, 128), BF), g1v=V((1, 1024), F32),
        la=S((16,)), xs=S((2,)), xr=S((2,)), os=S((2,)), ors=S((2,)), g1s=S((7,)), g1r=S((8,)),
        g2s=S((3, 1)), g2r=S((3, 1)), w1qs=S((8, 3)), w1qr=S((8, 3)), w1ms=S((8, 8)), w1mr=S((8, 8)),
        w2qs=S((3, 4)), w2qr=S((3, 4)), w2ms=S((3, 4)), w2mr=S((3, 4)), wos=S((31,)), wor=S((32,)),
        wds=S((3, 1)), wdr=S((4, 1)), ms=S((1,)), mr=S((3,)), axs=S((9,)), axr=S((9,)),
        aos=S((9,)), aor=S((9,)), ans=S((9,)), anr=S((9,)), ibs=S((3, 7)), ibr=S((3, 7)),
        a1s=S((7,)), a1r=S((8,)), a2s=S((7,)), a2r=S((8,)), rps=S((3,)), rpr=S((3,)),
        rrs=S((3, 3)), rrr=S((3, 3)), bos=S((2,)), bor=S((2,)), bis=S((2,)), bir=S((2,)),
        gps=S((7,)), gpr=S((7,)), gas=S((31,)), gar=S((32,)), gbs=S((31,)), gbr=S((32,)),
        gcs=S((3, 1)), gcr=S((4, 1)), gds=S((4, 7)), gdr=S((4, 7)),
    )
    names = list(inputs) + list(outputs) + list(scratch)
    return pl.pallas_call(
        functools.partial(layer_kernel, names),
        out_shape=[jax.ShapeDtypeStruct(shape, dtype) for shape, dtype in outputs.values()],
        in_specs=[pl.BlockSpec(memory_space=pl.ANY)] * len(inputs),
        out_specs=[pl.BlockSpec(memory_space=pl.ANY)] * len(outputs),
        scratch_shapes=list(scratch.values()),
        compiler_params=pltpu.CompilerParams(collective_id=0, has_side_effects=True, vmem_limit_bytes=63 * 2**20),
        name="layer",
    )(*inputs.values())


def place_kernel(ids, first, second, third, out_i, ig_i, out_o, ig_o, ae_o, al_o, oe_o, ol_o, me_o, ml_o, le_o, ll_o):
    a = pl.program_id(0)
    outs = (ae_o, al_o, oe_o, ol_o, me_o, ml_o, le_o, ll_o)

    @pl.when(a == 0)
    def _():
        out_o[...] = out_i[...]
        ig_o[...] = ig_i[...].astype(F32)

    for ref in outs:
        ref[...] = jnp.zeros(ref.shape, F32)
    for group in range(4):
        ident = ids[group % 2, 2 + group // 2, 0]

        @pl.when(ident == a)
        def _(group=group):
            for m in range(8):
                at = slice(m * 128, (m + 1) * 128)
                for i in range(3):
                    al_o[i, 0, :, at] += second[group, m, :, i * 128 : (i + 1) * 128].astype(F32)
                    ae_o[i, 0, :, at] += third[group, m, :, i * 128 : (i + 1) * 128].astype(F32)
                oe_o[0, :, at] += second[group, m, :, 384:512].astype(F32)
                ol_o[0, :, at] += second[group, m, :, 512:640].astype(F32)
                for i in range(2):
                    me_o[i, 0, :, at] += second[group, m, :, 640 + i * 128 : 768 + i * 128].astype(F32)
                ll_o[0, :, at] += third[group, m, :, 384:512].astype(F32)
                for q in range(4):
                    fb = ((m // 4) * 16 + (q // 2) * 8 + (m // 2 % 2) * 4 + (q % 2) * 2 + m % 2) * 128
                    for i in range(2):
                        ml_o[i, 0, :, fb : fb + 128] += first[group, m, :, i * 512 + q * 128 : i * 512 + (q + 1) * 128].astype(F32)
                    le_o[0, :, fb : fb + 128] += first[group, m, :, 1024 + q * 128 : 1024 + (q + 1) * 128].astype(F32)


def place_call(meta, *inputs):
    def whole(shape):
        return pl.BlockSpec(shape, lambda a, ids: (0,) * len(shape))

    def four(n, width):
        return pl.BlockSpec((n, 1, 16, width), lambda a, ids: (0, a, 0, 0))

    def three(width):
        return pl.BlockSpec((1, 16, width), lambda a, ids: (a, 0, 0))

    shapes = ((3, 8, 16, 1024), (3, 8, 16, 1024), (8, 16, 1024), (8, 16, 1024), (2, 8, 16, 1024), (2, 8, 16, 4096), (8, 16, 4096), (8, 16, 1024))
    return pl.pallas_call(
        place_kernel,
        out_shape=[jax.ShapeDtypeStruct((2, 64, 1024), BF), jax.ShapeDtypeStruct((2, 64, 1024), F32)]
        + [jax.ShapeDtypeStruct(shape, F32) for shape in shapes],
        grid_spec=pltpu.PrefetchScalarGridSpec(
            num_scalar_prefetch=1,
            grid=(8,),
            in_specs=[whole(array.shape) for array in inputs],
            out_specs=[whole((2, 64, 1024)), whole((2, 64, 1024)), four(3, 1024), four(3, 1024), three(1024), three(1024),
                       four(2, 1024), four(2, 4096), three(4096), three(1024)],
        ),
        compiler_params=pltpu.CompilerParams(vmem_limit_bytes=63 * 2**20),
        name="place",
    )(meta, *inputs)


def grouped(
    inputs, segment_ids, adapter_ids, w_query, w_key, w_value, w_out, w_gate, w_up, w_down, gain_attn, gain_ffn,
    attn_enter, attn_leave, out_enter, out_leave, mlp_enter, mlp_leave, last_enter, last_leave, out_grad,
):
    flat = lax.axis_index("dp") * 16 + lax.axis_index("ctx")
    seg = segment_ids[:, 0].reshape(2, 2, 2, 2, 2, 64)
    seg = jnp.transpose(seg, (0, 3, 2, 4, 1, 5)).reshape(2, 1024)
    ids = jnp.broadcast_to(adapter_ids, (2, 1024))
    meta = jnp.concatenate([seg, ids, jnp.zeros((4, 1024), jnp.int32)], axis=0)
    at = lax.broadcasted_iota(jnp.int32, (32, 32), 0) == flat
    gains = jnp.concatenate(
        [jnp.where(at, gain.astype(F32)[None, :], 0.0).reshape(8, 128) for gain in (gain_attn, gain_ffn)], axis=0
    )
    out, ig, *shares, meta_all = layer_call(
        x_h=inputs[:, 0], og_h=out_grad[:, 0], meta_h=meta, gain_h=gains, wq_h=w_query, wk_h=w_key, wv_h=w_value, wo_h=w_out,
        wg_h=w_gate, wu_h=w_up, wd_h=w_down, ae_h=attn_enter, al_h=attn_leave, oe_h=out_enter, ol_h=out_leave,
        me_h=mlp_enter, ml_h=mlp_leave, le_h=last_enter, ll_h=last_leave,
    )
    out, ig, *grads = place_call(meta_all, *shares, out, ig)
    return (out[:, None], ig[:, None], *grads)


def solution(mesh):
    def chosen(*args):
        sizes = (mesh.shape["dp"], mesh.shape["ctx"], *args[0].shape)
        return (grouped if sizes == (2, 16, 2, 1, 64, 1024) else per_device)(*args)

    return jax.shard_map(
        chosen,
        mesh=mesh,
        in_specs=(
            P(None, "dp", "ctx", None),
            P(None, "dp", None),
            P(None, "dp"),
            P(("dp", "ctx"), None),
            P(("dp", "ctx"), None),
            P(("dp", "ctx"), None),
            P(("dp", "ctx"), None),
            P(("dp", "ctx"), None),
            P(("dp", "ctx"), None),
            P(("dp", "ctx"), None),
            P(("dp", "ctx")),
            P(("dp", "ctx")),
            P(),
            P(),
            P(),
            P(),
            P(),
            P(),
            P(),
            P(),
            P(None, "dp", "ctx", None),
        ),
        out_specs=(
            P(None, "dp", "ctx", None),
            P(None, "dp", "ctx", None),
            P(),
            P(),
            P(),
            P(),
            P(),
            P(),
            P(),
            P(),
        ),
        check_vma=False,
    )
```

```python
import functools
import types

import jax
import jax.numpy as jnp
from jax import lax
from jax.experimental import pallas as pl
from jax.experimental.pallas import tpu as pltpu
from jax.sharding import PartitionSpec as P

H = 16
HD = 64


EPS = 1e-05
NEG = -1000000000.0
SCALE = 0.5


def rms_norm(rows, gain):
    inverse = lax.rsqrt(jnp.mean(rows * rows, axis=-1, keepdims=True) + EPS)
    return (rows * inverse * gain, inverse)


def norm_back(rows, inverse, gain, grad):
    weighted = grad * gain
    return inverse * weighted - rows * inverse**3 * jnp.mean(
        rows * weighted, axis=-1, keepdims=True
    )


def project(rows, weight, enter, leave):
    direct = jnp.einsum("sci,io->sco", rows, weight, preferred_element_type=jnp.float32)
    inner = jnp.einsum("sci,sri->scr", rows, enter, preferred_element_type=jnp.float32).astype(
        jnp.bfloat16
    )
    return (
        direct
        + SCALE * jnp.einsum("scr,sro->sco", inner, leave, preferred_element_type=jnp.float32),
        inner,
    )


def project_back(rows, inner, weight, enter, leave, grad):
    inner_grad = (
        SCALE * jnp.einsum("sco,sro->scr", grad, leave, preferred_element_type=jnp.float32)
    ).astype(jnp.bfloat16)
    rows_grad = jnp.einsum("sco,io->sci", grad, weight, preferred_element_type=jnp.float32)
    rows_grad = rows_grad + jnp.einsum(
        "scr,sri->sci", inner_grad, enter, preferred_element_type=jnp.float32
    )
    enter_grad = jnp.einsum("scr,sci->sri", inner_grad, rows, preferred_element_type=jnp.float32)
    leave_grad = SCALE * jnp.einsum("scr,sco->sro", inner, grad, preferred_element_type=jnp.float32)
    return (rows_grad, enter_grad, leave_grad)


def masked_scores(query_heads, key_block, seg_query, seg_key):
    seqs = query_heads.shape[0]
    key_heads = key_block.reshape(seqs, -1, H, HD)
    scores = (
        jnp.einsum("sqhd,skhd->shqk", query_heads, key_heads, preferred_element_type=jnp.float32)
        * 0.125
    )
    same = seg_query[:, None, :, None] == seg_key[:, None, None, :]
    return (jnp.where(same, scores, NEG), key_heads)


def forward_block(state, query_heads, seg_query, key_block, value_block, seg_key):
    best, total, accum = state
    seqs = query_heads.shape[0]
    scores, key_heads = masked_scores(query_heads, key_block, seg_query, seg_key)
    value_heads = value_block.reshape(seqs, -1, H, HD)
    new_best = jnp.maximum(best, jnp.max(scores, axis=-1))
    factor = jnp.exp(best - new_best)
    weights = jnp.exp(scores - new_best[..., None])
    total = total * factor + jnp.sum(weights, axis=-1)
    mixed = jnp.einsum(
        "shqk,skhd->sqhd",
        weights.astype(jnp.bfloat16),
        value_heads,
        preferred_element_type=jnp.float32,
    )
    accum = accum * jnp.transpose(factor, (0, 2, 1))[..., None] + mixed
    return (new_best, total, accum)


def attend(query, key, value, seg_rows, my_start):
    seqs, rows, width = query.shape
    query_heads = query.reshape(seqs, rows, H, HD)
    seg_query = lax.dynamic_slice_in_dim(seg_rows, my_start, rows, 1)
    state = (
        jnp.full((seqs, H, rows), -1e30, jnp.float32),
        jnp.zeros((seqs, H, rows), jnp.float32),
        jnp.zeros((seqs, rows, H, HD), jnp.float32),
    )

    def fold(carry, piece, start):
        key_piece, value_piece = piece
        count = key_piece.shape[1]
        block = 512

        def advance(index, inner_state):
            offset = index * block
            key_block = lax.dynamic_slice_in_dim(key_piece, offset, block, 1)
            value_block = lax.dynamic_slice_in_dim(value_piece, offset, block, 1)
            seg_key = lax.dynamic_slice_in_dim(seg_rows, offset, block, 1)
            return forward_block(
                inner_state, query_heads, seg_query, key_block, value_block, seg_key
            )

        return lax.fori_loop(0, count // block, advance, carry)

    best, total, accum = fold(
        state,
        (
            lax.all_gather(key, "ctx", axis=1, tiled=True),
            lax.all_gather(value, "ctx", axis=1, tiled=True),
        ),
        jnp.int32(0),
    )
    output = accum / jnp.transpose(total, (0, 2, 1))[..., None]
    return (output, best + jnp.log(total))


def block_grads(
    query_heads, grad_heads, log_total, delta, seg_query, key_block, value_block, seg_key
):
    seqs = query_heads.shape[0]
    scores, key_heads = masked_scores(query_heads, key_block, seg_query, seg_key)
    value_heads = value_block.reshape(seqs, -1, H, HD)
    probs = jnp.exp(scores - log_total[..., None])
    value_part = jnp.einsum(
        "shqk,sqhd->skhd",
        probs.astype(jnp.bfloat16),
        grad_heads,
        preferred_element_type=jnp.float32,
    )
    prob_grad = jnp.einsum(
        "sqhd,skhd->shqk", grad_heads, value_heads, preferred_element_type=jnp.float32
    )
    score_grad = (probs * (prob_grad - delta[..., None])).astype(jnp.bfloat16)
    query_part = 0.125 * jnp.einsum(
        "shqk,skhd->sqhd", score_grad, key_heads, preferred_element_type=jnp.float32
    )
    key_part = 0.125 * jnp.einsum(
        "shqk,sqhd->skhd", score_grad, query_heads, preferred_element_type=jnp.float32
    )
    return (query_part, key_part, value_part)


def attend_back(query, key, value, grad, output, log_total, seg_rows, my_start):
    seqs, rows, width = query.shape
    length = seg_rows.shape[1]
    query_heads = query.reshape(seqs, rows, H, HD)
    grad_heads = grad.reshape(seqs, rows, H, HD)
    seg_query = lax.dynamic_slice_in_dim(seg_rows, my_start, rows, 1)
    delta = jnp.transpose(jnp.sum(grad_heads.astype(jnp.float32) * output, axis=-1), (0, 2, 1))
    state = (
        jnp.zeros((seqs, rows, H, HD), jnp.float32),
        jnp.zeros((seqs, length, width), jnp.float32),
        jnp.zeros((seqs, length, width), jnp.float32),
    )

    def fold(carry, piece, start):
        key_piece, value_piece = piece
        count = key_piece.shape[1]
        block = 512

        def advance(index, inner_state):
            offset = index * block
            key_block = lax.dynamic_slice_in_dim(key_piece, offset, block, 1)
            value_block = lax.dynamic_slice_in_dim(value_piece, offset, block, 1)
            seg_key = lax.dynamic_slice_in_dim(seg_rows, offset, block, 1)
            query_part, key_part, value_part = block_grads(
                query_heads,
                grad_heads,
                log_total,
                delta,
                seg_query,
                key_block,
                value_block,
                seg_key,
            )
            query_grad, key_all, value_all = inner_state
            key_old = lax.dynamic_slice_in_dim(key_all, offset, block, 1)
            key_all = lax.dynamic_update_slice_in_dim(
                key_all, key_old + key_part.reshape(seqs, block, width), offset, 1
            )
            value_old = lax.dynamic_slice_in_dim(value_all, offset, block, 1)
            value_all = lax.dynamic_update_slice_in_dim(
                value_all, value_old + value_part.reshape(seqs, block, width), offset, 1
            )
            return (query_grad + query_part, key_all, value_all)

        return lax.fori_loop(0, count // block, advance, carry)

    folded = fold(
        state,
        (
            lax.all_gather(key, "ctx", axis=1, tiled=True),
            lax.all_gather(value, "ctx", axis=1, tiled=True),
        ),
        jnp.int32(0),
    )
    query_grad = folded[0]
    key_grad, value_grad = (
        lax.psum_scatter(
            folded[1].astype(jnp.bfloat16), "ctx", scatter_dimension=1, tiled=True
        ).astype(jnp.float32),
        lax.psum_scatter(
            folded[2].astype(jnp.bfloat16), "ctx", scatter_dimension=1, tiled=True
        ).astype(jnp.float32),
    )
    return (
        query_grad.reshape(seqs, rows, width).astype(jnp.bfloat16),
        key_grad.astype(jnp.bfloat16),
        value_grad.astype(jnp.bfloat16),
    )


def per_device(
    inputs,
    segment_ids,
    adapter_ids,
    w_query,
    w_key,
    w_value,
    w_out,
    w_gate,
    w_up,
    w_down,
    gain_attn,
    gain_ffn,
    attn_enter,
    attn_leave,
    out_enter,
    out_leave,
    mlp_enter,
    mlp_leave,
    last_enter,
    last_leave,
    out_grad,
):
    micro_count, seqs, rows, width = inputs.shape
    my_start = lax.axis_index("ctx") * rows
    adapter_count = attn_enter.shape[1]
    sum_attn_enter = jnp.zeros(attn_enter.shape, jnp.float32)
    sum_attn_leave = jnp.zeros(attn_leave.shape, jnp.float32)
    sum_out_enter = jnp.zeros(out_enter.shape, jnp.float32)
    sum_out_leave = jnp.zeros(out_leave.shape, jnp.float32)
    sum_mlp_enter = jnp.zeros(mlp_enter.shape, jnp.float32)
    sum_mlp_leave = jnp.zeros(mlp_leave.shape, jnp.float32)
    sum_last_enter = jnp.zeros(last_enter.shape, jnp.float32)
    sum_last_leave = jnp.zeros(last_leave.shape, jnp.float32)
    outputs = []
    gradients = []
    for micro in range(micro_count):
        frozen = (
            lax.all_gather(w_query, ("dp", "ctx"), axis=0, tiled=True),
            lax.all_gather(w_key, ("dp", "ctx"), axis=0, tiled=True),
            lax.all_gather(w_value, ("dp", "ctx"), axis=0, tiled=True),
            lax.all_gather(w_out, ("dp", "ctx"), axis=0, tiled=True),
            lax.all_gather(w_gate, ("dp", "ctx"), axis=0, tiled=True),
            lax.all_gather(w_up, ("dp", "ctx"), axis=0, tiled=True),
            lax.all_gather(w_down, ("dp", "ctx"), axis=0, tiled=True),
            lax.all_gather(gain_attn, ("dp", "ctx"), axis=0, tiled=True),
            lax.all_gather(gain_ffn, ("dp", "ctx"), axis=0, tiled=True),
        )
        query_w, key_w, value_w, out_w, gate_w, up_w, down_w, gain_one, gain_two = frozen
        chosen = adapter_ids[micro]
        attn_in = jnp.take(attn_enter, chosen, axis=1)
        attn_out = jnp.take(attn_leave, chosen, axis=1)
        out_in = jnp.take(out_enter, chosen, axis=0)
        out_out = jnp.take(out_leave, chosen, axis=0)
        mlp_in = jnp.take(mlp_enter, chosen, axis=1)
        mlp_out = jnp.take(mlp_leave, chosen, axis=1)
        last_in = jnp.take(last_enter, chosen, axis=0)
        last_out = jnp.take(last_leave, chosen, axis=0)
        seg_rows = segment_ids[micro]
        start_rows = inputs[micro].astype(jnp.float32)
        normed_f, inverse_one = rms_norm(start_rows, gain_one.astype(jnp.float32))
        normed = normed_f.astype(jnp.bfloat16)
        query_f, query_inner = project(normed, query_w, attn_in[0], attn_out[0])
        key_f, key_inner = project(normed, key_w, attn_in[1], attn_out[1])
        value_f, value_inner = project(normed, value_w, attn_in[2], attn_out[2])
        query = query_f.astype(jnp.bfloat16)
        key = key_f.astype(jnp.bfloat16)
        value = value_f.astype(jnp.bfloat16)
        mixed_f, log_total = attend(query, key, value, seg_rows, my_start)
        mixed = mixed_f.reshape(seqs, rows, width).astype(jnp.bfloat16)
        branch, out_inner = project(mixed, out_w, out_in, out_out)
        middle = start_rows + branch
        normed_two_f, inverse_two = rms_norm(middle, gain_two.astype(jnp.float32))
        normed_two = normed_two_f.astype(jnp.bfloat16)
        gate, gate_inner = project(normed_two, gate_w, mlp_in[0], mlp_out[0])
        upper, up_inner = project(normed_two, up_w, mlp_in[1], mlp_out[1])
        sigma = jax.nn.sigmoid(gate)
        hidden = (gate * sigma * upper).astype(jnp.bfloat16)
        closing, last_inner = project(hidden, down_w, last_in, last_out)
        outputs.append((middle + closing).astype(jnp.bfloat16))
        frozen = (
            lax.all_gather(w_query, ("dp", "ctx"), axis=0, tiled=True),
            lax.all_gather(w_key, ("dp", "ctx"), axis=0, tiled=True),
            lax.all_gather(w_value, ("dp", "ctx"), axis=0, tiled=True),
            lax.all_gather(w_out, ("dp", "ctx"), axis=0, tiled=True),
            lax.all_gather(w_gate, ("dp", "ctx"), axis=0, tiled=True),
            lax.all_gather(w_up, ("dp", "ctx"), axis=0, tiled=True),
            lax.all_gather(w_down, ("dp", "ctx"), axis=0, tiled=True),
            lax.all_gather(gain_attn, ("dp", "ctx"), axis=0, tiled=True),
            lax.all_gather(gain_ffn, ("dp", "ctx"), axis=0, tiled=True),
        )
        query_w, key_w, value_w, out_w, gate_w, up_w, down_w, gain_one, gain_two = frozen
        grad_rows = out_grad[micro].astype(jnp.float32)
        hidden_grad, last_in_grad, last_out_grad = project_back(
            hidden, last_inner, down_w, last_in, last_out, out_grad[micro]
        )
        gate_grad = (hidden_grad * upper * sigma * (1.0 + gate * (1.0 - sigma))).astype(
            jnp.bfloat16
        )
        up_grad = (hidden_grad * gate * sigma).astype(jnp.bfloat16)
        from_gate, gate_in_grad, gate_out_grad = project_back(
            normed_two, gate_inner, gate_w, mlp_in[0], mlp_out[0], gate_grad
        )
        from_up, up_in_grad, up_out_grad = project_back(
            normed_two, up_inner, up_w, mlp_in[1], mlp_out[1], up_grad
        )
        middle_grad = grad_rows + norm_back(
            middle, inverse_two, gain_two.astype(jnp.float32), from_gate + from_up
        )
        mixed_grad_f, out_in_grad, out_out_grad = project_back(
            mixed, out_inner, out_w, out_in, out_out, middle_grad.astype(jnp.bfloat16)
        )
        mixed_grad = mixed_grad_f.astype(jnp.bfloat16)
        query_grad, key_grad, value_grad = attend_back(
            query, key, value, mixed_grad, mixed_f, log_total, seg_rows, my_start
        )
        from_query, query_in_grad, query_out_grad = project_back(
            normed, query_inner, query_w, attn_in[0], attn_out[0], query_grad
        )
        from_key, key_in_grad, key_out_grad = project_back(
            normed, key_inner, key_w, attn_in[1], attn_out[1], key_grad
        )
        from_value, value_in_grad, value_out_grad = project_back(
            normed, value_inner, value_w, attn_in[2], attn_out[2], value_grad
        )
        gradients.append(
            middle_grad
            + norm_back(
                start_rows,
                inverse_one,
                gain_one.astype(jnp.float32),
                from_query + from_key + from_value,
            )
        )
        per_seq = (
            jnp.stack([query_in_grad, key_in_grad, value_in_grad]),
            jnp.stack([query_out_grad, key_out_grad, value_out_grad]),
            out_in_grad,
            out_out_grad,
            jnp.stack([gate_in_grad, up_in_grad]),
            jnp.stack([gate_out_grad, up_out_grad]),
            last_in_grad,
            last_out_grad,
        )
        onehot = (chosen[:, None] == jnp.arange(adapter_count, dtype=jnp.int32)[None, :]).astype(
            jnp.float32
        )
        sum_attn_enter = sum_attn_enter + jnp.einsum("sa,isrd->iard", onehot, per_seq[0])
        sum_attn_leave = sum_attn_leave + jnp.einsum("sa,isrd->iard", onehot, per_seq[1])
        sum_out_enter = sum_out_enter + jnp.einsum("sa,srd->ard", onehot, per_seq[2])
        sum_out_leave = sum_out_leave + jnp.einsum("sa,srd->ard", onehot, per_seq[3])
        sum_mlp_enter = sum_mlp_enter + jnp.einsum("sa,isrd->iard", onehot, per_seq[4])
        sum_mlp_leave = sum_mlp_leave + jnp.einsum("sa,isrf->iarf", onehot, per_seq[5])
        sum_last_enter = sum_last_enter + jnp.einsum("sa,srf->arf", onehot, per_seq[6])
        sum_last_leave = sum_last_leave + jnp.einsum("sa,srd->ard", onehot, per_seq[7])
    totals = (
        sum_attn_enter,
        sum_attn_leave,
        sum_out_enter,
        sum_out_leave,
        sum_mlp_enter,
        sum_mlp_leave,
        sum_last_enter,
        sum_last_leave,
    )
    summed = lax.psum(
        (totals[0], totals[1], totals[2], totals[3], totals[4], totals[5], totals[6], totals[7]),
        ("dp", "ctx"),
    )
    return (
        jnp.stack(outputs),
        jnp.stack(gradients),
        summed[0],
        summed[1],
        summed[2],
        summed[3],
        summed[4],
        summed[5],
        summed[6],
        summed[7],
    )


MESH = pl.DeviceIdType.MESH
BF = jnp.bfloat16
F32 = jnp.float32
SAME = (1, 4, 5)
PEERS = ((0, 1), (0, 4), (0, 5), (1, 0), (1, 1), (1, 4), (1, 5))
ACROSS = ((0, 2), (0, 8), (0, 10))
GREET = PEERS + ACROSS + ((1, 2), (1, 10))
DOUBLE = (8, 4, 1, 2)
FAR = 32
HELD = (0, 8, 4, 12, 1, 9, 5, 13, 2, 10, 6, 14, 3, 11, 7, 15)
WIDTHS = (1536, 896, 512)


def dot(left, right):
    return lax.dot_general(left, right, (((1,), (0,)), ((), ())), preferred_element_type=F32)


def dot_t(left, right):
    return lax.dot_general(left, right, (((1,), (1,)), ((), ())), preferred_element_type=F32)


class Spot:
    def __init__(self, p, x, y, zl, zh):
        self.p, self.x, self.y, self.zl, self.zh = p, x, y, zl, zh

    def flip(self, a, b):
        return Spot(
            1 - self.p if a else self.p,
            1 - self.x if b & 1 else self.x,
            1 - self.y if b & 2 else self.y,
            1 - self.zl if b & 4 else self.zl,
            1 - self.zh if b & 8 else self.zh,
        )

    def device(self):
        return (self.p, self.x + 2 * self.y + 4 * self.zl + 8 * self.zh)

    def member(self):
        return self.p * 4 + self.zl * 2 + self.x

    def group(self):
        return self.zh * 2 + self.y


def here():
    p, c = lax.axis_index("dp"), lax.axis_index("ctx")
    return Spot(p, lax.rem(c, 2), lax.rem(lax.div(c, 2), 2), lax.rem(lax.div(c, 4), 2), lax.div(c, 8))


def part(index, size):
    return pl.ds(pl.multiple_of(index * size, size), size)


def remote(src, dst, ssem, rsem, spot):
    return pltpu.make_async_remote_copy(
        src_ref=src, dst_ref=dst, send_sem=ssem, recv_sem=rsem, device_id=spot.device(), device_id_type=MESH
    )


def pick(raw, mask):
    total = raw[0].astype(F32) * mask(0)
    for a in range(1, raw.shape[0]):
        total = total + raw[a].astype(F32) * mask(a)
    return total


def layer_kernel(names, *refs):
    R = types.SimpleNamespace(**dict(zip(names, refs, strict=True)))
    me = here()
    p, x, y, zl, zh = me.p, me.x, me.y, me.zl, me.zh
    j = me.member()
    own = part(j, 128)
    partner = me.flip(1, 0)
    late = []

    def send(src, dst, ssem, rsem, spot):
        copy = remote(src, dst, ssem, rsem, spot)
        copy.start()
        late.append(copy)

    def arrived(ref, ssem, rsem, spot):
        remote(ref, ref, ssem, rsem, spot).wait_recv()

    place = lax.broadcasted_iota(jnp.int32, (8, 128), 0) * 4 + lax.broadcasted_iota(jnp.int32, (8, 128), 1) // 32
    for i, gain in enumerate((R.g1_h, R.g2_h)):
        wide = jnp.concatenate([gain[...].astype(F32)] * 4, axis=1)
        R.gl[pl.ds(8 * i, 8), :] = jnp.where(place == p * 16 + me.device()[1], jnp.broadcast_to(wide, (8, 128)), 0.0)
    for micro in range(2):
        seg = R.seg_h[micro]
        seg = [seg[:, c * 64 : (c + 1) * 64] for c in (b + a for a in (0, 1, 4, 5, 2, 3, 6, 7) for b in (0, 8))]
        R.own[pl.ds(micro, 1), :] = jnp.concatenate(seg, axis=1)
        R.own[pl.ds(2 + micro, 1), :] = jnp.broadcast_to(R.ids_h[:, micro : micro + 1], (1, 1024))
    R.own[pl.ds(4, 4), :] = jnp.zeros((4, 1024), jnp.int32)

    barrier = pltpu.get_barrier_semaphore()
    for a, b in GREET:
        pl.semaphore_signal(barrier, inc=1, device_id=me.flip(a, b).device(), device_id_type=MESH)
    pl.semaphore_wait(barrier, len(GREET))

    def reshard(src, dst, ssem, rsem):
        rows = pl.ds(pl.multiple_of((y * 4 + zl * 2 + x) * 128 + zh * 64, 64), 64)

        @pl.when(p == y)
        def _():
            pltpu.make_async_copy(src.at[zh], dst.at[rows], rsem.at[0]).start()
            remote(src.at[1 - zh], dst.at[rows], ssem.at[1], rsem.at[1], me.flip(0, 8)).start()

        @pl.when(p != y)
        def _():
            remote(src.at[zh], dst.at[rows], ssem.at[0], rsem.at[0], me.flip(1, 2)).start()
            remote(src.at[1 - zh], dst.at[rows], ssem.at[1], rsem.at[1], me.flip(1, 10)).start()

    def reshard_wait(dst, rsem):
        for k, t in enumerate((zh, 1 - zh)):
            rows = pl.ds(pl.multiple_of(j * 128 + t * 64, 64), 64)
            pltpu.make_async_copy(dst.at[rows], dst.at[rows], rsem.at[k]).wait()

    def reshard_sent(src, ssem):
        @pl.when(p != y)
        def _():
            remote(src.at[zh], src.at[zh], ssem.at[0], ssem.at[0], me.flip(1, 2)).wait_send()

        remote(src.at[zh], src.at[zh], ssem.at[1], ssem.at[1], me.flip(0, 8)).wait_send()

    def spread(ref, ssem, rsem):
        mine = ref.at[own]
        for k, spot in enumerate((me.flip(0, 1), me.flip(0, 4), partner)):
            send(mine, mine, ssem.at[k], rsem.at[k], spot)

    def rows_at(ref, spot, k):
        first, rows = ((0, FAR), (FAR, 128 - FAR))[k]
        return ref.at[pl.ds(pl.multiple_of(spot.member() * 128 + first, 32), rows)]

    def spread_on(ref, ssem, rsem):
        for k, (came, on) in enumerate(((1, 4), (4, 1))):
            spot = me.flip(0, came)
            got, half = ref.at[part(spot.member(), 128)], rows_at(ref, spot, k)
            arrived(got, ssem.at[k], rsem.at[k], spot)
            send(half, half, ssem.at[3 + k], rsem.at[3 + k], me.flip(0, on))
            send(got, got, ssem.at[5 + k], rsem.at[5 + k], partner)

    def spread_far(ref, ssem, rsem):
        for k, on in enumerate((4, 1)):
            half = rows_at(ref, me.flip(0, 5), k)
            arrived(half, ssem.at[3 + k], rsem.at[3 + k], me.flip(0, on))
            send(half, half, ssem.at[7 + k], rsem.at[7 + k], partner)

    def spread_end(ref, ssem, rsem):
        arrived(ref.at[part(partner.member(), 128)], ssem.at[2], rsem.at[2], partner)
        for k, came in enumerate((1, 4)):
            arrived(ref.at[part(me.flip(1, came).member(), 128)], ssem.at[5 + k], rsem.at[5 + k], partner)
            arrived(rows_at(ref, me.flip(1, 5), k), ssem.at[7 + k], rsem.at[7 + k], partner)

    def share(view, ssem, rsem):
        mine = view(me)
        for k, b in enumerate(SAME):
            send(mine, mine, ssem.at[k], rsem.at[k], me.flip(0, b))
        send(mine, mine, ssem.at[3], rsem.at[3], partner)

    def share_on(view, ssem, rsem):
        for k, b in enumerate(SAME):
            got = view(me.flip(0, b))
            arrived(got, ssem.at[k], rsem.at[k], me.flip(0, b))
            send(got, got, ssem.at[4 + k], rsem.at[4 + k], partner)

    def share_end(view, ssem, rsem):
        arrived(view(partner), ssem.at[3], rsem.at[3], partner)
        for k, b in enumerate(SAME):
            arrived(view(me.flip(1, b)), ssem.at[4 + k], rsem.at[4 + k], partner)

    def double(view, ssem, rsem, step):
        for k in range(2**step):
            ref, n = view(me.flip(0, HELD[k])), 2**step - 1 + k
            send(ref, ref, ssem.at[n], rsem.at[n], me.flip(0, DOUBLE[step]))
        if step == 0:
            send(view(me), view(me), ssem.at[15], rsem.at[15], partner)

    def double_on(view, ssem, rsem, step):
        for k in range(2**step):
            ref, n = view(me.flip(0, HELD[2**step + k])), 2**step - 1 + k
            arrived(ref, ssem.at[n], rsem.at[n], me.flip(0, DOUBLE[step]))
            send(ref, ref, ssem.at[16 + n], rsem.at[16 + n], partner)
        if step < 3:
            double(view, ssem, rsem, step + 1)

    def double_end(view, ssem, rsem):
        for k in range(16):
            arrived(view(me.flip(1, HELD[k])), ssem.at[15 + k], rsem.at[15 + k], partner)

    def across(views, ssem, rsem, axis, pieces=(0,)):
        for k in pieces:
            view = views(me)[k]
            send(view, view, ssem.at[axis, k], rsem.at[axis, k], me.flip(0, (8, 2)[axis]))

    def across_on(views, ssem, rsem, pieces=(0,)):
        for k in pieces:
            view = views(me.flip(0, 8))[k]
            arrived(view, ssem.at[0, k], rsem.at[0, k], me.flip(0, 8))
            send(view, view, ssem.at[2, k], rsem.at[2, k], me.flip(0, 2))

    def across_end(views, ssem, rsem):
        for k, view in enumerate(views(me.flip(0, 2))):
            arrived(view, ssem.at[1, k], rsem.at[1, k], me.flip(0, 2))
        for k, view in enumerate(views(me.flip(0, 10))):
            arrived(view, ssem.at[2, k], rsem.at[2, k], me.flip(0, 2))

    def row_views(ref, columns):
        def views(spot):
            return [
                ref.at[pl.ds(pl.multiple_of(pp * 512 + spot.zh * 256 + zz * 128 + spot.y * 64, 64), 64), pl.ds(0, columns)]
                for pp in range(2)
                for zz in range(2)
            ]

        return views

    qkv_views, gu_views = row_views(R.qkvb, 384), row_views(R.gub, 1024)

    def down_views(spot):
        return [R.db.at[part(spot.group(), 128), pl.ds(0, 1024)]]

    def out_view(spot):
        k_row = (spot.p * 16 + spot.zh * 8 + spot.zl * 4 + spot.y * 2 + spot.x) * 32
        return R.ob.at[pl.ds(pl.multiple_of(k_row, 32), 32), pl.ds(0, 1024)]

    def gain_views(spot):
        return [R.gs.at[spot.group()]]

    my_row = pl.ds(pl.multiple_of((p * 16 + zh * 8 + zl * 4 + y * 2 + x) * 32, 32), 32)

    raws = (
        (R.ae, R.ae_h), (R.al, R.al_h.at[:, :, :, own]), (R.oe, R.oe_h), (R.ol, R.ol_h), (R.me, R.me_h), (R.ll, R.ll_h),
    )
    locals_ = []
    for k, (dst, src) in enumerate(raws):
        locals_.append(pltpu.make_async_copy(src, dst, R.la.at[k]))
    for q in range(4):
        fb = part(p * 16 + (q // 2) * 8 + zl * 4 + (q % 2) * 2 + x, 128)
        locals_.append(pltpu.make_async_copy(R.ml_h.at[:, :, :, fb], R.ml.at[:, :, :, pl.ds(q * 128, 128)], R.la.at[8 + q]))
        locals_.append(pltpu.make_async_copy(R.le_h.at[:, :, fb], R.le.at[:, :, pl.ds(q * 128, 128)], R.la.at[12 + q]))

    reshard(R.x_h, R.xf, R.xs, R.xr)

    gain_mine = R.gs.at[me.group(), j]
    gain_local = pltpu.make_async_copy(R.gl, gain_mine, R.g1r.at[7])
    gain_local.start()
    for k, (a, b) in enumerate(PEERS):
        send(R.gl, gain_mine, R.g1s.at[k], R.g1r.at[k], me.flip(a, b))

    def columns_to(spot, k, start):
        t = spot.member()
        for i, src in enumerate((R.wq_h, R.wk_h, R.wv_h)):
            start(src.at[:, part(t, 128)], R.qkvb.at[my_row, pl.ds(i * 128, 128)], R.w1qs.at[k, i], R.w1qr.at[k, i])

    def mlp_columns_to(spot, k, start):
        for i, src in enumerate((R.wg_h, R.wu_h)):
            for q in range(4):
                fb = part(spot.p * 16 + (q // 2) * 8 + spot.zl * 4 + (q % 2) * 2 + spot.x, 128)
                at = (k, i * 4 + q)
                start(src.at[:, fb], R.gub.at[my_row, pl.ds(i * 512 + q * 128, 128)], R.w1ms.at[*at], R.w1mr.at[*at])

    def start_remote(spot):
        return lambda src, dst, ssem, rsem: send(src, dst, ssem, rsem, spot)

    def start_local(src, dst, ssem, rsem):
        pltpu.make_async_copy(src, dst, rsem).start()

    for k, (a, b) in enumerate(PEERS):
        columns_to(me.flip(a, b), k, start_remote(me.flip(a, b)))
    columns_to(me, 7, start_local)

    meta_local = pltpu.make_async_copy(R.own, R.meta.at[p], R.mr.at[1])
    meta_local.start()
    send(R.own, R.meta.at[p], R.ms.at[0], R.mr.at[0], partner)
    for copy in locals_:
        copy.start()

    out_local = pltpu.make_async_copy(R.wo_h, out_view(me), R.wor.at[31])
    out_local.start()
    send(R.wo_h, out_view(me), R.wos.at[0], R.wor.at[0], me.flip(0, DOUBLE[0]))
    send(R.wo_h, out_view(me), R.wos.at[15], R.wor.at[15], partner)
    for k, (a, b) in enumerate(PEERS):
        mlp_columns_to(me.flip(a, b), k, start_remote(me.flip(a, b)))
    mlp_columns_to(me, 7, start_local)

    reshard_wait(R.xf, R.xr)
    spread(R.xf, R.axs, R.axr)

    def rows_of(spot):
        return pl.ds(pl.multiple_of((spot.p * 16 + spot.zh * 8 + spot.zl * 4 + spot.y * 2 + spot.x) * 32, 32), 32)

    def first_end(target, rsem, pieces):
        for k, (a, b) in enumerate(PEERS + ((0, 0),)):
            rows = rows_of(me.flip(a, b))
            for i in range(pieces):
                ref = target.at[rows, pl.ds(i * 128, 128)]
                pltpu.make_async_copy(ref, ref, rsem.at[k, i]).wait()

    first_end(R.qkvb, R.w1qr, 3)
    across(qkv_views, R.w2qs, R.w2qr, 0, range(4))
    across(qkv_views, R.w2qs, R.w2qr, 1, range(4))
    reshard(R.og_h, R.ogf, R.os, R.ors)
    for k, (a, b) in enumerate(PEERS):
        spot = me.flip(a, b)
        arrived(R.gs.at[me.group(), spot.member()], R.g1s.at[k], R.g1r.at[k], spot)
    gain_local.wait()
    across(gain_views, R.g2s, R.g2r, 0)
    across(gain_views, R.g2s, R.g2r, 1)
    spread_on(R.xf, R.axs, R.axr)
    out_local.wait()
    double_on(out_view, R.wos, R.wor, 0)
    across_on(qkv_views, R.w2qs, R.w2qr, range(4))
    first_end(R.gub, R.w1mr, 8)
    across(gu_views, R.w2ms, R.w2mr, 1, range(4))
    across(gu_views, R.w2ms, R.w2mr, 0, (0,))
    down_mine = down_views(me)[0]
    down_local = pltpu.make_async_copy(R.wd_h, down_mine, R.wdr.at[3, 0])
    down_local.start()
    across_on(gain_views, R.g2s, R.g2r)

    pltpu.make_async_copy(R.own, R.meta.at[p], R.mr.at[1]).wait()
    arrived(R.meta.at[1 - p], R.ms.at[0], R.mr.at[0], partner)
    for copy in locals_:
        copy.wait()
    ids = R.meta[y, pl.ds(2 + zh, 1), :]

    def mask(width):
        return lambda a: (ids[:, 0:width] == a).astype(F32)

    def enter_columns(items):
        rows = [pick(item, mask(item.shape[-1])) for item in items]
        width = rows[0].shape[-1]
        rows.append(jnp.zeros((128 - 16 * len(rows), width), F32))
        return jnp.transpose(jnp.concatenate(rows, axis=0)).astype(BF)

    def leave_rows(ref, first, items):
        ref[pl.ds(first, 128), :] = jnp.zeros((128, ref.shape[1]), BF)
        column = 0
        for i, item in enumerate(items):
            width = item.shape[-1]
            ref[pl.ds(first + 16 * i, 16), pl.ds(column, width)] = (SCALE * pick(item, mask(width))).astype(BF)
            column += width

    R.qkvb[pl.ds(0, 1024), pl.ds(384, 128)] = enter_columns([R.ae.at[i] for i in range(3)])
    leave_rows(R.qkvb, 1024, [R.al.at[i] for i in range(3)])
    R.ob[pl.ds(0, 1024), pl.ds(1024, 128)] = enter_columns([R.oe])
    leave_rows(R.ob, 1024, [R.ol])
    R.gub[pl.ds(0, 1024), pl.ds(1024, 128)] = enter_columns([R.me.at[i] for i in range(2)])
    leave_rows(R.gub, 1024, [R.ml.at[i] for i in range(2)])
    R.db[pl.ds(0, 512), pl.ds(1024, 128)] = enter_columns([R.le])
    leave_rows(R.db, 512, [R.ll])

    seg_row = R.meta[y, pl.ds(zh, 1), :]
    R.segc[...] = jnp.transpose(jnp.broadcast_to(seg_row.astype(F32), (128, 1024)))

    across(gu_views, R.w2ms, R.w2mr, 0, (1,))
    double_on(out_view, R.wos, R.wor, 1)
    across_end(gain_views, R.g2s, R.g2r)
    gains = jnp.sum(jnp.sum(R.gs[...], axis=0), axis=0)
    gain_one = jnp.concatenate([gains[i : i + 1] for i in range(8)], axis=1)
    gain_two = jnp.concatenate([gains[i : i + 1] for i in range(8, 16)], axis=1)

    spread_far(R.xf, R.axs, R.axr)
    spread_end(R.xf, R.axs, R.axr)
    reshard_wait(R.ogf, R.ors)
    spread(R.ogf, R.aos, R.aor)
    across(gu_views, R.w2ms, R.w2mr, 0, (2,))
    double_on(out_view, R.wos, R.wor, 2)
    across_end(qkv_views, R.w2qs, R.w2qr)

    def qkv_tile(t, carry):
        rows = part(t, 256)
        held = R.xf[rows, :].astype(F32)
        inverse = lax.rsqrt(jnp.mean(held * held, axis=-1, keepdims=True) + EPS)
        normed = (held * inverse * gain_one).astype(BF)
        both = dot(normed, R.qkvb[0:1024, :])
        inner = both[:, 384:512]
        qkv = both[:, 0:384] + dot(inner.astype(BF), R.qkvb[1024:1152, 0:384])
        R.n1c[rows, :] = (R.xf[rows, own].astype(F32) * inverse * R.g1v[:, own]).astype(BF)
        R.r1t[:, rows] = jnp.transpose(inner).astype(BF)
        R.qb[rows, :] = (qkv[:, 0:128].astype(BF).astype(F32) * 0.125).astype(BF)
        R.kb[rows, :] = qkv[:, 128:256].astype(BF)
        R.vb[rows, :] = qkv[:, 256:384].astype(BF)
        R.kt[:, rows] = jnp.transpose(qkv[:, 128:256]).astype(BF)
        R.vt[:, rows] = jnp.transpose(qkv[:, 256:384]).astype(BF)
        return carry

    R.g1v[...] = gain_one
    lax.fori_loop(0, 4, qkv_tile, 0)

    across(gu_views, R.w2ms, R.w2mr, 0, (3,))

    head_of = lax.broadcasted_iota(jnp.int32, (256, 128), 1) // HD

    def attend_tile(t, carry):
        rows = part(t, 256)
        queries = R.qb[rows, :]
        same = R.segc[:, 0:1] == R.meta[y, pl.ds(zh, 1), rows].astype(F32)
        mixed = []
        for h in range(2):
            mine = jnp.where(head_of == h, queries.astype(F32), 0.0).astype(BF)
            scores = jnp.where(same, dot_t(R.kb[...], mine), NEG)
            weights = jnp.exp(scores - jnp.max(scores, axis=0, keepdims=True))
            probs = (weights * (1.0 / jnp.sum(weights, axis=0, keepdims=True))).astype(BF)
            R.pr[2 * t + h] = probs
            mixed.append(dot(R.vt[h * HD : (h + 1) * HD, :], probs))
        mixed = jnp.concatenate(mixed, axis=0)
        R.att[t] = mixed
        R.ath[rows, :] = jnp.transpose(mixed).astype(BF)
        return carry

    lax.fori_loop(0, 4, attend_tile, 0)

    for k, (a, b) in enumerate(PEERS):
        spot = me.flip(a, b)
        send(R.ath.at[part(spot.member(), 128)], R.ato.at[:, own], R.a1s.at[k], R.a1r.at[k], spot)
    mine_local = pltpu.make_async_copy(R.ath.at[own], R.ato.at[:, own], R.a1r.at[7])
    mine_local.start()

    send(R.wd_h, down_mine, R.wds.at[0, 0], R.wdr.at[0, 0], me.flip(0, 8))
    send(R.wd_h, down_mine, R.wds.at[1, 0], R.wdr.at[1, 0], me.flip(0, 2))
    spread_on(R.ogf, R.aos, R.aor)
    across_on(gu_views, R.w2ms, R.w2mr, (0, 1))
    mine_local.wait()
    for k, (a, b) in enumerate(PEERS):
        spot = me.flip(a, b)
        arrived(R.ato.at[:, part(spot.member(), 128)], R.a1s.at[k], R.a1r.at[k], spot)

    double_on(out_view, R.wos, R.wor, 3)
    double_end(out_view, R.wos, R.wor)
    start_rows = R.xf[own, :].astype(F32)
    both = dot(R.ato[...], R.ob[0:1024, :])
    out_inner = both[:, 1024:1152]
    middle = start_rows + both[:, 0:1024] + dot(out_inner.astype(BF), R.ob[1024:1152, 0:1024])
    R.mid[...] = middle
    inverse = lax.rsqrt(jnp.mean(middle * middle, axis=-1, keepdims=True) + EPS)
    R.n2f[own, :] = (middle * inverse * gain_two).astype(BF)
    R.rot[...] = jnp.transpose(out_inner).astype(BF)
    spread(R.n2f, R.ans, R.anr)

    down_local.wait()
    across_on(gu_views, R.w2ms, R.w2mr, (2, 3))
    across_on(down_views, R.wds, R.wdr)
    spread_far(R.ogf, R.aos, R.aor)
    spread_on(R.n2f, R.ans, R.anr)
    spread_far(R.n2f, R.ans, R.anr)
    spread_end(R.n2f, R.ans, R.anr)
    across_end(gu_views, R.w2ms, R.w2mr)
    R.cml[...] = jnp.zeros((128, 1024), F32)
    R.cle[...] = jnp.zeros((128, 512), F32)

    def order(i):
        return part(lax.rem((1 - p) * 2 + i, 4), 256)

    def pair_tile(i, carry):
        rows = order(i)
        both = dot(R.n2f[rows, :], R.gub[0:1024, :])
        inner = both[:, 1024:1152]
        pair = both[:, 0:1024] + dot(inner.astype(BF), R.gub[1024:1152, 0:1024])
        gate, upper = pair[:, 0:512], pair[:, 512:1024]
        R.pair[rows, :] = pair
        R.hid[rows, :] = (gate * jax.nn.sigmoid(gate) * upper).astype(BF)
        R.r2t[:, rows] = jnp.transpose(inner).astype(BF)
        return carry

    def down_tile(i, carry):
        rows = order(i)
        R.zd[rows, :] = dot(R.hid[rows, :], R.db[0:512, :]).astype(BF)
        return carry

    def mlp_back_tile(i, carry):
        rows = order(i)
        gate, upper = R.pair[rows, 0:512], R.pair[rows, 512:1024]
        sigma = jax.nn.sigmoid(gate)
        back = dot_t(R.ogf[rows, :], R.db[:, 0:1024])
        inner_back = back[:, 512:640]
        hidden_grad = back[:, 0:512] + dot_t(inner_back.astype(BF), R.db[0:512, 1024:1152])
        gate_grad = (hidden_grad * upper * sigma * (1.0 + gate * (1.0 - sigma))).astype(BF)
        up_grad = (hidden_grad * gate * sigma).astype(BF)
        pair_grad = jnp.concatenate([gate_grad, up_grad], axis=1)
        R.zn[rows, :] = dot_t(pair_grad, R.gub[:, 0:1024]).astype(BF)
        R.cml[...] += dot(R.r2t[:, rows], pair_grad)
        R.cle[...] += dot(jnp.transpose(inner_back).astype(BF), R.hid[rows, :])
        return carry

    def pair_send(parts, k):
        send(parts.at[part(1 - p, 512)], R.rp.at[k], R.rps.at[k], R.rpr.at[k], partner)

    def chip_send(parts, k):
        arrived(R.rp.at[k], R.rps.at[k], R.rpr.at[k], partner)

        def add(i, carry):
            rows = part(i, 128)
            R.rc[k, rows, :] = (
                parts[part(p * 4 + i, 128), :].astype(F32) + R.rp[k, rows, :].astype(F32)
            ).astype(BF)
            return carry

        lax.fori_loop(0, 4, add, 0)
        for i, b in enumerate(SAME):
            spot = me.flip(0, b)
            send(R.rc.at[k, part(spot.zl * 2 + spot.x, 128)], R.rr.at[k, i], R.rrs.at[k, i], R.rrr.at[k, i], spot)

    def summed(parts, k):
        for i, b in enumerate(SAME):
            arrived(R.rr.at[k, i], R.rrs.at[k, i], R.rrr.at[k, i], me.flip(0, b))
        total = parts[own, :].astype(F32) + R.rp[k, part(zl * 2 + x, 128), :].astype(F32)
        for i in range(3):
            total = total + R.rr[k, i].astype(F32)
        return total

    lax.fori_loop(0, 4, pair_tile, 0)
    across_end(down_views, R.wds, R.wdr)
    lax.fori_loop(0, 2, down_tile, 0)
    pair_send(R.zd, 1)
    lax.fori_loop(2, 4, down_tile, 0)
    spread_end(R.ogf, R.aos, R.aor)
    chip_send(R.zd, 1)
    lax.fori_loop(0, 2, mlp_back_tile, 0)
    pair_send(R.zn, 0)
    lax.fori_loop(2, 4, mlp_back_tile, 0)
    chip_send(R.zn, 0)
    for i in range(2):
        R.da[:, pl.ds(i * 512, 512)] = (SCALE * R.cml[i * 16 : (i + 1) * 16, i * 512 : (i + 1) * 512]).astype(BF)
    R.da[:, pl.ds(1024, 512)] = R.cle[0:16, :].astype(BF)

    def first_view(spot):
        return R.ga_o.at[spot.group(), spot.member()]

    def second_view(spot):
        return R.gb_o.at[spot.group(), spot.member()]

    def third_view(spot):
        return R.gc_o.at[spot.group(), spot.member()]

    first_local = pltpu.make_async_copy(R.da, first_view(me), R.gar.at[31])
    first_local.start()
    first_local.wait()
    double(first_view, R.gas, R.gar, 0)

    own_grad = R.ogf[own, :].astype(F32)
    total = summed(R.zn, 0)
    inner_back = total[:, 1024:1152]
    normed_grad = total[:, 0:1024] + dot_t(inner_back.astype(BF), R.gub[0:1024, 1024:1152])
    middle = R.mid[...]
    inverse = lax.rsqrt(jnp.mean(middle * middle, axis=-1, keepdims=True) + EPS)
    middle_grad = own_grad + norm_back(middle, inverse, gain_two, normed_grad)
    R.mg[...] = middle_grad
    rounded = middle_grad.astype(BF)
    both = dot_t(rounded, R.ob[:, 0:1024])
    out_back = both[:, 1024:1152]
    R.gao[...] = (both[:, 0:1024] + dot_t(out_back.astype(BF), R.ob[0:1024, 1024:1152])).astype(BF)
    for k, (a, b) in enumerate(PEERS):
        spot = me.flip(a, b)
        send(R.gao.at[:, part(spot.member(), 128)], R.gah.at[own], R.a2s.at[k], R.a2r.at[k], spot)
    mine_local = pltpu.make_async_copy(R.gao.at[:, own], R.gah.at[own], R.a2r.at[7])
    mine_local.start()
    R.ib[0, own, :] = (inner_back + pltpu.roll(out_back, 32, 1)).astype(BF)

    def rank_view(i):
        return lambda spot: R.ib.at[i, part(spot.member(), 128)]

    share(rank_view(0), R.ibs.at[0], R.ibr.at[0])
    out_leave = (SCALE * dot(R.rot[...], rounded))[0:16].astype(BF)
    for i in range(8):
        R.gp[i] = out_leave[:, i * 128 : (i + 1) * 128]
    for k, (a, b) in enumerate(PEERS):
        spot = me.flip(a, b)
        send(R.gp.at[spot.member()], R.gr.at[k], R.gps.at[k], R.gpr.at[k], spot)
    def give_back(src, dst, ssem, rsem):
        spot_same, spot_other = part(zh, 64), part(1 - zh, 64)

        @pl.when(p == y)
        def _():
            pltpu.make_async_copy(src.at[spot_same], dst.at[zh], rsem.at[0]).start()
            remote(src.at[spot_other], dst.at[zh], ssem.at[1], rsem.at[1], me.flip(0, 8)).start()

        @pl.when(p != y)
        def _():
            remote(src.at[spot_same], dst.at[zh], ssem.at[0], rsem.at[0], me.flip(1, 2)).start()
            remote(src.at[spot_other], dst.at[zh], ssem.at[1], rsem.at[1], me.flip(1, 10)).start()

    def give_back_wait(src, dst, ssem, rsem):
        pltpu.make_async_copy(dst.at[zh], dst.at[zh], rsem.at[0]).wait()
        pltpu.make_async_copy(dst.at[1 - zh], dst.at[1 - zh], rsem.at[1]).wait()

        @pl.when(p != y)
        def _():
            remote(src.at[part(zh, 64)], src.at[part(zh, 64)], ssem.at[0], rsem.at[0], me.flip(1, 2)).wait_send()

        remote(src.at[part(zh, 64)], src.at[part(zh, 64)], ssem.at[1], rsem.at[1], me.flip(0, 8)).wait_send()

    total = summed(R.zd, 1)
    last_inner = total[:, 1024:1152]
    R.ib[1, own, :] = last_inner.astype(BF)
    share(rank_view(1), R.ibs.at[1], R.ibr.at[1])
    R.outv[...] = (R.mid[...] + total[:, 0:1024] + dot(last_inner.astype(BF), R.db[512:640, 0:1024])).astype(BF)

    give_back(R.outv, R.out_o, R.bos, R.bor)
    double_on(first_view, R.gas, R.gar, 0)
    mine_local.wait()
    for k, (a, b) in enumerate(PEERS):
        spot = me.flip(a, b)
        arrived(R.gah.at[part(spot.member(), 128)], R.a2s.at[k], R.a2r.at[k], spot)

    share_on(rank_view(0), R.ibs.at[0], R.ibr.at[0])
    R.gk[...] = jnp.zeros((1024, 128), F32)
    R.gv[...] = jnp.zeros((1024, 128), F32)

    def attend_back_tile(t, carry):
        rows = part(t, 256)
        queries, grads = R.qb[rows, :].astype(F32), R.gah[rows, :].astype(F32)
        delta_parts = jnp.transpose(grads) * R.att[t]
        query_grad = []
        for h in range(2):
            mine = jnp.where(head_of == h, queries, 0.0).astype(BF)
            grad = jnp.where(head_of == h, grads, 0.0).astype(BF)
            probs = R.pr[2 * t + h]
            delta = jnp.sum(delta_parts[h * HD : (h + 1) * HD], axis=0, keepdims=True)
            score_grad = (probs.astype(F32) * (dot_t(R.vb[...], grad) - delta)).astype(BF)
            R.gk[...] += dot(score_grad, mine)
            R.gv[...] += dot(probs, grad)
            query_grad.append(dot(R.kt[h * HD : (h + 1) * HD, :], score_grad))
        R.gq[rows, pl.ds(0, 128)] = (jnp.transpose(jnp.concatenate(query_grad, axis=0)) * 0.125).astype(BF)
        return carry

    lax.fori_loop(0, 4, attend_back_tile, 0)
    share_on(rank_view(1), R.ibs.at[1], R.ibr.at[1])
    double_on(first_view, R.gas, R.gar, 1)
    R.gq[:, pl.ds(128, 128)] = R.gk[...].astype(BF)
    R.gq[:, pl.ds(256, 128)] = R.gv[...].astype(BF)

    def qkv_back_tile(i, carry):
        rows = part(lax.rem((1 - p) * 2 + i, 4), 256)
        R.zq[rows, :] = dot_t(R.gq[rows, :], R.qkvb[:, 0:384]).astype(BF)
        return carry

    lax.fori_loop(0, 2, qkv_back_tile, 0)
    pair_send(R.zq, 2)
    lax.fori_loop(2, 4, qkv_back_tile, 0)
    chip_send(R.zq, 2)
    double_on(first_view, R.gas, R.gar, 2)

    leave = SCALE * dot(R.r1t[...], R.gq[...])
    for i in range(3):
        R.db2[:, pl.ds(i * 128, 128)] = leave[i * 16 : (i + 1) * 16, i * 128 : (i + 1) * 128].astype(BF)
    share_end(rank_view(0), R.ibs.at[0], R.ibr.at[0])
    ranks = jnp.transpose(R.ib[0].astype(F32)).astype(BF)
    mlp_enter, out_enter = dot(ranks, R.n2f[:, own]), dot(ranks, R.ath[...])
    block = R.gp[j].astype(F32)
    for k, (a, b) in enumerate(PEERS):
        arrived(R.gr.at[k], R.gps.at[k], R.gpr.at[k], me.flip(a, b))
        block = block + R.gr[k].astype(F32)
    R.db2[:, pl.ds(384, 128)] = out_enter[32:48].astype(BF)
    R.db2[:, pl.ds(512, 128)] = block.astype(BF)
    R.db2[:, pl.ds(640, 128)] = mlp_enter[0:16].astype(BF)
    R.db2[:, pl.ds(768, 128)] = mlp_enter[16:32].astype(BF)
    second_local = pltpu.make_async_copy(R.db2, second_view(me), R.gbr.at[31])
    second_local.start()
    second_local.wait()
    double(second_view, R.gbs, R.gbr, 0)

    total = summed(R.zq, 2)
    inner_back = total[:, 1024:1152]
    normed_grad = total[:, 0:1024] + dot_t(inner_back.astype(BF), R.qkvb[0:1024, 384:512])
    start_rows = R.xf[own, :].astype(F32)
    inverse = lax.rsqrt(jnp.mean(start_rows * start_rows, axis=-1, keepdims=True) + EPS)
    R.ib[2, own, :] = inner_back.astype(BF)
    share(rank_view(2), R.ibs.at[2], R.ibr.at[2])
    double_on(second_view, R.gbs, R.gbr, 0)
    R.igv[...] = (R.mg[...] + norm_back(start_rows, inverse, gain_one, normed_grad)).astype(BF)

    share_end(rank_view(1), R.ibs.at[1], R.ibr.at[1])
    last_leave = SCALE * dot(jnp.transpose(R.ib[1].astype(F32)).astype(BF), R.ogf[:, own])
    R.dc[:, pl.ds(384, 128)] = last_leave[0:16].astype(BF)
    share_on(rank_view(2), R.ibs.at[2], R.ibr.at[2])
    share_end(rank_view(2), R.ibs.at[2], R.ibr.at[2])
    double_on(second_view, R.gbs, R.gbr, 1)
    attn_enter = dot(jnp.transpose(R.ib[2].astype(F32)).astype(BF), R.n1c[...])
    for i in range(3):
        R.dc[:, pl.ds(i * 128, 128)] = attn_enter[i * 16 : (i + 1) * 16].astype(BF)

    third_local = pltpu.make_async_copy(R.dc, third_view(me), R.gcr.at[3, 0])
    third_local.start()
    for k, (a, b) in enumerate(ACROSS):
        send(R.dc, third_view(me), R.gcs.at[k, 0], R.gcr.at[k, 0], me.flip(a, b))
    third_local.wait()
    share(third_view, R.gds.at[3], R.gdr.at[3])
    double_on(second_view, R.gbs, R.gbr, 2)
    give_back(R.igv, R.ig_o, R.bis, R.bir)
    for k, (a, b) in enumerate(ACROSS):
        arrived(third_view(me.flip(a, b)), R.gcs.at[k, 0], R.gcr.at[k, 0], me.flip(a, b))
        share(lambda spot, b=b: third_view(spot.flip(0, b)), R.gds.at[k], R.gdr.at[k])
    double_on(first_view, R.gas, R.gar, 3)
    flips = {0: 2, 1: 8, 2: 10, 3: 0}
    for k in (3, 0, 1, 2):
        share_on(lambda spot, k=k: third_view(spot.flip(0, flips[k])), R.gds.at[k], R.gdr.at[k])
    double_on(second_view, R.gbs, R.gbr, 3)
    double_end(first_view, R.gas, R.gar)
    double_end(second_view, R.gbs, R.gbr)
    for k in (3, 0, 1, 2):
        share_end(lambda spot, k=k: third_view(spot.flip(0, flips[k])), R.gds.at[k], R.gdr.at[k])

    meta_out = pltpu.make_async_copy(R.meta.at[:, :, pl.ds(0, 128)], R.meta_o, R.mr.at[2])
    meta_out.start()
    give_back_wait(R.outv, R.out_o, R.bos, R.bor)
    give_back_wait(R.igv, R.ig_o, R.bis, R.bir)
    reshard_sent(R.x_h, R.xs)
    reshard_sent(R.og_h, R.os)
    for copy in late:
        copy.wait_send()
    meta_out.wait()


SMALL = dict(seg_h=0, ids_h=0, g1_h=0, g2_h=0)


def layer_call(**inputs):
    V, S = pltpu.VMEM, pltpu.SemaphoreType.DMA
    outputs = dict(
        out_o=((2, 64, 1024), BF),
        ig_o=((2, 64, 1024), BF),
        ga_o=((4, 8, 16, WIDTHS[0]), BF),
        gb_o=((4, 8, 16, WIDTHS[1]), BF),
        gc_o=((4, 8, 16, WIDTHS[2]), BF),
        meta_o=((2, 8, 128), jnp.int32),
    )
    scratch = dict(
        xf=V((1024, 1024), BF), ogf=V((1024, 1024), BF), n2f=V((1024, 1024), BF),
        qkvb=V((1152, 512), BF), ob=V((1152, 1152), BF), gub=V((1152, 1152), BF), db=V((640, 1152), BF),
        ae=V((3, 8, 16, 1024), BF), al=V((3, 8, 16, 128), BF), oe=V((8, 16, 1024), BF), ol=V((8, 16, 1024), BF),
        me=V((2, 8, 16, 1024), BF), ml=V((2, 8, 16, 512), BF), le=V((8, 16, 512), BF), ll=V((8, 16, 1024), BF),
        own=V((8, 1024), jnp.int32), gl=V((16, 128), F32), meta=V((2, 8, 1024), jnp.int32), gs=V((4, 8, 16, 128), F32), segc=V((1024, 128), F32),
        qb=V((1024, 128), BF), kb=V((1024, 128), BF), vb=V((1024, 128), BF), kt=V((128, 1024), BF),
        vt=V((128, 1024), BF), r1t=V((128, 1024), BF), pr=V((8, 1024, 256), BF), att=V((4, 128, 256), F32),
        ath=V((1024, 128), BF), ato=V((128, 1024), BF), mid=V((128, 1024), F32), mg=V((128, 1024), F32),
        rot=V((128, 128), BF), zn=V((1024, 1152), BF), zd=V((1024, 1152), BF), zq=V((1024, 1152), BF),
        rp=V((3, 512, 1152), BF), rc=V((3, 512, 1152), BF), rr=V((3, 3, 128, 1152), BF),
        pair=V((1024, 1024), F32), hid=V((1024, 512), BF), r2t=V((128, 1024), BF), cml=V((128, 1024), F32), cle=V((128, 512), F32), gao=V((128, 1024), BF), gah=V((1024, 128), BF),
        gk=V((1024, 128), F32), gv=V((1024, 128), F32), gq=V((1024, 384), BF), outv=V((128, 1024), BF),
        igv=V((128, 1024), BF), gp=V((8, 16, 128), BF), gr=V((7, 16, 128), BF), da=V((16, WIDTHS[0]), BF),
        db2=V((16, WIDTHS[1]), BF), dc=V((16, WIDTHS[2]), BF), ib=V((3, 1024, 128), BF), n1c=V((1024, 128), BF), g1v=V((1, 1024), F32),
        la=S((16,)), xs=S((2,)), xr=S((2,)), os=S((2,)), ors=S((2,)), g1s=S((7,)), g1r=S((8,)),
        g2s=S((3, 1)), g2r=S((3, 1)), w1qs=S((8, 3)), w1qr=S((8, 3)), w1ms=S((8, 8)), w1mr=S((8, 8)),
        w2qs=S((3, 4)), w2qr=S((3, 4)), w2ms=S((3, 4)), w2mr=S((3, 4)), wos=S((31,)), wor=S((32,)),
        wds=S((3, 1)), wdr=S((4, 1)), ms=S((1,)), mr=S((3,)), axs=S((9,)), axr=S((9,)),
        aos=S((9,)), aor=S((9,)), ans=S((9,)), anr=S((9,)), ibs=S((3, 7)), ibr=S((3, 7)),
        a1s=S((7,)), a1r=S((8,)), a2s=S((7,)), a2r=S((8,)), rps=S((3,)), rpr=S((3,)),
        rrs=S((3, 3)), rrr=S((3, 3)), bos=S((2,)), bor=S((2,)), bis=S((2,)), bir=S((2,)),
        gps=S((7,)), gpr=S((7,)), gas=S((31,)), gar=S((32,)), gbs=S((31,)), gbr=S((32,)),
        gcs=S((3, 1)), gcr=S((4, 1)), gds=S((4, 7)), gdr=S((4, 7)),
    )
    names = list(inputs) + list(outputs) + list(scratch)
    return pl.pallas_call(
        functools.partial(layer_kernel, names),
        out_shape=[jax.ShapeDtypeStruct(shape, dtype) for shape, dtype in outputs.values()],
        in_specs=[pl.BlockSpec(memory_space=pltpu.VMEM if name in SMALL else pl.ANY) for name in inputs],
        out_specs=[pl.BlockSpec(memory_space=pl.ANY)] * len(outputs),
        scratch_shapes=list(scratch.values()),
        compiler_params=pltpu.CompilerParams(collective_id=0, has_side_effects=True, vmem_limit_bytes=63 * 2**20),
        name="layer",
    )(*inputs.values())


def place_kernel(ids, first, second, third, out_i, ig_i, out_o, ig_o, ae_o, al_o, oe_o, ol_o, me_o, ml_o, le_o, ll_o):
    a = pl.program_id(0)
    outs = (ae_o, al_o, oe_o, ol_o, me_o, ml_o, le_o, ll_o)

    @pl.when(a == 0)
    def _():
        out_o[...] = out_i[...]
        ig_o[...] = ig_i[...].astype(F32)

    for ref in outs:
        ref[...] = jnp.zeros(ref.shape, F32)
    for group in range(4):
        ident = ids[group % 2, 2 + group // 2, 0]

        @pl.when(ident == a)
        def _(group=group):
            for m in range(8):
                at = slice(m * 128, (m + 1) * 128)
                for i in range(3):
                    al_o[i, 0, :, at] += second[group, m, :, i * 128 : (i + 1) * 128].astype(F32)
                    ae_o[i, 0, :, at] += third[group, m, :, i * 128 : (i + 1) * 128].astype(F32)
                oe_o[0, :, at] += second[group, m, :, 384:512].astype(F32)
                ol_o[0, :, at] += second[group, m, :, 512:640].astype(F32)
                for i in range(2):
                    me_o[i, 0, :, at] += second[group, m, :, 640 + i * 128 : 768 + i * 128].astype(F32)
                ll_o[0, :, at] += third[group, m, :, 384:512].astype(F32)
                for q in range(4):
                    fb = ((m // 4) * 16 + (q // 2) * 8 + (m // 2 % 2) * 4 + (q % 2) * 2 + m % 2) * 128
                    for i in range(2):
                        ml_o[i, 0, :, fb : fb + 128] += first[group, m, :, i * 512 + q * 128 : i * 512 + (q + 1) * 128].astype(F32)
                    le_o[0, :, fb : fb + 128] += first[group, m, :, 1024 + q * 128 : 1024 + (q + 1) * 128].astype(F32)


def place_call(meta, *inputs):
    def whole(shape):
        return pl.BlockSpec(shape, lambda a, ids: (0,) * len(shape))

    def four(n, width):
        return pl.BlockSpec((n, 1, 16, width), lambda a, ids: (0, a, 0, 0))

    def three(width):
        return pl.BlockSpec((1, 16, width), lambda a, ids: (a, 0, 0))

    shapes = ((3, 8, 16, 1024), (3, 8, 16, 1024), (8, 16, 1024), (8, 16, 1024), (2, 8, 16, 1024), (2, 8, 16, 4096), (8, 16, 4096), (8, 16, 1024))
    return pl.pallas_call(
        place_kernel,
        out_shape=[jax.ShapeDtypeStruct((2, 64, 1024), BF), jax.ShapeDtypeStruct((2, 64, 1024), F32)]
        + [jax.ShapeDtypeStruct(shape, F32) for shape in shapes],
        grid_spec=pltpu.PrefetchScalarGridSpec(
            num_scalar_prefetch=1,
            grid=(8,),
            in_specs=[whole(array.shape) for array in inputs],
            out_specs=[whole((2, 64, 1024)), whole((2, 64, 1024)), four(3, 1024), four(3, 1024), three(1024), three(1024),
                       four(2, 1024), four(2, 4096), three(4096), three(1024)],
        ),
        compiler_params=pltpu.CompilerParams(vmem_limit_bytes=63 * 2**20),
        name="place",
    )(meta, *inputs)


def grouped(
    inputs, segment_ids, adapter_ids, w_query, w_key, w_value, w_out, w_gate, w_up, w_down, gain_attn, gain_ffn,
    attn_enter, attn_leave, out_enter, out_leave, mlp_enter, mlp_leave, last_enter, last_leave, out_grad,
):
    out, ig, *shares, meta_all = layer_call(
        x_h=inputs[:, 0], og_h=out_grad[:, 0], seg_h=segment_ids, ids_h=adapter_ids.reshape(1, 2), g1_h=gain_attn[None, :], g2_h=gain_ffn[None, :], wq_h=w_query, wk_h=w_key, wv_h=w_value, wo_h=w_out,
        wg_h=w_gate, wu_h=w_up, wd_h=w_down, ae_h=attn_enter, al_h=attn_leave, oe_h=out_enter, ol_h=out_leave,
        me_h=mlp_enter, ml_h=mlp_leave, le_h=last_enter, ll_h=last_leave,
    )
    out, ig, *grads = place_call(meta_all, *shares, out, ig)
    return (out[:, None], ig[:, None], *grads)


def solution(mesh):
    def chosen(*args):
        sizes = (mesh.shape["dp"], mesh.shape["ctx"], *args[0].shape)
        return (grouped if sizes == (2, 16, 2, 1, 64, 1024) else per_device)(*args)

    return jax.shard_map(
        chosen,
        mesh=mesh,
        in_specs=(
            P(None, "dp", "ctx", None),
            P(None, "dp", None),
            P(None, "dp"),
            P(("dp", "ctx"), None),
            P(("dp", "ctx"), None),
            P(("dp", "ctx"), None),
            P(("dp", "ctx"), None),
            P(("dp", "ctx"), None),
            P(("dp", "ctx"), None),
            P(("dp", "ctx"), None),
            P(("dp", "ctx")),
            P(("dp", "ctx")),
            P(),
            P(),
            P(),
            P(),
            P(),
            P(),
            P(),
            P(),
            P(None, "dp", "ctx", None),
        ),
        out_specs=(
            P(None, "dp", "ctx", None),
            P(None, "dp", "ctx", None),
            P(),
            P(),
            P(),
            P(),
            P(),
            P(),
            P(),
            P(),
        ),
        check_vma=False,
    )
```

```python
import functools
import types

import jax
import jax.numpy as jnp
from jax import lax
from jax.experimental import pallas as pl
from jax.experimental.pallas import tpu as pltpu
from jax.sharding import PartitionSpec as P

H = 16
HD = 64


EPS = 1e-05
NEG = -1000000000.0
SCALE = 0.5


def rms_norm(rows, gain):
    inverse = lax.rsqrt(jnp.mean(rows * rows, axis=-1, keepdims=True) + EPS)
    return (rows * inverse * gain, inverse)


def norm_back(rows, inverse, gain, grad):
    weighted = grad * gain
    return inverse * weighted - rows * inverse**3 * jnp.mean(
        rows * weighted, axis=-1, keepdims=True
    )


def project(rows, weight, enter, leave):
    direct = jnp.einsum("sci,io->sco", rows, weight, preferred_element_type=jnp.float32)
    inner = jnp.einsum("sci,sri->scr", rows, enter, preferred_element_type=jnp.float32).astype(
        jnp.bfloat16
    )
    return (
        direct
        + SCALE * jnp.einsum("scr,sro->sco", inner, leave, preferred_element_type=jnp.float32),
        inner,
    )


def project_back(rows, inner, weight, enter, leave, grad):
    inner_grad = (
        SCALE * jnp.einsum("sco,sro->scr", grad, leave, preferred_element_type=jnp.float32)
    ).astype(jnp.bfloat16)
    rows_grad = jnp.einsum("sco,io->sci", grad, weight, preferred_element_type=jnp.float32)
    rows_grad = rows_grad + jnp.einsum(
        "scr,sri->sci", inner_grad, enter, preferred_element_type=jnp.float32
    )
    enter_grad = jnp.einsum("scr,sci->sri", inner_grad, rows, preferred_element_type=jnp.float32)
    leave_grad = SCALE * jnp.einsum("scr,sco->sro", inner, grad, preferred_element_type=jnp.float32)
    return (rows_grad, enter_grad, leave_grad)


def masked_scores(query_heads, key_block, seg_query, seg_key):
    seqs = query_heads.shape[0]
    key_heads = key_block.reshape(seqs, -1, H, HD)
    scores = (
        jnp.einsum("sqhd,skhd->shqk", query_heads, key_heads, preferred_element_type=jnp.float32)
        * 0.125
    )
    same = seg_query[:, None, :, None] == seg_key[:, None, None, :]
    return (jnp.where(same, scores, NEG), key_heads)


def forward_block(state, query_heads, seg_query, key_block, value_block, seg_key):
    best, total, accum = state
    seqs = query_heads.shape[0]
    scores, key_heads = masked_scores(query_heads, key_block, seg_query, seg_key)
    value_heads = value_block.reshape(seqs, -1, H, HD)
    new_best = jnp.maximum(best, jnp.max(scores, axis=-1))
    factor = jnp.exp(best - new_best)
    weights = jnp.exp(scores - new_best[..., None])
    total = total * factor + jnp.sum(weights, axis=-1)
    mixed = jnp.einsum(
        "shqk,skhd->sqhd",
        weights.astype(jnp.bfloat16),
        value_heads,
        preferred_element_type=jnp.float32,
    )
    accum = accum * jnp.transpose(factor, (0, 2, 1))[..., None] + mixed
    return (new_best, total, accum)


def attend(query, key, value, seg_rows, my_start):
    seqs, rows, width = query.shape
    query_heads = query.reshape(seqs, rows, H, HD)
    seg_query = lax.dynamic_slice_in_dim(seg_rows, my_start, rows, 1)
    state = (
        jnp.full((seqs, H, rows), -1e30, jnp.float32),
        jnp.zeros((seqs, H, rows), jnp.float32),
        jnp.zeros((seqs, rows, H, HD), jnp.float32),
    )

    def fold(carry, piece, start):
        key_piece, value_piece = piece
        count = key_piece.shape[1]
        block = 512

        def advance(index, inner_state):
            offset = index * block
            key_block = lax.dynamic_slice_in_dim(key_piece, offset, block, 1)
            value_block = lax.dynamic_slice_in_dim(value_piece, offset, block, 1)
            seg_key = lax.dynamic_slice_in_dim(seg_rows, offset, block, 1)
            return forward_block(
                inner_state, query_heads, seg_query, key_block, value_block, seg_key
            )

        return lax.fori_loop(0, count // block, advance, carry)

    best, total, accum = fold(
        state,
        (
            lax.all_gather(key, "ctx", axis=1, tiled=True),
            lax.all_gather(value, "ctx", axis=1, tiled=True),
        ),
        jnp.int32(0),
    )
    output = accum / jnp.transpose(total, (0, 2, 1))[..., None]
    return (output, best + jnp.log(total))


def block_grads(
    query_heads, grad_heads, log_total, delta, seg_query, key_block, value_block, seg_key
):
    seqs = query_heads.shape[0]
    scores, key_heads = masked_scores(query_heads, key_block, seg_query, seg_key)
    value_heads = value_block.reshape(seqs, -1, H, HD)
    probs = jnp.exp(scores - log_total[..., None])
    value_part = jnp.einsum(
        "shqk,sqhd->skhd",
        probs.astype(jnp.bfloat16),
        grad_heads,
        preferred_element_type=jnp.float32,
    )
    prob_grad = jnp.einsum(
        "sqhd,skhd->shqk", grad_heads, value_heads, preferred_element_type=jnp.float32
    )
    score_grad = (probs * (prob_grad - delta[..., None])).astype(jnp.bfloat16)
    query_part = 0.125 * jnp.einsum(
        "shqk,skhd->sqhd", score_grad, key_heads, preferred_element_type=jnp.float32
    )
    key_part = 0.125 * jnp.einsum(
        "shqk,sqhd->skhd", score_grad, query_heads, preferred_element_type=jnp.float32
    )
    return (query_part, key_part, value_part)


def attend_back(query, key, value, grad, output, log_total, seg_rows, my_start):
    seqs, rows, width = query.shape
    length = seg_rows.shape[1]
    query_heads = query.reshape(seqs, rows, H, HD)
    grad_heads = grad.reshape(seqs, rows, H, HD)
    seg_query = lax.dynamic_slice_in_dim(seg_rows, my_start, rows, 1)
    delta = jnp.transpose(jnp.sum(grad_heads.astype(jnp.float32) * output, axis=-1), (0, 2, 1))
    state = (
        jnp.zeros((seqs, rows, H, HD), jnp.float32),
        jnp.zeros((seqs, length, width), jnp.float32),
        jnp.zeros((seqs, length, width), jnp.float32),
    )

    def fold(carry, piece, start):
        key_piece, value_piece = piece
        count = key_piece.shape[1]
        block = 512

        def advance(index, inner_state):
            offset = index * block
            key_block = lax.dynamic_slice_in_dim(key_piece, offset, block, 1)
            value_block = lax.dynamic_slice_in_dim(value_piece, offset, block, 1)
            seg_key = lax.dynamic_slice_in_dim(seg_rows, offset, block, 1)
            query_part, key_part, value_part = block_grads(
                query_heads,
                grad_heads,
                log_total,
                delta,
                seg_query,
                key_block,
                value_block,
                seg_key,
            )
            query_grad, key_all, value_all = inner_state
            key_old = lax.dynamic_slice_in_dim(key_all, offset, block, 1)
            key_all = lax.dynamic_update_slice_in_dim(
                key_all, key_old + key_part.reshape(seqs, block, width), offset, 1
            )
            value_old = lax.dynamic_slice_in_dim(value_all, offset, block, 1)
            value_all = lax.dynamic_update_slice_in_dim(
                value_all, value_old + value_part.reshape(seqs, block, width), offset, 1
            )
            return (query_grad + query_part, key_all, value_all)

        return lax.fori_loop(0, count // block, advance, carry)

    folded = fold(
        state,
        (
            lax.all_gather(key, "ctx", axis=1, tiled=True),
            lax.all_gather(value, "ctx", axis=1, tiled=True),
        ),
        jnp.int32(0),
    )
    query_grad = folded[0]
    key_grad, value_grad = (
        lax.psum_scatter(
            folded[1].astype(jnp.bfloat16), "ctx", scatter_dimension=1, tiled=True
        ).astype(jnp.float32),
        lax.psum_scatter(
            folded[2].astype(jnp.bfloat16), "ctx", scatter_dimension=1, tiled=True
        ).astype(jnp.float32),
    )
    return (
        query_grad.reshape(seqs, rows, width).astype(jnp.bfloat16),
        key_grad.astype(jnp.bfloat16),
        value_grad.astype(jnp.bfloat16),
    )


def per_device(
    inputs,
    segment_ids,
    adapter_ids,
    w_query,
    w_key,
    w_value,
    w_out,
    w_gate,
    w_up,
    w_down,
    gain_attn,
    gain_ffn,
    attn_enter,
    attn_leave,
    out_enter,
    out_leave,
    mlp_enter,
    mlp_leave,
    last_enter,
    last_leave,
    out_grad,
):
    micro_count, seqs, rows, width = inputs.shape
    my_start = lax.axis_index("ctx") * rows
    adapter_count = attn_enter.shape[1]
    sum_attn_enter = jnp.zeros(attn_enter.shape, jnp.float32)
    sum_attn_leave = jnp.zeros(attn_leave.shape, jnp.float32)
    sum_out_enter = jnp.zeros(out_enter.shape, jnp.float32)
    sum_out_leave = jnp.zeros(out_leave.shape, jnp.float32)
    sum_mlp_enter = jnp.zeros(mlp_enter.shape, jnp.float32)
    sum_mlp_leave = jnp.zeros(mlp_leave.shape, jnp.float32)
    sum_last_enter = jnp.zeros(last_enter.shape, jnp.float32)
    sum_last_leave = jnp.zeros(last_leave.shape, jnp.float32)
    outputs = []
    gradients = []
    for micro in range(micro_count):
        frozen = (
            lax.all_gather(w_query, ("dp", "ctx"), axis=0, tiled=True),
            lax.all_gather(w_key, ("dp", "ctx"), axis=0, tiled=True),
            lax.all_gather(w_value, ("dp", "ctx"), axis=0, tiled=True),
            lax.all_gather(w_out, ("dp", "ctx"), axis=0, tiled=True),
            lax.all_gather(w_gate, ("dp", "ctx"), axis=0, tiled=True),
            lax.all_gather(w_up, ("dp", "ctx"), axis=0, tiled=True),
            lax.all_gather(w_down, ("dp", "ctx"), axis=0, tiled=True),
            lax.all_gather(gain_attn, ("dp", "ctx"), axis=0, tiled=True),
            lax.all_gather(gain_ffn, ("dp", "ctx"), axis=0, tiled=True),
        )
        query_w, key_w, value_w, out_w, gate_w, up_w, down_w, gain_one, gain_two = frozen
        chosen = adapter_ids[micro]
        attn_in = jnp.take(attn_enter, chosen, axis=1)
        attn_out = jnp.take(attn_leave, chosen, axis=1)
        out_in = jnp.take(out_enter, chosen, axis=0)
        out_out = jnp.take(out_leave, chosen, axis=0)
        mlp_in = jnp.take(mlp_enter, chosen, axis=1)
        mlp_out = jnp.take(mlp_leave, chosen, axis=1)
        last_in = jnp.take(last_enter, chosen, axis=0)
        last_out = jnp.take(last_leave, chosen, axis=0)
        seg_rows = segment_ids[micro]
        start_rows = inputs[micro].astype(jnp.float32)
        normed_f, inverse_one = rms_norm(start_rows, gain_one.astype(jnp.float32))
        normed = normed_f.astype(jnp.bfloat16)
        query_f, query_inner = project(normed, query_w, attn_in[0], attn_out[0])
        key_f, key_inner = project(normed, key_w, attn_in[1], attn_out[1])
        value_f, value_inner = project(normed, value_w, attn_in[2], attn_out[2])
        query = query_f.astype(jnp.bfloat16)
        key = key_f.astype(jnp.bfloat16)
        value = value_f.astype(jnp.bfloat16)
        mixed_f, log_total = attend(query, key, value, seg_rows, my_start)
        mixed = mixed_f.reshape(seqs, rows, width).astype(jnp.bfloat16)
        branch, out_inner = project(mixed, out_w, out_in, out_out)
        middle = start_rows + branch
        normed_two_f, inverse_two = rms_norm(middle, gain_two.astype(jnp.float32))
        normed_two = normed_two_f.astype(jnp.bfloat16)
        gate, gate_inner = project(normed_two, gate_w, mlp_in[0], mlp_out[0])
        upper, up_inner = project(normed_two, up_w, mlp_in[1], mlp_out[1])
        sigma = jax.nn.sigmoid(gate)
        hidden = (gate * sigma * upper).astype(jnp.bfloat16)
        closing, last_inner = project(hidden, down_w, last_in, last_out)
        outputs.append((middle + closing).astype(jnp.bfloat16))
        frozen = (
            lax.all_gather(w_query, ("dp", "ctx"), axis=0, tiled=True),
            lax.all_gather(w_key, ("dp", "ctx"), axis=0, tiled=True),
            lax.all_gather(w_value, ("dp", "ctx"), axis=0, tiled=True),
            lax.all_gather(w_out, ("dp", "ctx"), axis=0, tiled=True),
            lax.all_gather(w_gate, ("dp", "ctx"), axis=0, tiled=True),
            lax.all_gather(w_up, ("dp", "ctx"), axis=0, tiled=True),
            lax.all_gather(w_down, ("dp", "ctx"), axis=0, tiled=True),
            lax.all_gather(gain_attn, ("dp", "ctx"), axis=0, tiled=True),
            lax.all_gather(gain_ffn, ("dp", "ctx"), axis=0, tiled=True),
        )
        query_w, key_w, value_w, out_w, gate_w, up_w, down_w, gain_one, gain_two = frozen
        grad_rows = out_grad[micro].astype(jnp.float32)
        hidden_grad, last_in_grad, last_out_grad = project_back(
            hidden, last_inner, down_w, last_in, last_out, out_grad[micro]
        )
        gate_grad = (hidden_grad * upper * sigma * (1.0 + gate * (1.0 - sigma))).astype(
            jnp.bfloat16
        )
        up_grad = (hidden_grad * gate * sigma).astype(jnp.bfloat16)
        from_gate, gate_in_grad, gate_out_grad = project_back(
            normed_two, gate_inner, gate_w, mlp_in[0], mlp_out[0], gate_grad
        )
        from_up, up_in_grad, up_out_grad = project_back(
            normed_two, up_inner, up_w, mlp_in[1], mlp_out[1], up_grad
        )
        middle_grad = grad_rows + norm_back(
            middle, inverse_two, gain_two.astype(jnp.float32), from_gate + from_up
        )
        mixed_grad_f, out_in_grad, out_out_grad = project_back(
            mixed, out_inner, out_w, out_in, out_out, middle_grad.astype(jnp.bfloat16)
        )
        mixed_grad = mixed_grad_f.astype(jnp.bfloat16)
        query_grad, key_grad, value_grad = attend_back(
            query, key, value, mixed_grad, mixed_f, log_total, seg_rows, my_start
        )
        from_query, query_in_grad, query_out_grad = project_back(
            normed, query_inner, query_w, attn_in[0], attn_out[0], query_grad
        )
        from_key, key_in_grad, key_out_grad = project_back(
            normed, key_inner, key_w, attn_in[1], attn_out[1], key_grad
        )
        from_value, value_in_grad, value_out_grad = project_back(
            normed, value_inner, value_w, attn_in[2], attn_out[2], value_grad
        )
        gradients.append(
            middle_grad
            + norm_back(
                start_rows,
                inverse_one,
                gain_one.astype(jnp.float32),
                from_query + from_key + from_value,
            )
        )
        per_seq = (
            jnp.stack([query_in_grad, key_in_grad, value_in_grad]),
            jnp.stack([query_out_grad, key_out_grad, value_out_grad]),
            out_in_grad,
            out_out_grad,
            jnp.stack([gate_in_grad, up_in_grad]),
            jnp.stack([gate_out_grad, up_out_grad]),
            last_in_grad,
            last_out_grad,
        )
        onehot = (chosen[:, None] == jnp.arange(adapter_count, dtype=jnp.int32)[None, :]).astype(
            jnp.float32
        )
        sum_attn_enter = sum_attn_enter + jnp.einsum("sa,isrd->iard", onehot, per_seq[0])
        sum_attn_leave = sum_attn_leave + jnp.einsum("sa,isrd->iard", onehot, per_seq[1])
        sum_out_enter = sum_out_enter + jnp.einsum("sa,srd->ard", onehot, per_seq[2])
        sum_out_leave = sum_out_leave + jnp.einsum("sa,srd->ard", onehot, per_seq[3])
        sum_mlp_enter = sum_mlp_enter + jnp.einsum("sa,isrd->iard", onehot, per_seq[4])
        sum_mlp_leave = sum_mlp_leave + jnp.einsum("sa,isrf->iarf", onehot, per_seq[5])
        sum_last_enter = sum_last_enter + jnp.einsum("sa,srf->arf", onehot, per_seq[6])
        sum_last_leave = sum_last_leave + jnp.einsum("sa,srd->ard", onehot, per_seq[7])
    totals = (
        sum_attn_enter,
        sum_attn_leave,
        sum_out_enter,
        sum_out_leave,
        sum_mlp_enter,
        sum_mlp_leave,
        sum_last_enter,
        sum_last_leave,
    )
    summed = lax.psum(
        (totals[0], totals[1], totals[2], totals[3], totals[4], totals[5], totals[6], totals[7]),
        ("dp", "ctx"),
    )
    return (
        jnp.stack(outputs),
        jnp.stack(gradients),
        summed[0],
        summed[1],
        summed[2],
        summed[3],
        summed[4],
        summed[5],
        summed[6],
        summed[7],
    )


MESH = pl.DeviceIdType.MESH
BF = jnp.bfloat16
F32 = jnp.float32
SAME = (1, 4, 5)
PEERS = ((0, 1), (0, 4), (0, 5), (1, 0), (1, 1), (1, 4), (1, 5))
ACROSS = ((0, 2), (0, 8), (0, 10))
GREET = PEERS + ACROSS + ((1, 2), (1, 10))
DOUBLE = (8, 4, 1, 2)
FAR = 64
HELD = (0, 8, 4, 12, 1, 9, 5, 13, 2, 10, 6, 14, 3, 11, 7, 15)
WIDTHS = (1536, 896, 512)


def dot(left, right):
    return lax.dot_general(left, right, (((1,), (0,)), ((), ())), preferred_element_type=F32)


def dot_t(left, right):
    return lax.dot_general(left, right, (((1,), (1,)), ((), ())), preferred_element_type=F32)


class Spot:
    def __init__(self, p, x, y, zl, zh):
        self.p, self.x, self.y, self.zl, self.zh = p, x, y, zl, zh

    def flip(self, a, b):
        return Spot(
            1 - self.p if a else self.p,
            1 - self.x if b & 1 else self.x,
            1 - self.y if b & 2 else self.y,
            1 - self.zl if b & 4 else self.zl,
            1 - self.zh if b & 8 else self.zh,
        )

    def device(self):
        return (self.p, self.x + 2 * self.y + 4 * self.zl + 8 * self.zh)

    def member(self):
        return self.p * 4 + self.zl * 2 + self.x

    def group(self):
        return self.zh * 2 + self.y


def here():
    p, c = lax.axis_index("dp"), lax.axis_index("ctx")
    return Spot(p, lax.rem(c, 2), lax.rem(lax.div(c, 2), 2), lax.rem(lax.div(c, 4), 2), lax.div(c, 8))


def part(index, size):
    return pl.ds(pl.multiple_of(index * size, size), size)


def remote(src, dst, ssem, rsem, spot):
    return pltpu.make_async_remote_copy(
        src_ref=src, dst_ref=dst, send_sem=ssem, recv_sem=rsem, device_id=spot.device(), device_id_type=MESH
    )


def pick(raw, mask):
    total = raw[0].astype(F32) * mask(0)
    for a in range(1, raw.shape[0]):
        total = total + raw[a].astype(F32) * mask(a)
    return total


def layer_kernel(names, *refs):
    R = types.SimpleNamespace(**dict(zip(names, refs, strict=True)))
    me = here()
    p, x, y, zl, zh = me.p, me.x, me.y, me.zl, me.zh
    j = me.member()
    own = part(j, 128)
    partner = me.flip(1, 0)
    late = []

    def send(src, dst, ssem, rsem, spot):
        copy = remote(src, dst, ssem, rsem, spot)
        copy.start()
        late.append(copy)

    def arrived(ref, ssem, rsem, spot):
        remote(ref, ref, ssem, rsem, spot).wait_recv()

    place = lax.broadcasted_iota(jnp.int32, (8, 128), 0) * 4 + lax.broadcasted_iota(jnp.int32, (8, 128), 1) // 32
    for i, gain in enumerate((R.g1_h, R.g2_h)):
        wide = jnp.concatenate([gain[...].astype(F32)] * 4, axis=1)
        R.gl[pl.ds(8 * i, 8), :] = jnp.where(place == p * 16 + me.device()[1], jnp.broadcast_to(wide, (8, 128)), 0.0)
    for micro in range(2):
        seg = R.seg_h[micro]
        seg = [seg[:, c * 64 : (c + 1) * 64] for c in (b + a for a in (0, 1, 4, 5, 2, 3, 6, 7) for b in (0, 8))]
        R.own[pl.ds(micro, 1), :] = jnp.concatenate(seg, axis=1)
        R.own[pl.ds(2 + micro, 1), :] = jnp.broadcast_to(R.ids_h[:, micro : micro + 1], (1, 1024))
    R.own[pl.ds(4, 4), :] = jnp.zeros((4, 1024), jnp.int32)

    barrier = pltpu.get_barrier_semaphore()
    for a, b in GREET:
        pl.semaphore_signal(barrier, inc=1, device_id=me.flip(a, b).device(), device_id_type=MESH)
    pl.semaphore_wait(barrier, len(GREET))

    def reshard(src, dst, ssem, rsem):
        rows = pl.ds(pl.multiple_of((y * 4 + zl * 2 + x) * 128 + zh * 64, 64), 64)

        @pl.when(p == y)
        def _():
            pltpu.make_async_copy(src.at[zh], dst.at[rows], rsem.at[0]).start()
            remote(src.at[1 - zh], dst.at[rows], ssem.at[1], rsem.at[1], me.flip(0, 8)).start()

        @pl.when(p != y)
        def _():
            remote(src.at[zh], dst.at[rows], ssem.at[0], rsem.at[0], me.flip(1, 2)).start()
            remote(src.at[1 - zh], dst.at[rows], ssem.at[1], rsem.at[1], me.flip(1, 10)).start()

    def reshard_wait(dst, rsem):
        for k, t in enumerate((zh, 1 - zh)):
            rows = pl.ds(pl.multiple_of(j * 128 + t * 64, 64), 64)
            pltpu.make_async_copy(dst.at[rows], dst.at[rows], rsem.at[k]).wait()

    def reshard_sent(src, ssem):
        @pl.when(p != y)
        def _():
            remote(src.at[zh], src.at[zh], ssem.at[0], ssem.at[0], me.flip(1, 2)).wait_send()

        remote(src.at[zh], src.at[zh], ssem.at[1], ssem.at[1], me.flip(0, 8)).wait_send()

    def spread(ref, ssem, rsem):
        mine = ref.at[own]
        for k, spot in enumerate((me.flip(0, 1), me.flip(0, 4), partner)):
            send(mine, mine, ssem.at[k], rsem.at[k], spot)

    def rows_at(ref, spot, k):
        first, rows = ((0, FAR), (FAR, 128 - FAR))[k]
        return ref.at[pl.ds(pl.multiple_of(spot.member() * 128 + first, 32), rows)]

    def spread_on(ref, ssem, rsem):
        for k, (came, on) in enumerate(((1, 4), (4, 1))):
            spot = me.flip(0, came)
            got, half = ref.at[part(spot.member(), 128)], rows_at(ref, spot, k)
            arrived(got, ssem.at[k], rsem.at[k], spot)
            send(half, half, ssem.at[3 + k], rsem.at[3 + k], me.flip(0, on))
            send(got, got, ssem.at[5 + k], rsem.at[5 + k], partner)

    def spread_far(ref, ssem, rsem):
        for k, on in enumerate((4, 1)):
            half = rows_at(ref, me.flip(0, 5), k)
            arrived(half, ssem.at[3 + k], rsem.at[3 + k], me.flip(0, on))
            send(half, half, ssem.at[7 + k], rsem.at[7 + k], partner)

    def spread_end(ref, ssem, rsem):
        arrived(ref.at[part(partner.member(), 128)], ssem.at[2], rsem.at[2], partner)
        for k, came in enumerate((1, 4)):
            arrived(ref.at[part(me.flip(1, came).member(), 128)], ssem.at[5 + k], rsem.at[5 + k], partner)
            arrived(rows_at(ref, me.flip(1, 5), k), ssem.at[7 + k], rsem.at[7 + k], partner)

    def share(view, ssem, rsem):
        mine = view(me)
        for k, b in enumerate(SAME):
            send(mine, mine, ssem.at[k], rsem.at[k], me.flip(0, b))
        send(mine, mine, ssem.at[3], rsem.at[3], partner)

    def share_on(view, ssem, rsem):
        for k, b in enumerate(SAME):
            got = view(me.flip(0, b))
            arrived(got, ssem.at[k], rsem.at[k], me.flip(0, b))
            send(got, got, ssem.at[4 + k], rsem.at[4 + k], partner)

    def share_end(view, ssem, rsem):
        arrived(view(partner), ssem.at[3], rsem.at[3], partner)
        for k, b in enumerate(SAME):
            arrived(view(me.flip(1, b)), ssem.at[4 + k], rsem.at[4 + k], partner)

    def double(view, ssem, rsem, step):
        for k in range(2**step):
            ref, n = view(me.flip(0, HELD[k])), 2**step - 1 + k
            send(ref, ref, ssem.at[n], rsem.at[n], me.flip(0, DOUBLE[step]))
        if step == 0:
            send(view(me), view(me), ssem.at[15], rsem.at[15], partner)

    def double_on(view, ssem, rsem, step):
        for k in range(2**step):
            ref, n = view(me.flip(0, HELD[2**step + k])), 2**step - 1 + k
            arrived(ref, ssem.at[n], rsem.at[n], me.flip(0, DOUBLE[step]))
            send(ref, ref, ssem.at[16 + n], rsem.at[16 + n], partner)
        if step < 3:
            double(view, ssem, rsem, step + 1)

    def double_end(view, ssem, rsem):
        for k in range(16):
            arrived(view(me.flip(1, HELD[k])), ssem.at[15 + k], rsem.at[15 + k], partner)

    def across(views, ssem, rsem, axis, pieces=(0,)):
        for k in pieces:
            view = views(me)[k]
            send(view, view, ssem.at[axis, k], rsem.at[axis, k], me.flip(0, (8, 2)[axis]))

    def across_on(views, ssem, rsem, pieces=(0,)):
        for k in pieces:
            view = views(me.flip(0, 8))[k]
            arrived(view, ssem.at[0, k], rsem.at[0, k], me.flip(0, 8))
            send(view, view, ssem.at[2, k], rsem.at[2, k], me.flip(0, 2))

    def across_end(views, ssem, rsem):
        for k, view in enumerate(views(me.flip(0, 2))):
            arrived(view, ssem.at[1, k], rsem.at[1, k], me.flip(0, 2))
        for k, view in enumerate(views(me.flip(0, 10))):
            arrived(view, ssem.at[2, k], rsem.at[2, k], me.flip(0, 2))

    def row_views(ref, columns):
        def views(spot):
            return [
                ref.at[pl.ds(pl.multiple_of(pp * 512 + spot.zh * 256 + zz * 128 + spot.y * 64, 64), 64), pl.ds(0, columns)]
                for pp in range(2)
                for zz in range(2)
            ]

        return views

    qkv_views, gu_views = row_views(R.qkvb, 384), row_views(R.gub, 1024)

    def down_views(spot):
        return [R.db.at[part(spot.group(), 128), pl.ds(0, 1024)]]

    def out_view(spot):
        k_row = (spot.p * 16 + spot.zh * 8 + spot.zl * 4 + spot.y * 2 + spot.x) * 32
        return R.ob.at[pl.ds(pl.multiple_of(k_row, 32), 32), pl.ds(0, 1024)]

    def gain_views(spot):
        return [R.gs.at[spot.group()]]

    my_row = pl.ds(pl.multiple_of((p * 16 + zh * 8 + zl * 4 + y * 2 + x) * 32, 32), 32)

    raws = (
        (R.ae, R.ae_h), (R.al, R.al_h.at[:, :, :, own]), (R.oe, R.oe_h), (R.ol, R.ol_h), (R.me, R.me_h), (R.ll, R.ll_h),
    )
    locals_ = []
    for k, (dst, src) in enumerate(raws):
        locals_.append(pltpu.make_async_copy(src, dst, R.la.at[k]))
    for q in range(4):
        fb = part(p * 16 + (q // 2) * 8 + zl * 4 + (q % 2) * 2 + x, 128)
        locals_.append(pltpu.make_async_copy(R.ml_h.at[:, :, :, fb], R.ml.at[:, :, :, pl.ds(q * 128, 128)], R.la.at[8 + q]))
        locals_.append(pltpu.make_async_copy(R.le_h.at[:, :, fb], R.le.at[:, :, pl.ds(q * 128, 128)], R.la.at[12 + q]))

    reshard(R.x_h, R.xf, R.xs, R.xr)

    gain_mine = R.gs.at[me.group(), j]
    gain_local = pltpu.make_async_copy(R.gl, gain_mine, R.g1r.at[7])
    gain_local.start()
    for k, (a, b) in enumerate(PEERS):
        send(R.gl, gain_mine, R.g1s.at[k], R.g1r.at[k], me.flip(a, b))

    def columns_to(spot, k, start):
        t = spot.member()
        for i, src in enumerate((R.wq_h, R.wk_h, R.wv_h)):
            start(src.at[:, part(t, 128)], R.qkvb.at[my_row, pl.ds(i * 128, 128)], R.w1qs.at[k, i], R.w1qr.at[k, i])

    def mlp_columns_to(spot, k, start):
        for i, src in enumerate((R.wg_h, R.wu_h)):
            for q in range(4):
                fb = part(spot.p * 16 + (q // 2) * 8 + spot.zl * 4 + (q % 2) * 2 + spot.x, 128)
                at = (k, i * 4 + q)
                start(src.at[:, fb], R.gub.at[my_row, pl.ds(i * 512 + q * 128, 128)], R.w1ms.at[*at], R.w1mr.at[*at])

    def start_remote(spot):
        return lambda src, dst, ssem, rsem: send(src, dst, ssem, rsem, spot)

    def start_local(src, dst, ssem, rsem):
        pltpu.make_async_copy(src, dst, rsem).start()

    for k, (a, b) in enumerate(PEERS):
        columns_to(me.flip(a, b), k, start_remote(me.flip(a, b)))
    columns_to(me, 7, start_local)

    meta_local = pltpu.make_async_copy(R.own, R.meta.at[p], R.mr.at[1])
    meta_local.start()
    send(R.own, R.meta.at[p], R.ms.at[0], R.mr.at[0], partner)
    for copy in locals_:
        copy.start()

    out_local = pltpu.make_async_copy(R.wo_h, out_view(me), R.wor.at[31])
    out_local.start()
    send(R.wo_h, out_view(me), R.wos.at[0], R.wor.at[0], me.flip(0, DOUBLE[0]))
    send(R.wo_h, out_view(me), R.wos.at[15], R.wor.at[15], partner)
    for k, (a, b) in enumerate(PEERS):
        mlp_columns_to(me.flip(a, b), k, start_remote(me.flip(a, b)))
    mlp_columns_to(me, 7, start_local)

    reshard_wait(R.xf, R.xr)
    spread(R.xf, R.axs, R.axr)

    def rows_of(spot):
        return pl.ds(pl.multiple_of((spot.p * 16 + spot.zh * 8 + spot.zl * 4 + spot.y * 2 + spot.x) * 32, 32), 32)

    def first_end(target, rsem, pieces):
        for k, (a, b) in enumerate(PEERS + ((0, 0),)):
            rows = rows_of(me.flip(a, b))
            for i in range(pieces):
                ref = target.at[rows, pl.ds(i * 128, 128)]
                pltpu.make_async_copy(ref, ref, rsem.at[k, i]).wait()

    first_end(R.qkvb, R.w1qr, 3)
    across(qkv_views, R.w2qs, R.w2qr, 0, range(4))
    across(qkv_views, R.w2qs, R.w2qr, 1, range(4))
    reshard(R.og_h, R.ogf, R.os, R.ors)
    for k, (a, b) in enumerate(PEERS):
        spot = me.flip(a, b)
        arrived(R.gs.at[me.group(), spot.member()], R.g1s.at[k], R.g1r.at[k], spot)
    gain_local.wait()
    across(gain_views, R.g2s, R.g2r, 0)
    across(gain_views, R.g2s, R.g2r, 1)
    spread_on(R.xf, R.axs, R.axr)
    out_local.wait()
    double_on(out_view, R.wos, R.wor, 0)
    across_on(qkv_views, R.w2qs, R.w2qr, range(4))
    first_end(R.gub, R.w1mr, 8)
    across(gu_views, R.w2ms, R.w2mr, 1, range(4))
    across(gu_views, R.w2ms, R.w2mr, 0, (0,))
    down_mine = down_views(me)[0]
    down_local = pltpu.make_async_copy(R.wd_h, down_mine, R.wdr.at[3, 0])
    down_local.start()
    across_on(gain_views, R.g2s, R.g2r)

    pltpu.make_async_copy(R.own, R.meta.at[p], R.mr.at[1]).wait()
    arrived(R.meta.at[1 - p], R.ms.at[0], R.mr.at[0], partner)
    for copy in locals_:
        copy.wait()
    ids = R.meta[y, pl.ds(2 + zh, 1), :]

    def mask(width):
        return lambda a: (ids[:, 0:width] == a).astype(F32)

    def enter_columns(items):
        rows = [pick(item, mask(item.shape[-1])) for item in items]
        width = rows[0].shape[-1]
        rows.append(jnp.zeros((128 - 16 * len(rows), width), F32))
        return jnp.transpose(jnp.concatenate(rows, axis=0)).astype(BF)

    def leave_rows(ref, first, items):
        ref[pl.ds(first, 128), :] = jnp.zeros((128, ref.shape[1]), BF)
        column = 0
        for i, item in enumerate(items):
            width = item.shape[-1]
            ref[pl.ds(first + 16 * i, 16), pl.ds(column, width)] = (SCALE * pick(item, mask(width))).astype(BF)
            column += width

    R.qkvb[pl.ds(0, 1024), pl.ds(384, 128)] = enter_columns([R.ae.at[i] for i in range(3)])
    leave_rows(R.qkvb, 1024, [R.al.at[i] for i in range(3)])
    R.ob[pl.ds(0, 1024), pl.ds(1024, 128)] = enter_columns([R.oe])
    leave_rows(R.ob, 1024, [R.ol])
    R.gub[pl.ds(0, 1024), pl.ds(1024, 128)] = enter_columns([R.me.at[i] for i in range(2)])
    leave_rows(R.gub, 1024, [R.ml.at[i] for i in range(2)])
    R.db[pl.ds(0, 512), pl.ds(1024, 128)] = enter_columns([R.le])
    leave_rows(R.db, 512, [R.ll])

    seg_row = R.meta[y, pl.ds(zh, 1), :]
    R.segc[...] = jnp.transpose(jnp.broadcast_to(seg_row.astype(F32), (128, 1024)))

    across(gu_views, R.w2ms, R.w2mr, 0, (1,))
    double_on(out_view, R.wos, R.wor, 1)
    across_end(gain_views, R.g2s, R.g2r)
    gains = jnp.sum(jnp.sum(R.gs[...], axis=0), axis=0)
    gain_one = jnp.concatenate([gains[i : i + 1] for i in range(8)], axis=1)
    gain_two = jnp.concatenate([gains[i : i + 1] for i in range(8, 16)], axis=1)

    spread_far(R.xf, R.axs, R.axr)
    spread_end(R.xf, R.axs, R.axr)
    reshard_wait(R.ogf, R.ors)
    spread(R.ogf, R.aos, R.aor)
    across(gu_views, R.w2ms, R.w2mr, 0, (2,))
    double_on(out_view, R.wos, R.wor, 2)
    across_end(qkv_views, R.w2qs, R.w2qr)

    def qkv_tile(t, carry):
        rows = part(t, 256)
        held = R.xf[rows, :].astype(F32)
        inverse = lax.rsqrt(jnp.mean(held * held, axis=-1, keepdims=True) + EPS)
        normed = (held * inverse * gain_one).astype(BF)
        both = dot(normed, R.qkvb[0:1024, :])
        inner = both[:, 384:512]
        qkv = both[:, 0:384] + dot(inner.astype(BF), R.qkvb[1024:1152, 0:384])
        R.n1c[rows, :] = (R.xf[rows, own].astype(F32) * inverse * R.g1v[:, own]).astype(BF)
        R.r1t[:, rows] = jnp.transpose(inner).astype(BF)
        R.qb[rows, :] = (qkv[:, 0:128].astype(BF).astype(F32) * 0.125).astype(BF)
        R.kb[rows, :] = qkv[:, 128:256].astype(BF)
        R.vb[rows, :] = qkv[:, 256:384].astype(BF)
        R.kt[:, rows] = jnp.transpose(qkv[:, 128:256]).astype(BF)
        R.vt[:, rows] = jnp.transpose(qkv[:, 256:384]).astype(BF)
        return carry

    R.g1v[...] = gain_one
    lax.fori_loop(0, 4, qkv_tile, 0)

    across(gu_views, R.w2ms, R.w2mr, 0, (3,))

    head_of = lax.broadcasted_iota(jnp.int32, (256, 128), 1) // HD

    def attend_tile(t, carry):
        rows = part(t, 256)
        queries = R.qb[rows, :]
        same = R.segc[:, 0:1] == R.meta[y, pl.ds(zh, 1), rows].astype(F32)
        mixed = []
        for h in range(2):
            mine = jnp.where(head_of == h, queries.astype(F32), 0.0).astype(BF)
            scores = jnp.where(same, dot_t(R.kb[...], mine), NEG)
            weights = jnp.exp(scores - jnp.max(scores, axis=0, keepdims=True))
            probs = (weights * (1.0 / jnp.sum(weights, axis=0, keepdims=True))).astype(BF)
            R.pr[2 * t + h] = probs
            mixed.append(dot(R.vt[h * HD : (h + 1) * HD, :], probs))
        mixed = jnp.concatenate(mixed, axis=0)
        R.att[t] = mixed
        R.ath[rows, :] = jnp.transpose(mixed).astype(BF)
        return carry

    lax.fori_loop(0, 4, attend_tile, 0)

    for k, (a, b) in enumerate(PEERS):
        spot = me.flip(a, b)
        send(R.ath.at[part(spot.member(), 128)], R.ato.at[:, own], R.a1s.at[k], R.a1r.at[k], spot)
    mine_local = pltpu.make_async_copy(R.ath.at[own], R.ato.at[:, own], R.a1r.at[7])
    mine_local.start()

    send(R.wd_h, down_mine, R.wds.at[0, 0], R.wdr.at[0, 0], me.flip(0, 8))
    send(R.wd_h, down_mine, R.wds.at[1, 0], R.wdr.at[1, 0], me.flip(0, 2))
    spread_on(R.ogf, R.aos, R.aor)
    across_on(gu_views, R.w2ms, R.w2mr, (0, 1))
    mine_local.wait()
    for k, (a, b) in enumerate(PEERS):
        spot = me.flip(a, b)
        arrived(R.ato.at[:, part(spot.member(), 128)], R.a1s.at[k], R.a1r.at[k], spot)

    double_on(out_view, R.wos, R.wor, 3)
    double_end(out_view, R.wos, R.wor)
    start_rows = R.xf[own, :].astype(F32)
    both = dot(R.ato[...], R.ob[0:1024, :])
    out_inner = both[:, 1024:1152]
    middle = start_rows + both[:, 0:1024] + dot(out_inner.astype(BF), R.ob[1024:1152, 0:1024])
    R.mid[...] = middle
    inverse = lax.rsqrt(jnp.mean(middle * middle, axis=-1, keepdims=True) + EPS)
    R.n2f[own, :] = (middle * inverse * gain_two).astype(BF)
    R.rot[...] = jnp.transpose(out_inner).astype(BF)
    spread(R.n2f, R.ans, R.anr)

    down_local.wait()
    across_on(gu_views, R.w2ms, R.w2mr, (2, 3))
    across_on(down_views, R.wds, R.wdr)
    spread_far(R.ogf, R.aos, R.aor)
    spread_on(R.n2f, R.ans, R.anr)
    spread_far(R.n2f, R.ans, R.anr)
    spread_end(R.n2f, R.ans, R.anr)
    across_end(gu_views, R.w2ms, R.w2mr)
    R.cml[...] = jnp.zeros((128, 1024), F32)
    R.cle[...] = jnp.zeros((128, 512), F32)

    def order(i):
        return part(lax.rem((1 - p) * 2 + i, 4), 256)

    def pair_tile(i, carry):
        rows = order(i)
        both = dot(R.n2f[rows, :], R.gub[0:1024, :])
        inner = both[:, 1024:1152]
        pair = both[:, 0:1024] + dot(inner.astype(BF), R.gub[1024:1152, 0:1024])
        gate, upper = pair[:, 0:512], pair[:, 512:1024]
        R.pair[rows, :] = pair
        R.hid[rows, :] = (gate * jax.nn.sigmoid(gate) * upper).astype(BF)
        R.r2t[:, rows] = jnp.transpose(inner).astype(BF)
        return carry

    def down_tile(i, carry):
        rows = order(i)
        R.zd[rows, :] = dot(R.hid[rows, :], R.db[0:512, :]).astype(BF)
        return carry

    def mlp_back_tile(i, carry):
        rows = order(i)
        gate, upper = R.pair[rows, 0:512], R.pair[rows, 512:1024]
        sigma = jax.nn.sigmoid(gate)
        back = dot_t(R.ogf[rows, :], R.db[:, 0:1024])
        inner_back = back[:, 512:640]
        hidden_grad = back[:, 0:512] + dot_t(inner_back.astype(BF), R.db[0:512, 1024:1152])
        gate_grad = (hidden_grad * upper * sigma * (1.0 + gate * (1.0 - sigma))).astype(BF)
        up_grad = (hidden_grad * gate * sigma).astype(BF)
        pair_grad = jnp.concatenate([gate_grad, up_grad], axis=1)
        R.zn[rows, :] = dot_t(pair_grad, R.gub[:, 0:1024]).astype(BF)
        R.cml[...] += dot(R.r2t[:, rows], pair_grad)
        R.cle[...] += dot(jnp.transpose(inner_back).astype(BF), R.hid[rows, :])
        return carry

    def pair_send(parts, k):
        send(parts.at[part(1 - p, 512)], R.rp.at[k], R.rps.at[k], R.rpr.at[k], partner)

    def chip_send(parts, k):
        arrived(R.rp.at[k], R.rps.at[k], R.rpr.at[k], partner)

        def add(i, carry):
            rows = part(i, 128)
            R.rc[k, rows, :] = (
                parts[part(p * 4 + i, 128), :].astype(F32) + R.rp[k, rows, :].astype(F32)
            ).astype(BF)
            return carry

        lax.fori_loop(0, 4, add, 0)
        for i, b in enumerate(SAME):
            spot = me.flip(0, b)
            send(R.rc.at[k, part(spot.zl * 2 + spot.x, 128)], R.rr.at[k, i], R.rrs.at[k, i], R.rrr.at[k, i], spot)

    def summed(parts, k):
        for i, b in enumerate(SAME):
            arrived(R.rr.at[k, i], R.rrs.at[k, i], R.rrr.at[k, i], me.flip(0, b))
        total = parts[own, :].astype(F32) + R.rp[k, part(zl * 2 + x, 128), :].astype(F32)
        for i in range(3):
            total = total + R.rr[k, i].astype(F32)
        return total

    lax.fori_loop(0, 4, pair_tile, 0)
    across_end(down_views, R.wds, R.wdr)
    lax.fori_loop(0, 2, down_tile, 0)
    pair_send(R.zd, 1)
    lax.fori_loop(2, 4, down_tile, 0)
    spread_end(R.ogf, R.aos, R.aor)
    chip_send(R.zd, 1)
    lax.fori_loop(0, 2, mlp_back_tile, 0)
    pair_send(R.zn, 0)
    lax.fori_loop(2, 4, mlp_back_tile, 0)
    chip_send(R.zn, 0)
    for i in range(2):
        R.da[:, pl.ds(i * 512, 512)] = (SCALE * R.cml[i * 16 : (i + 1) * 16, i * 512 : (i + 1) * 512]).astype(BF)
    R.da[:, pl.ds(1024, 512)] = R.cle[0:16, :].astype(BF)

    def first_view(spot):
        return R.ga_o.at[spot.group(), spot.member()]

    def second_view(spot):
        return R.gb_o.at[spot.group(), spot.member()]

    def third_view(spot):
        return R.gc_o.at[spot.group(), spot.member()]

    first_local = pltpu.make_async_copy(R.da, first_view(me), R.gar.at[31])
    first_local.start()
    first_local.wait()
    double(first_view, R.gas, R.gar, 0)

    own_grad = R.ogf[own, :].astype(F32)
    total = summed(R.zn, 0)
    inner_back = total[:, 1024:1152]
    normed_grad = total[:, 0:1024] + dot_t(inner_back.astype(BF), R.gub[0:1024, 1024:1152])
    middle = R.mid[...]
    inverse = lax.rsqrt(jnp.mean(middle * middle, axis=-1, keepdims=True) + EPS)
    middle_grad = own_grad + norm_back(middle, inverse, gain_two, normed_grad)
    R.mg[...] = middle_grad
    rounded = middle_grad.astype(BF)
    both = dot_t(rounded, R.ob[:, 0:1024])
    out_back = both[:, 1024:1152]
    R.gao[...] = (both[:, 0:1024] + dot_t(out_back.astype(BF), R.ob[0:1024, 1024:1152])).astype(BF)
    for k, (a, b) in enumerate(PEERS):
        spot = me.flip(a, b)
        send(R.gao.at[:, part(spot.member(), 128)], R.gah.at[own], R.a2s.at[k], R.a2r.at[k], spot)
    mine_local = pltpu.make_async_copy(R.gao.at[:, own], R.gah.at[own], R.a2r.at[7])
    mine_local.start()
    R.ib[0, own, :] = (inner_back + pltpu.roll(out_back, 32, 1)).astype(BF)

    def rank_view(i):
        return lambda spot: R.ib.at[i, part(spot.member(), 128)]

    share(rank_view(0), R.ibs.at[0], R.ibr.at[0])
    out_leave = (SCALE * dot(R.rot[...], rounded))[0:16].astype(BF)
    for i in range(8):
        R.gp[i] = out_leave[:, i * 128 : (i + 1) * 128]
    for k, (a, b) in enumerate(PEERS):
        spot = me.flip(a, b)
        send(R.gp.at[spot.member()], R.gr.at[k], R.gps.at[k], R.gpr.at[k], spot)
    def give_back(src, dst, ssem, rsem):
        spot_same, spot_other = part(zh, 64), part(1 - zh, 64)

        @pl.when(p == y)
        def _():
            pltpu.make_async_copy(src.at[spot_same], dst.at[zh], rsem.at[0]).start()
            remote(src.at[spot_other], dst.at[zh], ssem.at[1], rsem.at[1], me.flip(0, 8)).start()

        @pl.when(p != y)
        def _():
            remote(src.at[spot_same], dst.at[zh], ssem.at[0], rsem.at[0], me.flip(1, 2)).start()
            remote(src.at[spot_other], dst.at[zh], ssem.at[1], rsem.at[1], me.flip(1, 10)).start()

    def give_back_wait(src, dst, ssem, rsem):
        pltpu.make_async_copy(dst.at[zh], dst.at[zh], rsem.at[0]).wait()
        pltpu.make_async_copy(dst.at[1 - zh], dst.at[1 - zh], rsem.at[1]).wait()

        @pl.when(p != y)
        def _():
            remote(src.at[part(zh, 64)], src.at[part(zh, 64)], ssem.at[0], rsem.at[0], me.flip(1, 2)).wait_send()

        remote(src.at[part(zh, 64)], src.at[part(zh, 64)], ssem.at[1], rsem.at[1], me.flip(0, 8)).wait_send()

    total = summed(R.zd, 1)
    last_inner = total[:, 1024:1152]
    R.ib[1, own, :] = last_inner.astype(BF)
    share(rank_view(1), R.ibs.at[1], R.ibr.at[1])
    R.outv[...] = (R.mid[...] + total[:, 0:1024] + dot(last_inner.astype(BF), R.db[512:640, 0:1024])).astype(BF)

    give_back(R.outv, R.out_o, R.bos, R.bor)
    double_on(first_view, R.gas, R.gar, 0)
    mine_local.wait()
    for k, (a, b) in enumerate(PEERS):
        spot = me.flip(a, b)
        arrived(R.gah.at[part(spot.member(), 128)], R.a2s.at[k], R.a2r.at[k], spot)

    share_on(rank_view(0), R.ibs.at[0], R.ibr.at[0])
    R.gk[...] = jnp.zeros((1024, 128), F32)
    R.gv[...] = jnp.zeros((1024, 128), F32)

    def attend_back_tile(t, carry):
        rows = part(t, 256)
        queries, grads = R.qb[rows, :].astype(F32), R.gah[rows, :].astype(F32)
        delta_parts = jnp.transpose(grads) * R.att[t]
        query_grad = []
        for h in range(2):
            mine = jnp.where(head_of == h, queries, 0.0).astype(BF)
            grad = jnp.where(head_of == h, grads, 0.0).astype(BF)
            probs = R.pr[2 * t + h]
            delta = jnp.sum(delta_parts[h * HD : (h + 1) * HD], axis=0, keepdims=True)
            score_grad = (probs.astype(F32) * (dot_t(R.vb[...], grad) - delta)).astype(BF)
            R.gk[...] += dot(score_grad, mine)
            R.gv[...] += dot(probs, grad)
            query_grad.append(dot(R.kt[h * HD : (h + 1) * HD, :], score_grad))
        R.gq[rows, pl.ds(0, 128)] = (jnp.transpose(jnp.concatenate(query_grad, axis=0)) * 0.125).astype(BF)
        return carry

    lax.fori_loop(0, 4, attend_back_tile, 0)
    share_on(rank_view(1), R.ibs.at[1], R.ibr.at[1])
    double_on(first_view, R.gas, R.gar, 1)
    R.gq[:, pl.ds(128, 128)] = R.gk[...].astype(BF)
    R.gq[:, pl.ds(256, 128)] = R.gv[...].astype(BF)

    def qkv_back_tile(i, carry):
        rows = part(lax.rem((1 - p) * 2 + i, 4), 256)
        R.zq[rows, :] = dot_t(R.gq[rows, :], R.qkvb[:, 0:384]).astype(BF)
        return carry

    lax.fori_loop(0, 2, qkv_back_tile, 0)
    pair_send(R.zq, 2)
    lax.fori_loop(2, 4, qkv_back_tile, 0)
    chip_send(R.zq, 2)
    double_on(first_view, R.gas, R.gar, 2)

    leave = SCALE * dot(R.r1t[...], R.gq[...])
    for i in range(3):
        R.db2[:, pl.ds(i * 128, 128)] = leave[i * 16 : (i + 1) * 16, i * 128 : (i + 1) * 128].astype(BF)
    share_end(rank_view(0), R.ibs.at[0], R.ibr.at[0])
    ranks = jnp.transpose(R.ib[0].astype(F32)).astype(BF)
    mlp_enter, out_enter = dot(ranks, R.n2f[:, own]), dot(ranks, R.ath[...])
    block = R.gp[j].astype(F32)
    for k, (a, b) in enumerate(PEERS):
        arrived(R.gr.at[k], R.gps.at[k], R.gpr.at[k], me.flip(a, b))
        block = block + R.gr[k].astype(F32)
    R.db2[:, pl.ds(384, 128)] = out_enter[32:48].astype(BF)
    R.db2[:, pl.ds(512, 128)] = block.astype(BF)
    R.db2[:, pl.ds(640, 128)] = mlp_enter[0:16].astype(BF)
    R.db2[:, pl.ds(768, 128)] = mlp_enter[16:32].astype(BF)
    second_local = pltpu.make_async_copy(R.db2, second_view(me), R.gbr.at[31])
    second_local.start()
    second_local.wait()
    double(second_view, R.gbs, R.gbr, 0)

    total = summed(R.zq, 2)
    inner_back = total[:, 1024:1152]
    normed_grad = total[:, 0:1024] + dot_t(inner_back.astype(BF), R.qkvb[0:1024, 384:512])
    start_rows = R.xf[own, :].astype(F32)
    inverse = lax.rsqrt(jnp.mean(start_rows * start_rows, axis=-1, keepdims=True) + EPS)
    R.ib[2, own, :] = inner_back.astype(BF)
    share(rank_view(2), R.ibs.at[2], R.ibr.at[2])
    double_on(second_view, R.gbs, R.gbr, 0)
    R.igv[...] = (R.mg[...] + norm_back(start_rows, inverse, gain_one, normed_grad)).astype(BF)

    share_end(rank_view(1), R.ibs.at[1], R.ibr.at[1])
    last_leave = SCALE * dot(jnp.transpose(R.ib[1].astype(F32)).astype(BF), R.ogf[:, own])
    R.dc[:, pl.ds(384, 128)] = last_leave[0:16].astype(BF)
    share_on(rank_view(2), R.ibs.at[2], R.ibr.at[2])
    share_end(rank_view(2), R.ibs.at[2], R.ibr.at[2])
    double_on(second_view, R.gbs, R.gbr, 1)
    attn_enter = dot(jnp.transpose(R.ib[2].astype(F32)).astype(BF), R.n1c[...])
    for i in range(3):
        R.dc[:, pl.ds(i * 128, 128)] = attn_enter[i * 16 : (i + 1) * 16].astype(BF)

    third_local = pltpu.make_async_copy(R.dc, third_view(me), R.gcr.at[3, 0])
    third_local.start()
    for k, (a, b) in enumerate(ACROSS):
        send(R.dc, third_view(me), R.gcs.at[k, 0], R.gcr.at[k, 0], me.flip(a, b))
    third_local.wait()
    share(third_view, R.gds.at[3], R.gdr.at[3])
    double_on(second_view, R.gbs, R.gbr, 2)
    give_back(R.igv, R.ig_o, R.bis, R.bir)
    for k, (a, b) in enumerate(ACROSS):
        arrived(third_view(me.flip(a, b)), R.gcs.at[k, 0], R.gcr.at[k, 0], me.flip(a, b))
        share(lambda spot, b=b: third_view(spot.flip(0, b)), R.gds.at[k], R.gdr.at[k])
    double_on(first_view, R.gas, R.gar, 3)
    flips = {0: 2, 1: 8, 2: 10, 3: 0}
    for k in (3, 0, 1, 2):
        share_on(lambda spot, k=k: third_view(spot.flip(0, flips[k])), R.gds.at[k], R.gdr.at[k])
    double_on(second_view, R.gbs, R.gbr, 3)
    double_end(first_view, R.gas, R.gar)
    double_end(second_view, R.gbs, R.gbr)
    for k in (3, 0, 1, 2):
        share_end(lambda spot, k=k: third_view(spot.flip(0, flips[k])), R.gds.at[k], R.gdr.at[k])

    meta_out = pltpu.make_async_copy(R.meta.at[:, :, pl.ds(0, 128)], R.meta_o, R.mr.at[2])
    meta_out.start()
    give_back_wait(R.outv, R.out_o, R.bos, R.bor)
    give_back_wait(R.igv, R.ig_o, R.bis, R.bir)
    reshard_sent(R.x_h, R.xs)
    reshard_sent(R.og_h, R.os)
    for copy in late:
        copy.wait_send()
    meta_out.wait()


SMALL = dict(seg_h=0, ids_h=0, g1_h=0, g2_h=0)


def layer_call(**inputs):
    V, S = pltpu.VMEM, pltpu.SemaphoreType.DMA
    outputs = dict(
        out_o=((2, 64, 1024), BF),
        ig_o=((2, 64, 1024), BF),
        ga_o=((4, 8, 16, WIDTHS[0]), BF),
        gb_o=((4, 8, 16, WIDTHS[1]), BF),
        gc_o=((4, 8, 16, WIDTHS[2]), BF),
        meta_o=((2, 8, 128), jnp.int32),
    )
    scratch = dict(
        xf=V((1024, 1024), BF), ogf=V((1024, 1024), BF), n2f=V((1024, 1024), BF),
        qkvb=V((1152, 512), BF), ob=V((1152, 1152), BF), gub=V((1152, 1152), BF), db=V((640, 1152), BF),
        ae=V((3, 8, 16, 1024), BF), al=V((3, 8, 16, 128), BF), oe=V((8, 16, 1024), BF), ol=V((8, 16, 1024), BF),
        me=V((2, 8, 16, 1024), BF), ml=V((2, 8, 16, 512), BF), le=V((8, 16, 512), BF), ll=V((8, 16, 1024), BF),
        own=V((8, 1024), jnp.int32), gl=V((16, 128), F32), meta=V((2, 8, 1024), jnp.int32), gs=V((4, 8, 16, 128), F32), segc=V((1024, 128), F32),
        qb=V((1024, 128), BF), kb=V((1024, 128), BF), vb=V((1024, 128), BF), kt=V((128, 1024), BF),
        vt=V((128, 1024), BF), r1t=V((128, 1024), BF), pr=V((8, 1024, 256), BF), att=V((4, 128, 256), F32),
        ath=V((1024, 128), BF), ato=V((128, 1024), BF), mid=V((128, 1024), F32), mg=V((128, 1024), F32),
        rot=V((128, 128), BF), zn=V((1024, 1152), BF), zd=V((1024, 1152), BF), zq=V((1024, 1152), BF),
        rp=V((3, 512, 1152), BF), rc=V((3, 512, 1152), BF), rr=V((3, 3, 128, 1152), BF),
        pair=V((1024, 1024), F32), hid=V((1024, 512), BF), r2t=V((128, 1024), BF), cml=V((128, 1024), F32), cle=V((128, 512), F32), gao=V((128, 1024), BF), gah=V((1024, 128), BF),
        gk=V((1024, 128), F32), gv=V((1024, 128), F32), gq=V((1024, 384), BF), outv=V((128, 1024), BF),
        igv=V((128, 1024), BF), gp=V((8, 16, 128), BF), gr=V((7, 16, 128), BF), da=V((16, WIDTHS[0]), BF),
        db2=V((16, WIDTHS[1]), BF), dc=V((16, WIDTHS[2]), BF), ib=V((3, 1024, 128), BF), n1c=V((1024, 128), BF), g1v=V((1, 1024), F32),
        la=S((16,)), xs=S((2,)), xr=S((2,)), os=S((2,)), ors=S((2,)), g1s=S((7,)), g1r=S((8,)),
        g2s=S((3, 1)), g2r=S((3, 1)), w1qs=S((8, 3)), w1qr=S((8, 3)), w1ms=S((8, 8)), w1mr=S((8, 8)),
        w2qs=S((3, 4)), w2qr=S((3, 4)), w2ms=S((3, 4)), w2mr=S((3, 4)), wos=S((31,)), wor=S((32,)),
        wds=S((3, 1)), wdr=S((4, 1)), ms=S((1,)), mr=S((3,)), axs=S((9,)), axr=S((9,)),
        aos=S((9,)), aor=S((9,)), ans=S((9,)), anr=S((9,)), ibs=S((3, 7)), ibr=S((3, 7)),
        a1s=S((7,)), a1r=S((8,)), a2s=S((7,)), a2r=S((8,)), rps=S((3,)), rpr=S((3,)),
        rrs=S((3, 3)), rrr=S((3, 3)), bos=S((2,)), bor=S((2,)), bis=S((2,)), bir=S((2,)),
        gps=S((7,)), gpr=S((7,)), gas=S((31,)), gar=S((32,)), gbs=S((31,)), gbr=S((32,)),
        gcs=S((3, 1)), gcr=S((4, 1)), gds=S((4, 7)), gdr=S((4, 7)),
    )
    names = list(inputs) + list(outputs) + list(scratch)
    return pl.pallas_call(
        functools.partial(layer_kernel, names),
        out_shape=[jax.ShapeDtypeStruct(shape, dtype) for shape, dtype in outputs.values()],
        in_specs=[pl.BlockSpec(memory_space=pltpu.VMEM if name in SMALL else pl.ANY) for name in inputs],
        out_specs=[pl.BlockSpec(memory_space=pl.ANY)] * len(outputs),
        scratch_shapes=list(scratch.values()),
        compiler_params=pltpu.CompilerParams(collective_id=0, has_side_effects=True, vmem_limit_bytes=63 * 2**20),
        name="layer",
    )(*inputs.values())


def place_kernel(ids, first, second, third, out_i, ig_i, out_o, ig_o, ae_o, al_o, oe_o, ol_o, me_o, ml_o, le_o, ll_o):
    a = pl.program_id(0)
    outs = (ae_o, al_o, oe_o, ol_o, me_o, ml_o, le_o, ll_o)

    @pl.when(a == 0)
    def _():
        out_o[...] = out_i[...]
        ig_o[...] = ig_i[...].astype(F32)

    for ref in outs:
        ref[...] = jnp.zeros(ref.shape, F32)
    for group in range(4):
        ident = ids[group % 2, 2 + group // 2, 0]

        @pl.when(ident == a)
        def _(group=group):
            for m in range(8):
                at = slice(m * 128, (m + 1) * 128)
                for i in range(3):
                    al_o[i, 0, :, at] += second[group, m, :, i * 128 : (i + 1) * 128].astype(F32)
                    ae_o[i, 0, :, at] += third[group, m, :, i * 128 : (i + 1) * 128].astype(F32)
                oe_o[0, :, at] += second[group, m, :, 384:512].astype(F32)
                ol_o[0, :, at] += second[group, m, :, 512:640].astype(F32)
                for i in range(2):
                    me_o[i, 0, :, at] += second[group, m, :, 640 + i * 128 : 768 + i * 128].astype(F32)
                ll_o[0, :, at] += third[group, m, :, 384:512].astype(F32)
                for q in range(4):
                    fb = ((m // 4) * 16 + (q // 2) * 8 + (m // 2 % 2) * 4 + (q % 2) * 2 + m % 2) * 128
                    for i in range(2):
                        ml_o[i, 0, :, fb : fb + 128] += first[group, m, :, i * 512 + q * 128 : i * 512 + (q + 1) * 128].astype(F32)
                    le_o[0, :, fb : fb + 128] += first[group, m, :, 1024 + q * 128 : 1024 + (q + 1) * 128].astype(F32)


def place_call(meta, *inputs):
    def whole(shape):
        return pl.BlockSpec(shape, lambda a, ids: (0,) * len(shape))

    def four(n, width):
        return pl.BlockSpec((n, 1, 16, width), lambda a, ids: (0, a, 0, 0))

    def three(width):
        return pl.BlockSpec((1, 16, width), lambda a, ids: (a, 0, 0))

    shapes = ((3, 8, 16, 1024), (3, 8, 16, 1024), (8, 16, 1024), (8, 16, 1024), (2, 8, 16, 1024), (2, 8, 16, 4096), (8, 16, 4096), (8, 16, 1024))
    return pl.pallas_call(
        place_kernel,
        out_shape=[jax.ShapeDtypeStruct((2, 64, 1024), BF), jax.ShapeDtypeStruct((2, 64, 1024), F32)]
        + [jax.ShapeDtypeStruct(shape, F32) for shape in shapes],
        grid_spec=pltpu.PrefetchScalarGridSpec(
            num_scalar_prefetch=1,
            grid=(8,),
            in_specs=[whole(array.shape) for array in inputs],
            out_specs=[whole((2, 64, 1024)), whole((2, 64, 1024)), four(3, 1024), four(3, 1024), three(1024), three(1024),
                       four(2, 1024), four(2, 4096), three(4096), three(1024)],
        ),
        compiler_params=pltpu.CompilerParams(vmem_limit_bytes=63 * 2**20),
        name="place",
    )(meta, *inputs)


def grouped(
    inputs, segment_ids, adapter_ids, w_query, w_key, w_value, w_out, w_gate, w_up, w_down, gain_attn, gain_ffn,
    attn_enter, attn_leave, out_enter, out_leave, mlp_enter, mlp_leave, last_enter, last_leave, out_grad,
):
    out, ig, *shares, meta_all = layer_call(
        x_h=inputs[:, 0], og_h=out_grad[:, 0], seg_h=segment_ids, ids_h=adapter_ids.reshape(1, 2), g1_h=gain_attn[None, :], g2_h=gain_ffn[None, :], wq_h=w_query, wk_h=w_key, wv_h=w_value, wo_h=w_out,
        wg_h=w_gate, wu_h=w_up, wd_h=w_down, ae_h=attn_enter, al_h=attn_leave, oe_h=out_enter, ol_h=out_leave,
        me_h=mlp_enter, ml_h=mlp_leave, le_h=last_enter, ll_h=last_leave,
    )
    out, ig, *grads = place_call(meta_all, *shares, out, ig)
    return (out[:, None], ig[:, None], *grads)


def solution(mesh):
    def chosen(*args):
        sizes = (mesh.shape["dp"], mesh.shape["ctx"], *args[0].shape)
        return (grouped if sizes == (2, 16, 2, 1, 64, 1024) else per_device)(*args)

    return jax.shard_map(
        chosen,
        mesh=mesh,
        in_specs=(
            P(None, "dp", "ctx", None),
            P(None, "dp", None),
            P(None, "dp"),
            P(("dp", "ctx"), None),
            P(("dp", "ctx"), None),
            P(("dp", "ctx"), None),
            P(("dp", "ctx"), None),
            P(("dp", "ctx"), None),
            P(("dp", "ctx"), None),
            P(("dp", "ctx"), None),
            P(("dp", "ctx")),
            P(("dp", "ctx")),
            P(),
            P(),
            P(),
            P(),
            P(),
            P(),
            P(),
            P(),
            P(None, "dp", "ctx", None),
        ),
        out_specs=(
            P(None, "dp", "ctx", None),
            P(None, "dp", "ctx", None),
            P(),
            P(),
            P(),
            P(),
            P(),
            P(),
            P(),
            P(),
        ),
        check_vma=False,
    )
```
